32 devices in a mesh: dp: 16 (over z, y, x), space: 2 (over core).
Axes of the slice: x: 2, y: 2, z: 4, core: 2. Of those that a mesh axis runs over, the one named last changes fastest.
Arguments:
- images: bfloat16 [16, 16, 288, 256], P('dp', 'space'), may hold values from -12 to 12
- w_reduce: bfloat16 [256, 64], replicated, may hold values from -0.375 to 0.375
- w_dilated: bfloat16 [3, 3, 64, 64], replicated, may hold values from -0.25 to 0.25
- w_expand: bfloat16 [64, 256], replicated, may hold values from -0.75 to 0.75
- gain_one: float32 [64], replicated, may hold values from 0.25 to 1.75
- shift_one: float32 [64], replicated, may hold values from -3 to 3
- gain_two: float32 [64], replicated, may hold values from 0.25 to 1.75
- shift_two: float32 [64], replicated, may hold values from -3 to 3
- gain_three: float32 [256], replicated, may hold values from 0.25 to 1.75
- shift_three: float32 [256], replicated, may hold values from -3 to 3
- cotangent: bfloat16 [16, 16, 288, 256], P('dp', 'space'), may hold values from -6 to 6
Outputs:
- result: bfloat16 [16, 16, 288, 256], P('dp', 'space')
- grad_images: bfloat16 [16, 16, 288, 256], P('dp', 'space')
- grad_reduce: float32 [256, 64], replicated
- grad_dilated: float32 [3, 3, 64, 64], replicated
- grad_expand: float32 [64, 256], replicated
- grad_gain_one: float32 [64], replicated
- grad_shift_one: float32 [64], replicated
- grad_gain_two: float32 [64], replicated
- grad_shift_two: float32 [64], replicated
- grad_gain_three: float32 [256], replicated
- grad_shift_three: float32 [256], replicated
The draws below stay inside these ranges and needn't reach their ends.
All inputs are finite; a program needn't handle non-finite values.
Results may differ from the reference program's by a relative error of at most 0.012.
Values may be sent and summed in bfloat16 or wider, within the bound.
No kernel may reach another device: no remote copies, remote signals or barrier semaphores. Data moves between devices by JAX's collectives and lax.ppermute only.
A program may use at most 64 MiB of HBM per device.

```python
import jax
import jax.numpy as jnp
from jax import lax

C = 256
M = 64
W = 288
H = 16
B = 16


def draw_images(key, part):
    key_base = jax.random.fold_in(key, 11)
    key_scale = jax.random.fold_in(key, 23)
    row_pos = jnp.arange(H, dtype=jnp.float32)
    row_scale = 1.0 + 2.0 * row_pos / max(H - 1, 1)
    pixel_scale = jnp.exp(jax.random.uniform(key_scale, (B, H, W, 1), jnp.float32, minval=-1.0986, maxval=0.0))
    base_vals = jax.random.truncated_normal(key_base, -4.0, 4.0, (B, H, W, C), jnp.float32)
    return (base_vals * pixel_scale * row_scale[None, :, None, None]).astype(jnp.bfloat16)


def shard_levels(own_key, dims, cuts, least, largest):
    level = 1.0
    for position, parts in cuts:
        draws = jax.random.uniform(jax.random.fold_in(jax.random.fold_in(own_key, 6), position), (parts,), jnp.float32, least / len(cuts), largest / len(cuts))
        level = level * jnp.repeat(jnp.exp(draws), dims[position] // parts).reshape((-1,) + (1,) * (len(dims) - 1 - position))
    return level


def scatter_about(stream_key, extent, spread, most, split=(), kind=jnp.bfloat16):
    values = spread * jax.random.normal(stream_key, extent, jnp.float32)
    if split:
        values = values * shard_levels(stream_key, extent, split, -0.22, 0.18)
    return jnp.clip(values, -most, most).astype(kind)


def setup_inputs(seed: int = 0) -> dict:
    arg_keys = jax.random.split(jax.random.key(seed), 12)
    images = draw_images(jax.random.fold_in(arg_keys[11], 71), 0)
    w_reduce = scatter_about(arg_keys[1], (C, M), C ** -0.5, 0.375)
    w_dilated = scatter_about(arg_keys[2], (3, 3, M, M), (9 * M) ** -0.5, 0.25)
    w_expand = scatter_about(arg_keys[3], (M, C), M ** -0.5, 0.75)
    gain_one = jnp.clip(1.0 + 0.15 * jax.random.normal(arg_keys[4], (M,), jnp.float32), 0.25, 1.75)
    shift_one = scatter_about(arg_keys[5], (M,), 0.5, 3.0, (), jnp.float32)
    gain_two = jnp.clip(1.0 + 0.15 * jax.random.normal(arg_keys[6], (M,), jnp.float32), 0.25, 1.75)
    shift_two = scatter_about(arg_keys[7], (M,), 0.5, 3.0, (), jnp.float32)
    gain_three = jnp.clip(1.0 + 0.15 * jax.random.normal(arg_keys[8], (C,), jnp.float32), 0.25, 1.75)
    shift_three = scatter_about(arg_keys[9], (C,), 0.5, 3.0, (), jnp.float32)
    cotangent = scatter_about(arg_keys[10], (B, H, W, C), 1.0, 6.0, ((0, 16), (1, 2)))
    return {"images": images, "w_reduce": w_reduce, "w_dilated": w_dilated, "w_expand": w_expand, "gain_one": gain_one, "shift_one": shift_one, "gain_two": gain_two, "shift_two": shift_two, "gain_three": gain_three, "shift_three": shift_three, "cotangent": cotangent}


epsilon = 1e-05

def smooth_act(value):
    return value * jax.nn.sigmoid(value)

def smooth_slope(value):
    sig = jax.nn.sigmoid(value)
    return sig * (1.0 + value * (1.0 - sig))

def norm_fwd(pre, gain, shift):
    count = pre.shape[0]
    average = lax.optimization_barrier(jnp.sum(pre, 0)) / count
    centred = pre - average
    variance = lax.optimization_barrier(jnp.sum(centred * centred, 0)) / count
    inv_std = lax.rsqrt(variance + epsilon)
    normed = centred * inv_std
    return (normed, inv_std, gain * normed + shift)

def norm_bwd(grad, normed, inv_std, gain):
    count = grad.shape[0]
    grad_sum = lax.optimization_barrier(jnp.sum(grad, 0))
    grad_cross = lax.optimization_barrier(jnp.sum(grad * normed, 0))
    back = (gain * inv_std * (grad - grad_sum / count - normed * grad_cross / count)).astype(jnp.bfloat16)
    return (back, grad_cross, grad_sum)

def dilated(padded, kernel, rows, cols):
    output = jnp.zeros((rows * cols, kernel.shape[3]), jnp.float32)
    for tap_row in range(3):
        for tap_col in range(3):
            window = padded[2 * tap_row:2 * tap_row + rows, 2 * tap_col:2 * tap_col + cols].reshape(rows * cols, -1)
            output = output + jnp.dot(window, kernel[tap_row, tap_col], preferred_element_type=jnp.float32)
    return output

def contract(left, right):
    return lax.dot_general(left, right, (((0,), (0,)), ((), ())), preferred_element_type=jnp.float32)

def one_sample(inputs, w_reduce, w_dilated, w_expand, gain_one, shift_one, gain_two, shift_two, gain_three, shift_three):
    images, cotangent = inputs
    rows, cols, chans = images.shape
    mids = w_reduce.shape[1]
    flat_in = images.reshape(rows * cols, chans)
    pre_one = jnp.dot(flat_in, w_reduce, preferred_element_type=jnp.float32)
    normed_one, istd_one, out_one = norm_fwd(pre_one, gain_one, shift_one)
    act_one = smooth_act(out_one).astype(jnp.bfloat16)
    padded_one = jnp.pad(act_one.reshape(rows, cols, mids), ((2, 2), (2, 2), (0, 0)))
    pre_two = dilated(padded_one, w_dilated, rows, cols)
    normed_two, istd_two, out_two = norm_fwd(pre_two, gain_two, shift_two)
    act_two = smooth_act(out_two).astype(jnp.bfloat16)
    pre_three = jnp.dot(act_two, w_expand, preferred_element_type=jnp.float32)
    normed_three, istd_three, out_three = norm_fwd(pre_three, gain_three, shift_three)
    summed = out_three + flat_in.astype(jnp.float32)
    result = smooth_act(summed).astype(jnp.bfloat16)
    grad_three = cotangent.reshape(rows * cols, chans).astype(jnp.float32) * smooth_slope(summed)
    dh_three, gg_three, gs_three = norm_bwd(grad_three, normed_three, istd_three, gain_three)
    gw_expand = contract(act_two, dh_three)
    back_two = lax.dot_general(dh_three, w_expand, (((1,), (1,)), ((), ())), preferred_element_type=jnp.float32)
    grad_two = back_two * smooth_slope(out_two)
    dh_two, gg_two, gs_two = norm_bwd(grad_two, normed_two, istd_two, gain_two)
    taps = []
    for tap_row in range(3):
        for tap_col in range(3):
            window = padded_one[2 * tap_row:2 * tap_row + rows, 2 * tap_col:2 * tap_col + cols].reshape(rows * cols, mids)
            taps.append(contract(window, dh_two))
    gw_dilated = jnp.stack(taps).reshape(3, 3, mids, mids)
    padded_back = jnp.pad(dh_two.reshape(rows, cols, mids), ((2, 2), (2, 2), (0, 0)))
    flipped = jnp.transpose(w_dilated[::-1, ::-1], (0, 1, 3, 2))
    grad_one = dilated(padded_back, flipped, rows, cols) * smooth_slope(out_one)
    dh_one, gg_one, gs_one = norm_bwd(grad_one, normed_one, istd_one, gain_one)
    gw_reduce = contract(flat_in, dh_one)
    back_in = lax.dot_general(dh_one, w_reduce, (((1,), (1,)), ((), ())), preferred_element_type=jnp.float32)
    grad_images = (back_in + grad_three).astype(jnp.bfloat16)
    return (result.reshape(rows, cols, chans), grad_images.reshape(rows, cols, chans), gw_reduce, gw_dilated, gw_expand, gg_one, gs_one, gg_two, gs_two, gg_three, gs_three)

def reference(images, w_reduce, w_dilated, w_expand, gain_one, shift_one, gain_two, shift_two, gain_three, shift_three, cotangent):

    def runner(inputs):
        return one_sample(inputs, w_reduce, w_dilated, w_expand, gain_one, shift_one, gain_two, shift_two, gain_three, shift_three)
    outputs = lax.map(runner, (images, cotangent))
    batch = images.shape[0]
    grads = [lax.optimization_barrier(jnp.sum(item, 0)) / batch for item in outputs[2:]]
    return (outputs[0], outputs[1], grads[0], grads[1], grads[2], grads[3], grads[4], grads[5], grads[6], grads[7], grads[8])
```

```python
import functools

import jax
import jax.numpy as jnp
from jax import lax
from jax.experimental import pallas as pl
from jax.experimental.pallas import tpu as pltpu
from jax.sharding import PartitionSpec as P

epsilon = 1e-05
F32 = jnp.float32
BF16 = jnp.bfloat16
HEAD = 8
GAP = 8


def nn(left, right):
    return jnp.dot(left, right, preferred_element_type=F32)


def nt(left, right):
    return lax.dot_general(left, right, (((1,), (1,)), ((), ())), preferred_element_type=F32)


def tn(left, right):
    return lax.dot_general(left, right, (((0,), (0,)), ((), ())), preferred_element_type=F32)


def swap_halves(value):
    return pltpu.roll(value, value.shape[1] // 2, 1)


def lower_half(shape):
    return lax.broadcasted_iota(jnp.int32, shape, 1) < shape[1] // 2


def both_halves(row):
    return row + swap_halves(row)


def rowsum(value):
    return jnp.sum(value, 0, keepdims=True)


def group(value):
    return jnp.sum(value.reshape(value.shape[0] // 8, 8, value.shape[1]), 0)


def silu(value):
    half = 0.5 * value
    return half + half * jnp.tanh(half)


def slope(value):
    half = 0.5 * value
    turn = jnp.tanh(half)
    return (0.5 + 0.5 * turn) * (1.0 + half * (1.0 - turn))


def moments(own, rec, peers, local):
    means = [own[0:1, :]] + [rec[HEAD * k : HEAD * k + 1, :] for k in range(peers)]
    squares = [own[1:2, :]] + [rec[HEAD * k + 1 : HEAD * k + 2, :] for k in range(peers)]
    mean = sum(means) / (peers + 1)
    total = sum(squares) + local * sum((item - mean) * (item - mean) for item in means)
    return mean, lax.rsqrt(total / (local * (peers + 1)) + epsilon)


def totals(own, rec, peers):
    sums = own[0:1, :] + sum(rec[HEAD * k : HEAD * k + 1, :] for k in range(peers))
    cross = own[1:2, :] + sum(rec[HEAD * k + 1 : HEAD * k + 2, :] for k in range(peers))
    return sums, cross


def head_rows(first, second):
    rest = jnp.zeros((HEAD - 2, first.shape[1]), F32)
    return jnp.concatenate([first, second, rest], 0)


def edges(ref, edge):
    size = ref.shape[0]
    top = ref[0:edge, :]
    return swap_halves(jnp.where(lower_half(top.shape), top, ref[size - edge : size, :]))


def fill_edges(ext, first, last, halo, mask, edge):
    size = ext.shape[0]
    low = lower_half(halo.shape)
    halo = halo * mask
    ext[0:edge, :] = jnp.where(low, halo, swap_halves(last)).astype(BF16)
    ext[size - edge : size, :] = jnp.where(low, swap_halves(first), halo).astype(BF16)


def norm_coefs(gain, shift, mean, inv):
    scale = gain * inv
    return scale, shift - mean * scale


def back_coefs(gain, mean, inv, sums, cross, count):
    scale = gain * inv
    slant = -scale * inv * cross / count
    return scale, slant, -scale * sums / count - slant * mean


def centred_squares(ref, mean, step):
    acc = jnp.zeros((8, ref.shape[1]), F32)
    for at in range(0, ref.shape[0], step):
        gap = ref[at : at + step, :] - mean
        acc = acc + group(gap * gap)
    return rowsum(acc)


def first_kernel(edge, im, w, pre, msg, wpack):
    half, cols = pre.shape[0], edge // 2
    weight = w[...]
    zero = jnp.zeros_like(weight)
    upper = jnp.concatenate([weight, zero], 1)
    lower = jnp.concatenate([zero, weight], 1)
    wpack[0] = upper
    wpack[1] = lower
    acc = jnp.zeros((8, pre.shape[1]), F32)
    for at in range(0, half, cols):
        part = nn(im[at : at + cols, :], upper) + nn(im[half + at : half + at + cols, :], lower)
        pre[at : at + cols, :] = part
        acc = acc + group(part)
    mean = both_halves(rowsum(acc)) / (2 * half)
    msg[0:HEAD, :] = head_rows(mean, both_halves(centred_squares(pre, mean, cols)))
    msg[HEAD:, :] = edges(pre, edge)


def weights_kernel(w, fwd, bwd):
    mids = w.shape[-1]
    wide = 2 * mids
    zero = jnp.zeros((mids, mids), BF16)
    for a in range(3):
        for b in range(3):
            block = w[a, b]
            both = jnp.concatenate(
                [jnp.concatenate([block, zero], 1), jnp.concatenate([zero, block], 1)], 0
            )
            fwd[a * wide : (a + 1) * wide, b * wide : (b + 1) * wide] = both
            k = 2 - a
            bwd[b * wide : (b + 1) * wide, k * wide : (k + 1) * wide] = both


def taps(ext, edge, at, cols):
    return jnp.concatenate([ext[a * edge + at : a * edge + at + cols, :] for a in range(3)], 1)


def clear_gaps(scr, cols):
    zero = jnp.zeros((scr.shape[0], GAP, scr.shape[2]), F32)
    scr[:, 0:GAP, :] = zero
    scr[:, GAP + cols :, :] = zero


def second_kernel(peers, edge, pre1, own1, rec1, g1, s1, mask, w, ext, pre2, msg, scr):
    half, cols, wide = pre2.shape[0], edge // 2, pre2.shape[1]
    mean, inv = moments(own1, rec1, peers, 2.0 * half)
    scale, bias = norm_coefs(g1[...], s1[...], mean, inv)
    clear_gaps(scr, cols)
    last = first = None
    acts = []
    for at in range(0, half, cols):
        act = silu(pre1[at : at + cols, :] * scale + bias)
        ext[edge + at : edge + at + cols, :] = act.astype(BF16)
        if at < edge or at >= half - edge:
            acts.append((at, act))
    first = jnp.concatenate([act for at, act in acts if at < edge], 0)
    last = jnp.concatenate([act for at, act in acts if at >= half - edge], 0)
    halo = silu(rec1[HEAD * peers :, :] * scale + bias) if peers else jnp.zeros((edge, wide), F32)
    fill_edges(ext, first, last, halo, mask[...], edge)
    acc = jnp.zeros((8, wide), F32)
    for i, at in enumerate(range(0, half, cols)):
        out = nn(taps(ext, edge, at, cols), w[...])
        scr[2 * i, GAP : GAP + cols, :] = out[:, 0:wide]
        scr[2 * i + 1, GAP : GAP + cols, :] = out[:, 2 * wide :]
        part = (
            out[:, wide : 2 * wide]
            + scr[2 * i, GAP - 2 : GAP - 2 + cols, :]
            + scr[2 * i + 1, GAP + 2 : GAP + 2 + cols, :]
        )
        pre2[at : at + cols, :] = part
        acc = acc + group(part)
    mean = both_halves(rowsum(acc)) / (2 * half)
    msg[...] = head_rows(mean, both_halves(centred_squares(pre2, mean, cols)))


def third_kernel(peers, cols, pre2, own2, rec2, g2, s2, w, act2, pre3, msg):
    half = pre2.shape[0]
    mean, inv = moments(own2, rec2, peers, 2.0 * half)
    scale, bias = norm_coefs(g2[...], s2[...], mean, inv)
    weight = w[...]
    zero = jnp.zeros_like(weight)
    upper = jnp.concatenate([weight, zero], 0)
    lower = jnp.concatenate([zero, weight], 0)
    acc = jnp.zeros((8, pre3.shape[1]), F32)
    for at in range(0, half, cols):
        act = silu(pre2[at : at + cols, :] * scale + bias).astype(BF16)
        act2[at : at + cols, :] = act
        part = nn(act, upper)
        pre3[at : at + cols, :] = part
        acc = acc + group(part)
        part = nn(act, lower)
        pre3[half + at : half + at + cols, :] = part
        acc = acc + group(part)
    mean = rowsum(acc) / (2 * half)
    msg[...] = head_rows(mean, centred_squares(pre3, mean, cols))


def fourth_kernel(peers, step, pre3, own3, rec3, g3, s3, im, cot, result, e3, msg):
    size, chans = pre3.shape
    mean, inv = moments(own3, rec3, peers, float(size))
    scale, bias = norm_coefs(g3[...], s3[...], mean, inv)

    def body(i, carry):
        sums, cross = carry
        at = pl.ds(pl.multiple_of(i * step, step), step)
        pre = pre3[at, :]
        half = 0.5 * (pre * scale + bias + im[at, :].astype(F32))
        turn = jnp.tanh(half)
        result[at, :] = (half + half * turn).astype(BF16)
        grad = cot[at, :].astype(F32) * ((0.5 + 0.5 * turn) * (1.0 + half * (1.0 - turn)))
        e3[at, :] = grad
        return sums + group(grad), cross + group(grad * (pre - mean))

    zero = jnp.zeros((8, chans), F32)
    sums, cross = lax.fori_loop(0, size // step, body, (zero, zero), unroll=2)
    msg[...] = head_rows(rowsum(sums), rowsum(cross) * inv)


def fifth_kernel(
    peers, edge, pre3, e3, own3, rec3, own4, rec4, g3, w, pre2, own2, rec2, g2, s2, dh3, e2, msg
):
    size, half, cols, wide = pre3.shape[0], pre2.shape[0], edge // 2, pre2.shape[1]
    count = float(size * (peers + 1))
    mean3, inv3 = moments(own3, rec3, peers, float(size))
    sums3, cross3 = totals(own4, rec4, peers)
    scale3, slant3, bias3 = back_coefs(g3[...], mean3, inv3, sums3, cross3, count)
    mean, inv = moments(own2, rec2, peers, float(size))
    scale, bias = norm_coefs(g2[...], s2[...], mean, inv)
    weight = w[...]
    zero = jnp.zeros_like(weight)
    upper = jnp.concatenate([weight, zero], 0)
    lower = jnp.concatenate([zero, weight], 0)
    sums = jnp.zeros((8, wide), F32)
    cross = jnp.zeros((8, wide), F32)
    for at in range(0, half, cols):
        back = None
        for base, side in ((at, upper), (half + at, lower)):
            rows = slice(base, base + cols)
            dh = (e3[rows, :] * scale3 + pre3[rows, :] * slant3 + bias3).astype(BF16)
            dh3[rows, :] = dh
            part = nt(dh, side)
            back = part if back is None else back + part
        pre = pre2[at : at + cols, :]
        grad = back * slope(pre * scale + bias)
        e2[at : at + cols, :] = grad
        sums = sums + group(grad)
        cross = cross + group(grad * (pre - mean))
    msg[0:HEAD, :] = head_rows(both_halves(rowsum(sums)), both_halves(rowsum(cross) * inv))
    msg[HEAD : HEAD + edge, :] = edges(e2, edge)
    msg[HEAD + edge :, :] = edges(pre2, edge)


def expand_kernel(act2, dh3, out):
    half = act2.shape[0]
    mids = act2.shape[1] // 2
    out[...] = tn(act2[...], dh3[0:half, :])[0:mids, :] + tn(act2[...], dh3[half:, :])[mids:, :]


def sixth_kernel(
    peers, edge, pre2, e2, own5, rec5, own2, rec2, g2, pre1, own1, rec1, g1, s1, mask, w,
    dext, e1, msg, scr,
):
    half, cols, wide = pre2.shape[0], edge // 2, pre2.shape[1]
    size = 2.0 * half
    count = size * (peers + 1)
    mean2, inv2 = moments(own2, rec2, peers, size)
    sums2, cross2 = totals(own5, rec5, peers)
    scale2, slant2, bias2 = back_coefs(g2[...], mean2, inv2, sums2, cross2, count)
    mean, inv = moments(own1, rec1, peers, size)
    scale, bias = norm_coefs(g1[...], s1[...], mean, inv)
    clear_gaps(scr, cols)
    acts = []
    for at in range(0, half, cols):
        dh = e2[at : at + cols, :] * scale2 + pre2[at : at + cols, :] * slant2 + bias2
        dext[edge + at : edge + at + cols, :] = dh.astype(BF16)
        if at < edge or at >= half - edge:
            acts.append((at, dh))
    first = jnp.concatenate([act for at, act in acts if at < edge], 0)
    last = jnp.concatenate([act for at, act in acts if at >= half - edge], 0)
    if peers:
        base = HEAD * peers
        halo = rec5[base : base + edge, :] * scale2 + rec5[base + edge :, :] * slant2 + bias2
    else:
        halo = jnp.zeros((edge, wide), F32)
    fill_edges(dext, first, last, halo, mask[...], edge)
    sums = jnp.zeros((8, wide), F32)
    cross = jnp.zeros((8, wide), F32)
    for i, at in enumerate(range(0, half, cols)):
        out = nt(taps(dext, edge, at, cols), w[...])
        scr[2 * i, GAP : GAP + cols, :] = out[:, 0:wide]
        scr[2 * i + 1, GAP : GAP + cols, :] = out[:, 2 * wide :]
        back = (
            out[:, wide : 2 * wide]
            + scr[2 * i, GAP + 2 : GAP + 2 + cols, :]
            + scr[2 * i + 1, GAP - 2 : GAP - 2 + cols, :]
        )
        pre = pre1[at : at + cols, :]
        grad = back * slope(pre * scale + bias)
        e1[at : at + cols, :] = grad
        sums = sums + group(grad)
        cross = cross + group(grad * (pre - mean))
    msg[...] = head_rows(both_halves(rowsum(sums)), both_halves(rowsum(cross) * inv))


def fold(block, upper):
    mids = block.shape[0] // 2
    if upper:
        return swap_halves(block[0:mids, :]) + block[mids:, :]
    return block[0:mids, :] + swap_halves(block[mids:, :])


def dilated_kernel(edge, ext, dext, gwe, own4, own5, out, scr, dcat):
    cols, wide = edge // 2, ext.shape[1]
    half = dext.shape[0] - 2 * edge
    mids = wide // 2
    clear_gaps(scr, cols)
    for i, at in enumerate(range(0, half, cols)):
        mid = dext[edge + at : edge + at + cols, :]
        scr[i, GAP : GAP + cols, :] = mid.astype(F32)
        dcat[at : at + cols, 0:wide] = scr[i, GAP + 2 : GAP + 2 + cols, :].astype(BF16)
        dcat[at : at + cols, wide : 2 * wide] = mid
        dcat[at : at + cols, 2 * wide :] = scr[i, GAP - 2 : GAP - 2 + cols, :].astype(BF16)
    blocks = []
    for a in range(3):
        prod = tn(ext[a * edge : a * edge + half, :], dcat[...])
        blocks = blocks + [prod[:, b * wide : (b + 1) * wide] for b in range(3)]
    low = lower_half((mids, wide))
    for k in range(4):
        pair = jnp.where(low, fold(blocks[2 * k], False), fold(blocks[2 * k + 1], True))
        out[k * mids : (k + 1) * mids, :] = pair.astype(BF16)
    out[4 * mids : 5 * mids, :] = fold(blocks[8], False).astype(BF16)
    chans = gwe.shape[1]
    base = 5 * mids
    for part in range(chans // wide):
        out[base : base + mids, :] = gwe[:, part * wide : (part + 1) * wide].astype(BF16)
        base = base + mids
    rows = [own5[1:2, :], own5[0:1, :]]
    for row in (1, 0):
        rows = rows + [own4[row : row + 1, p * wide : (p + 1) * wide] for p in range(chans // wide)]
    pad = out.shape[0] - base - len(rows)
    rows.append(jnp.zeros((pad, wide), F32))
    out[base:, :] = jnp.concatenate(rows, 0).astype(BF16)


def seventh_kernel(peers, pre1, e1, own6, rec6, own1, rec1, g1, im, dh1, out):
    half, wide = pre1.shape
    chans = im.shape[1]
    size = 2.0 * half
    count = size * (peers + 1)
    mean, inv = moments(own1, rec1, peers, size)
    sums, cross = totals(own6, rec6, peers)
    scale, slant, bias = back_coefs(g1[...], mean, inv, sums, cross, count)
    dh = (e1[...] * scale + pre1[...] * slant + bias).astype(BF16)
    dh1[...] = dh
    prod = tn(im[0:half, :], dh)
    other = tn(im[half:, :], dh)
    mid = chans // 2
    low = lower_half((mid, wide))
    first = prod[0:mid, :] + swap_halves(other[0:mid, :])
    second = swap_halves(prod[mid:, :]) + other[mid:, :]
    out[0:mid, :] = jnp.where(low, first, second).astype(BF16)
    pad = jnp.zeros((out.shape[0] - mid - 2, wide), F32)
    out[mid:, :] = jnp.concatenate([own6[1:2, :], own6[0:1, :], pad], 0).astype(BF16)


def images_kernel(cols, dh1, wpack, e3, out):
    half = dh1.shape[0]
    for at in range(0, half, cols):
        dh = dh1[at : at + cols, :]
        for side, base in ((0, at), (1, half + at)):
            back = nt(dh, wpack[side])
            out[base : base + cols, :] = (back + e3[base : base + cols, :]).astype(BF16)


def unpack_kernel(batch, early, tail, gwr, gwd, gwe, gg1, gs1, gg2, gs2, gg3, gs3):
    wide = tail.shape[1]
    mids = wide // 2
    chans = gwe.shape[1]
    parts = chans // wide
    mid = chans // 2
    late = tail[...].astype(F32) / batch
    gwr[0:mid, :] = late[0:mid, 0:mids]
    gwr[mid:, :] = swap_halves(late[0:mid, :])[:, 0:mids]
    gg1[...] = late[mid : mid + 1, 0:mids]
    gs1[...] = late[mid + 1 : mid + 2, 0:mids]
    soon = early[...].astype(F32) / batch
    for k in range(5):
        block = soon[k * mids : (k + 1) * mids, :]
        gwd[2 * k] = block[:, 0:mids]
        if k < 4:
            gwd[2 * k + 1] = swap_halves(block)[:, 0:mids]
    base = 5 * mids
    for part in range(parts):
        gwe[:, part * wide : (part + 1) * wide] = soon[base : base + mids, :]
        base = base + mids
    gg2[...] = soon[base : base + 1, 0:mids]
    gs2[...] = soon[base + 1 : base + 2, 0:mids]
    base = base + 2
    for ref in (gg3, gs3):
        for part in range(parts):
            ref[:, part * wide : (part + 1) * wide] = soon[base : base + 1, :]
            base = base + 1


def call(kernel, name, outs, *args, scratch=(), flops=0):
    size = sum(item.size * item.dtype.itemsize for item in args)
    size = size + sum(functools.reduce(lambda x, y: x * y, s, 1) * 4 for s, _ in outs)
    out = pl.pallas_call(
        kernel,
        name=name,
        out_shape=[jax.ShapeDtypeStruct(shape, kind) for shape, kind in outs],
        in_specs=[pl.BlockSpec(memory_space=pltpu.VMEM)] * len(args),
        out_specs=[pl.BlockSpec(memory_space=pltpu.VMEM)] * len(outs),
        scratch_shapes=list(scratch),
        cost_estimate=pl.CostEstimate(flops=flops, bytes_accessed=size, transcendentals=0),
        compiler_params=pltpu.CompilerParams(vmem_limit_bytes=24 * 1024 * 1024),
    )(*args)
    return out[0] if len(outs) == 1 else out


def swapped(value, axis, step):
    count = lax.axis_size(axis)
    return lax.ppermute(value, axis, [(i, (i + step) % count) for i in range(count)])


def exchange(msg, peers):
    if peers == 0:
        return msg
    if peers == 1:
        return swapped(msg, "space", 1)
    heads = [swapped(msg[0:HEAD], "space", k + 1) for k in range(peers)]
    if msg.shape[0] > HEAD:
        above = swapped(msg[HEAD:], "space", 1)
        below = swapped(msg[HEAD:], "space", peers)
        low = lax.broadcasted_iota(jnp.int32, above.shape, 1) < above.shape[1] // 2
        heads.append(jnp.where(low, above, below))
    return jnp.concatenate(heads, 0)


def summed_over(part, peers):
    total = part.astype(F32)
    for k in range(peers):
        total = total + swapped(part, "space", k + 1).astype(F32)
    count = lax.axis_size("dp")
    if count & (count - 1):
        return lax.psum(total, "dp")
    bit = 1
    while bit < count:
        part = total.astype(BF16)
        pairs = [(i, i ^ bit) for i in range(count)]
        total = part.astype(F32) + lax.ppermute(part, "dp", pairs).astype(F32)
        bit = 2 * bit
    return total


def shards(
    images, w_reduce, w_dilated, w_expand, gain_one, shift_one, gain_two, shift_two,
    gain_three, shift_three, cotangent,
):
    rows, cols, chans = images.shape[1:]
    mids = w_reduce.shape[1]
    wide = 2 * mids
    pixels = rows * cols
    half, edge = pixels // 2, 2 * cols
    ext_rows = half + 2 * edge
    count = lax.axis_size("space")
    peers = count - 1
    me = lax.axis_index("space")
    part = functools.partial
    im = images.reshape(pixels, chans)
    cot = cotangent.reshape(pixels, chans)
    pack = lambda row: jnp.tile(row, 2).reshape(1, wide)
    g1, s1, g2, s2 = pack(gain_one), pack(shift_one), pack(gain_two), pack(shift_two)
    g3, s3 = gain_three.reshape(1, chans), shift_three.reshape(1, chans)
    low = jnp.arange(wide) < mids
    mask = jnp.where(low, me > 0, me < count - 1).astype(F32).reshape(1, wide)
    gaps = lambda n: pltpu.VMEM((n, cols + 2 * GAP, wide), F32)
    chunks = half // cols

    pre1, own1, wpack = call(
        part(first_kernel, edge), "first",
        [((half, wide), F32), ((HEAD + edge, wide), F32), ((2, chans, wide), BF16)],
        im, w_reduce, flops=2 * pixels * chans * wide,
    )
    fwd, bwd = call(
        weights_kernel, "weights", [((3 * wide, 3 * wide), BF16)] * 2, w_dilated, flops=10**6
    )
    rec1 = exchange(own1, peers)
    ext, pre2, own2 = call(
        part(second_kernel, peers, edge), "second",
        [((ext_rows, wide), BF16), ((half, wide), F32), ((HEAD, wide), F32)],
        pre1, own1, rec1, g1, s1, mask, fwd,
        scratch=[gaps(2 * chunks)], flops=2 * half * 9 * wide * wide,
    )
    rec2 = exchange(own2, peers)
    act2, pre3, own3 = call(
        part(third_kernel, peers, cols), "third",
        [((half, wide), BF16), ((pixels, chans), F32), ((HEAD, chans), F32)],
        pre2, own2, rec2, g2, s2, w_expand, flops=2 * pixels * wide * chans,
    )
    rec3 = exchange(own3, peers)
    result, e3, own4 = call(
        part(fourth_kernel, peers, 64), "fourth",
        [((pixels, chans), BF16), ((pixels, chans), F32), ((HEAD, chans), F32)],
        pre3, own3, rec3, g3, s3, im, cot, flops=30 * pixels * chans,
    )
    rec4 = exchange(own4, peers)
    dh3, e2, own5 = call(
        part(fifth_kernel, peers, edge), "fifth",
        [((pixels, chans), BF16), ((half, wide), F32), ((HEAD + 2 * edge, wide), F32)],
        pre3, e3, own3, rec3, own4, rec4, g3, w_expand, pre2, own2, rec2, g2, s2,
        flops=2 * pixels * wide * chans,
    )
    rec5 = exchange(own5, peers)
    gwe = call(
        expand_kernel, "expand", [((mids, chans), F32)], act2, dh3, flops=2 * pixels * wide * chans
    )
    dext, e1, own6 = call(
        part(sixth_kernel, peers, edge), "sixth",
        [((ext_rows, wide), BF16), ((half, wide), F32), ((HEAD, wide), F32)],
        pre2, e2, own5, rec5, own2, rec2, g2, pre1, own1, rec1, g1, s1, mask, bwd,
        scratch=[gaps(2 * chunks)], flops=2 * half * 9 * wide * wide,
    )
    rec6 = exchange(own6, peers)
    early = call(
        part(dilated_kernel, edge), "dilated",
        [((5 * mids + chans // wide * mids + 16, wide), BF16)],
        ext, dext, gwe, own4, own5,
        scratch=[gaps(chunks), pltpu.VMEM((half, 3 * wide), BF16)],
        flops=2 * half * 9 * wide * wide,
    )
    dh1, tail = call(
        part(seventh_kernel, peers), "seventh",
        [((half, wide), BF16), ((chans // 2 + 16, wide), BF16)],
        pre1, e1, own6, rec6, own1, rec1, g1, im, flops=2 * pixels * wide * chans,
    )
    early_sum = summed_over(early, peers)
    tail_sum = summed_over(tail, peers)
    grad_images = call(
        part(images_kernel, cols), "images", [((pixels, chans), BF16)], dh1, wpack, e3,
        flops=2 * pixels * wide * chans,
    )
    grads = call(
        part(unpack_kernel, float(lax.axis_size("dp"))), "unpack",
        [((chans, mids), F32), ((9, mids, mids), F32), ((mids, chans), F32)]
        + [((1, mids), F32)] * 4 + [((1, chans), F32)] * 2,
        early_sum, tail_sum,
    )
    gwr, gwd, gwe = grads[:3]
    shape = images.shape
    return (
        result.reshape(shape), grad_images.reshape(shape), gwr, gwd.reshape(3, 3, mids, mids), gwe,
    ) + tuple(item.reshape(-1) for item in grads[3:])


def solution(mesh):
    big = P("dp", "space", None, None)
    return jax.shard_map(
        shards,
        mesh=mesh,
        in_specs=(big,) + (P(),) * 9 + (big,),
        out_specs=(big, big) + (P(),) * 9,
        check_vma=False,
    )
```

```python
import functools

import jax
import jax.numpy as jnp
from jax import lax
from jax.experimental import pallas as pl
from jax.experimental.pallas import tpu as pltpu
from jax.sharding import PartitionSpec as P

epsilon = 1e-05
F32 = jnp.float32
BF16 = jnp.bfloat16
HEAD = 8
GAP = 8


def nn(left, right):
    return jnp.dot(left, right, preferred_element_type=F32)


def nt(left, right):
    return lax.dot_general(left, right, (((1,), (1,)), ((), ())), preferred_element_type=F32)


def tn(left, right):
    return lax.dot_general(left, right, (((0,), (0,)), ((), ())), preferred_element_type=F32)


def swap_halves(value):
    return pltpu.roll(value, value.shape[1] // 2, 1)


def lower_half(shape):
    return lax.broadcasted_iota(jnp.int32, shape, 1) < shape[1] // 2


def both_halves(row):
    return row + swap_halves(row)


def rowsum(value):
    return jnp.sum(value, 0, keepdims=True)


def group(value):
    return jnp.sum(value.reshape(value.shape[0] // 8, 8, value.shape[1]), 0)


def silu(value):
    half = 0.5 * value
    return half + half * jnp.tanh(half)


def slope(value):
    half = 0.5 * value
    turn = jnp.tanh(half)
    return (0.5 + 0.5 * turn) * (1.0 + half * (1.0 - turn))


def moments(own, rec, peers, local):
    means = [own[0:1, :]] + [rec[HEAD * k : HEAD * k + 1, :] for k in range(peers)]
    squares = [own[1:2, :]] + [rec[HEAD * k + 1 : HEAD * k + 2, :] for k in range(peers)]
    mean = sum(means) / (peers + 1)
    total = sum(squares) + local * sum((item - mean) * (item - mean) for item in means)
    return mean, lax.rsqrt(total / (local * (peers + 1)) + epsilon)


def totals(own, rec, peers):
    sums = own[0:1, :] + sum(rec[HEAD * k : HEAD * k + 1, :] for k in range(peers))
    cross = own[1:2, :] + sum(rec[HEAD * k + 1 : HEAD * k + 2, :] for k in range(peers))
    return sums, cross


def head_rows(first, second):
    rest = jnp.zeros((HEAD - 2, first.shape[1]), F32)
    return jnp.concatenate([first, second, rest], 0)


def edges(ref, edge):
    size = ref.shape[0]
    top = ref[0:edge, :]
    return swap_halves(jnp.where(lower_half(top.shape), top, ref[size - edge : size, :]))


def fill_edges(ext, first, last, halo, edge):
    size = ext.shape[0]
    low = lower_half(halo.shape)
    halo = halo * edge_mask(halo.shape)
    ext[0:edge, :] = jnp.where(low, halo, swap_halves(last)).astype(BF16)
    ext[size - edge : size, :] = jnp.where(low, swap_halves(first), halo).astype(BF16)


def norm_coefs(gain, shift, mean, inv):
    scale = gain * inv
    return scale, shift - mean * scale


def back_coefs(gain, mean, inv, sums, cross, count):
    scale = gain * inv
    slant = -scale * inv * cross / count
    return scale, slant, -scale * sums / count - slant * mean


def centred_squares(ref, mean, step):
    acc = jnp.zeros((8, ref.shape[1]), F32)
    for at in range(0, ref.shape[0], step):
        gap = ref[at : at + step, :] - mean
        acc = acc + group(gap * gap)
    return rowsum(acc)


def first_kernel(edge, im, w, pre, msg, held, sems):
    half, cols = pre.shape[0], edge // 2
    order = [base + at for at in range(0, half, cols) for base in (0, half)]
    copies = []
    for k, base in enumerate(order):
        rows = pl.ds(base, cols)
        copies.append(pltpu.make_async_copy(im.at[rows, :], held.at[rows, :], sems.at[k]))
        copies[-1].start()
    weight = w[...]
    zero = jnp.zeros_like(weight)
    upper = jnp.concatenate([weight, zero], 0)
    lower = jnp.concatenate([zero, weight], 0)
    acc = jnp.zeros((8, pre.shape[1]), F32)
    for k, at in enumerate(range(0, half, cols)):
        copies[2 * k].wait()
        copies[2 * k + 1].wait()
        part = nt(held[at : at + cols, :], upper) + nt(held[half + at : half + at + cols, :], lower)
        pre[at : at + cols, :] = part
        acc = acc + group(part)
    mean = both_halves(rowsum(acc)) / (2 * half)
    msg[0:HEAD, :] = head_rows(mean, both_halves(centred_squares(pre, mean, cols)))
    msg[HEAD:, :] = edges(pre, edge)


def tap_blocks(w):
    mids = w.shape[-1]
    zero = jnp.zeros((mids, mids), BF16)
    for a in range(3):
        for b in range(3):
            block = w[a, b]
            yield a, b, jnp.concatenate(
                [jnp.concatenate([block, zero], 1), jnp.concatenate([zero, block], 1)], 0
            )


def weights_kernel(w, we, g1, s1, g2, s2, g3, s3, fwd, held, prm):
    wide = 2 * w.shape[-1]
    for a, b, both in tap_blocks(w):
        fwd[a * wide : (a + 1) * wide, b * wide : (b + 1) * wide] = both
    held[...] = we[...]
    prm[...] = jnp.zeros(prm.shape, F32)
    for k, ref in enumerate((g1, s1, g2, s2)):
        prm[k : k + 1, 0:wide] = jnp.concatenate([ref[...], ref[...]], 1)
    prm[4:5, :] = g3[...]
    prm[5:6, :] = s3[...]


def gain_shift(prm, norm, wide):
    return prm[2 * norm : 2 * norm + 1, 0:wide], prm[2 * norm + 1 : 2 * norm + 2, 0:wide]


def edge_mask(shape):
    me = lax.axis_index("space")
    above = jnp.where(me > 0, 1.0, 0.0)
    below = jnp.where(me < lax.axis_size("space") - 1, 1.0, 0.0)
    return jnp.where(lower_half(shape), above, below)


def taps(ext, edge, at, cols):
    return jnp.concatenate([ext[a * edge + at : a * edge + at + cols, :] for a in range(3)], 1)


def clear_gaps(scr, cols):
    zero = jnp.zeros((scr.shape[0], GAP, scr.shape[2]), F32)
    scr[:, 0:GAP, :] = zero
    scr[:, GAP + cols :, :] = zero


def second_kernel(
    peers, edge, pre1, own1, rec1, prm, w, cot, ext, pre2, msg, held, scr, sem
):
    half, cols, wide = pre2.shape[0], edge // 2, pre2.shape[1]
    fetch = pltpu.make_async_copy(cot, held, sem)
    fetch.start()
    g1, s1 = gain_shift(prm, 0, wide)
    mean, inv = moments(own1, rec1, peers, 2.0 * half)
    scale, bias = norm_coefs(g1, s1, mean, inv)
    clear_gaps(scr, cols)
    last = first = None
    acts = []
    for at in range(0, half, cols):
        act = silu(pre1[at : at + cols, :] * scale + bias)
        ext[edge + at : edge + at + cols, :] = act.astype(BF16)
        if at < edge or at >= half - edge:
            acts.append((at, act))
    first = jnp.concatenate([act for at, act in acts if at < edge], 0)
    last = jnp.concatenate([act for at, act in acts if at >= half - edge], 0)
    halo = silu(rec1[HEAD * peers :, :] * scale + bias) if peers else jnp.zeros((edge, wide), F32)
    fill_edges(ext, first, last, halo, edge)
    acc = jnp.zeros((8, wide), F32)
    for i, at in enumerate(range(0, half, cols)):
        out = nn(taps(ext, edge, at, cols), w[...])
        scr[2 * i, GAP : GAP + cols, :] = out[:, 0:wide]
        scr[2 * i + 1, GAP : GAP + cols, :] = out[:, 2 * wide :]
        part = (
            out[:, wide : 2 * wide]
            + scr[2 * i, GAP - 2 : GAP - 2 + cols, :]
            + scr[2 * i + 1, GAP + 2 : GAP + 2 + cols, :]
        )
        pre2[at : at + cols, :] = part
        acc = acc + group(part)
    mean = both_halves(rowsum(acc)) / (2 * half)
    msg[...] = head_rows(mean, both_halves(centred_squares(pre2, mean, cols)))
    fetch.wait()


def third_kernel(peers, cols, pre2, own2, rec2, prm, w, act2, pre3, msg):
    half = pre2.shape[0]
    g2, s2 = gain_shift(prm, 1, pre2.shape[1])
    mean, inv = moments(own2, rec2, peers, 2.0 * half)
    scale, bias = norm_coefs(g2, s2, mean, inv)
    weight = w[...]
    zero = jnp.zeros_like(weight)
    upper = jnp.concatenate([weight, zero], 0)
    lower = jnp.concatenate([zero, weight], 0)
    acc = jnp.zeros((8, pre3.shape[1]), F32)
    for at in range(0, half, cols):
        act = silu(pre2[at : at + cols, :] * scale + bias).astype(BF16)
        act2[at : at + cols, :] = act
        part = nn(act, upper)
        pre3[at : at + cols, :] = part
        acc = acc + group(part)
        part = nn(act, lower)
        pre3[half + at : half + at + cols, :] = part
        acc = acc + group(part)
    mean = rowsum(acc) / (2 * half)
    msg[...] = head_rows(mean, centred_squares(pre3, mean, cols))


def halved_coefs(peers, own3, rec3, prm, size):
    mean, inv = moments(own3, rec3, peers, float(size))
    gain, shift = gain_shift(prm, 2, own3.shape[1])
    scale, bias = norm_coefs(gain, shift, mean, inv)
    return 0.5 * scale, 0.5 * bias, mean, inv


def fourth_kernel(peers, step, pre3, own3, rec3, prm, im, cot, e3, msg):
    size, chans = pre3.shape
    scale, bias, mean, inv = halved_coefs(peers, own3, rec3, prm, size)

    def body(i, carry):
        sums, cross = carry
        at = pl.ds(pl.multiple_of(i * step, step), step)
        pre = pre3[at, :]
        half = pre * scale + (bias + 0.5 * im[at, :].astype(F32))
        turn = jnp.tanh(half)
        grad = cot[at, :].astype(F32) * ((0.5 + 0.5 * turn) * (1.0 + half * (1.0 - turn)))
        e3[at, :] = grad
        return sums + group(grad), cross + group(grad * (pre - mean))

    zero = jnp.zeros((8, chans), F32)
    sums, cross = lax.fori_loop(0, size // step, body, (zero, zero), unroll=2)
    msg[...] = head_rows(rowsum(sums), rowsum(cross) * inv)


def result_kernel(peers, step, pre3, own3, rec3, prm, im, out):
    size = pre3.shape[0]
    scale, bias, _, _ = halved_coefs(peers, own3, rec3, prm, size)

    def body(i, carry):
        at = pl.ds(pl.multiple_of(i * step, step), step)
        half = pre3[at, :] * scale + (bias + 0.5 * im[at, :].astype(F32))
        out[at, :] = (half + half * jnp.tanh(half)).astype(BF16)
        return carry

    lax.fori_loop(0, size // step, body, 0, unroll=2)


def fifth_kernel(
    peers, edge, pre3, e3, own3, rec3, own4, rec4, prm, w, pre2, own2, rec2, dh3, e2, msg
):
    size, half, cols, wide = pre3.shape[0], pre2.shape[0], edge // 2, pre2.shape[1]
    count = float(size * (peers + 1))
    g2, s2 = gain_shift(prm, 1, wide)
    g3, _ = gain_shift(prm, 2, pre3.shape[1])
    mean3, inv3 = moments(own3, rec3, peers, float(size))
    sums3, cross3 = totals(own4, rec4, peers)
    scale3, slant3, bias3 = back_coefs(g3, mean3, inv3, sums3, cross3, count)
    mean, inv = moments(own2, rec2, peers, float(size))
    scale, bias = norm_coefs(g2, s2, mean, inv)
    weight = w[...]
    zero = jnp.zeros_like(weight)
    upper = jnp.concatenate([weight, zero], 0)
    lower = jnp.concatenate([zero, weight], 0)
    sums = jnp.zeros((8, wide), F32)
    cross = jnp.zeros((8, wide), F32)
    for at in range(0, half, cols):
        back = None
        for base, side in ((at, upper), (half + at, lower)):
            rows = slice(base, base + cols)
            dh = (e3[rows, :] * scale3 + pre3[rows, :] * slant3 + bias3).astype(BF16)
            dh3[rows, :] = dh
            part = nt(dh, side)
            back = part if back is None else back + part
        pre = pre2[at : at + cols, :]
        grad = back * slope(pre * scale + bias)
        e2[at : at + cols, :] = grad
        sums = sums + group(grad)
        cross = cross + group(grad * (pre - mean))
    msg[0:HEAD, :] = head_rows(both_halves(rowsum(sums)), both_halves(rowsum(cross) * inv))
    msg[HEAD : HEAD + edge, :] = edges(e2, edge)
    msg[HEAD + edge :, :] = edges(pre2, edge)


def expand_kernel(act2, dh3, w, out, bwd):
    half = act2.shape[0]
    mids, wide = act2.shape[1] // 2, act2.shape[1]
    out[...] = tn(act2[...], dh3[0:half, :])[0:mids, :] + tn(act2[...], dh3[half:, :])[mids:, :]
    for a, b, both in tap_blocks(w):
        k = 2 - a
        bwd[b * wide : (b + 1) * wide, k * wide : (k + 1) * wide] = both


def sixth_kernel(
    peers, edge, pre2, e2, own5, rec5, own2, rec2, pre1, own1, rec1, prm, w,
    dext, e1, msg, scr,
):
    half, cols, wide = pre2.shape[0], edge // 2, pre2.shape[1]
    size = 2.0 * half
    count = size * (peers + 1)
    g1, s1 = gain_shift(prm, 0, wide)
    g2, _ = gain_shift(prm, 1, wide)
    mean2, inv2 = moments(own2, rec2, peers, size)
    sums2, cross2 = totals(own5, rec5, peers)
    scale2, slant2, bias2 = back_coefs(g2, mean2, inv2, sums2, cross2, count)
    mean, inv = moments(own1, rec1, peers, size)
    scale, bias = norm_coefs(g1, s1, mean, inv)
    clear_gaps(scr, cols)
    acts = []
    for at in range(0, half, cols):
        dh = e2[at : at + cols, :] * scale2 + pre2[at : at + cols, :] * slant2 + bias2
        dext[edge + at : edge + at + cols, :] = dh.astype(BF16)
        if at < edge or at >= half - edge:
            acts.append((at, dh))
    first = jnp.concatenate([act for at, act in acts if at < edge], 0)
    last = jnp.concatenate([act for at, act in acts if at >= half - edge], 0)
    if peers:
        base = HEAD * peers
        halo = rec5[base : base + edge, :] * scale2 + rec5[base + edge :, :] * slant2 + bias2
    else:
        halo = jnp.zeros((edge, wide), F32)
    fill_edges(dext, first, last, halo, edge)
    sums = jnp.zeros((8, wide), F32)
    cross = jnp.zeros((8, wide), F32)
    for i, at in enumerate(range(0, half, cols)):
        out = nt(taps(dext, edge, at, cols), w[...])
        scr[2 * i, GAP : GAP + cols, :] = out[:, 0:wide]
        scr[2 * i + 1, GAP : GAP + cols, :] = out[:, 2 * wide :]
        back = (
            out[:, wide : 2 * wide]
            + scr[2 * i, GAP + 2 : GAP + 2 + cols, :]
            + scr[2 * i + 1, GAP - 2 : GAP - 2 + cols, :]
        )
        pre = pre1[at : at + cols, :]
        grad = back * slope(pre * scale + bias)
        e1[at : at + cols, :] = grad
        sums = sums + group(grad)
        cross = cross + group(grad * (pre - mean))
    msg[...] = head_rows(both_halves(rowsum(sums)), both_halves(rowsum(cross) * inv))


def fold(block, upper):
    mids = block.shape[0] // 2
    if upper:
        return swap_halves(block[0:mids, :]) + block[mids:, :]
    return block[0:mids, :] + swap_halves(block[mids:, :])


def dilated_kernel(edge, ext, dext, out, scr, dcat):
    cols, wide = edge // 2, ext.shape[1]
    half = dext.shape[0] - 2 * edge
    mids = wide // 2
    clear_gaps(scr, cols)
    for i, at in enumerate(range(0, half, cols)):
        mid = dext[edge + at : edge + at + cols, :]
        scr[i, GAP : GAP + cols, :] = mid.astype(F32)
        dcat[at : at + cols, 0:wide] = scr[i, GAP + 2 : GAP + 2 + cols, :].astype(BF16)
        dcat[at : at + cols, wide : 2 * wide] = mid
        dcat[at : at + cols, 2 * wide :] = scr[i, GAP - 2 : GAP - 2 + cols, :].astype(BF16)
    blocks = []
    for a in range(3):
        prod = tn(ext[a * edge : a * edge + half, :], dcat[...])
        blocks = blocks + [prod[:, b * wide : (b + 1) * wide] for b in range(3)]
    low = lower_half((mids, wide))
    for k in range(4):
        pair = jnp.where(low, fold(blocks[2 * k], False), fold(blocks[2 * k + 1], True))
        out[k * mids : (k + 1) * mids, :] = pair.astype(BF16)
    out[4 * mids : 5 * mids, :] = fold(blocks[8], False).astype(BF16)


def seventh_kernel(
    peers, pre1, e1, own6, rec6, own1, rec1, prm, im, gwd, gwe, own4, own5, dh1, *rest
):
    outs, scr = rest[:-1], rest[-1]
    half, wide = pre1.shape
    mids, chans = wide // 2, im.shape[1]
    size = 2.0 * half
    count = size * (peers + 1)
    g1, _ = gain_shift(prm, 0, wide)
    mean, inv = moments(own1, rec1, peers, size)
    sums, cross = totals(own6, rec6, peers)
    scale, slant, bias = back_coefs(g1, mean, inv, sums, cross, count)
    dh = (e1[...] * scale + pre1[...] * slant + bias).astype(BF16)
    dh1[...] = dh
    prod = tn(dh, im[0:half, :])[0:mids, :] + tn(dh, im[half:, :])[mids:, :]
    base = gwd.shape[0]
    scr[0:base, :] = gwd[...]
    for whole in (prod, gwe[...]):
        for part in range(chans // wide):
            scr[base : base + mids, :] = whole[:, part * wide : (part + 1) * wide].astype(BF16)
            base = base + mids
    rows = [own6[1:2, :], own6[0:1, :], own5[1:2, :], own5[0:1, :]]
    for row in (1, 0):
        rows = rows + [own4[row : row + 1, p * wide : (p + 1) * wide] for p in range(chans // wide)]
    rows.append(jnp.zeros((scr.shape[0] - base - len(rows), wide), F32))
    scr[base:, :] = jnp.concatenate(rows, 0).astype(BF16)
    me = lax.axis_index("space")
    for k, out in enumerate(outs):
        piece = out.shape[0]
        start = lax.rem(me + k, peers + 1) * piece
        out[...] = scr[pl.ds(pl.multiple_of(start, 16), piece), :]


def images_kernel(cols, dh1, w, e3, out):
    half = dh1.shape[0]
    weight = w[...]
    zero = jnp.zeros_like(weight)
    sides = (jnp.concatenate([weight, zero], 0), jnp.concatenate([zero, weight], 0))
    for at in range(0, half, cols):
        dh = dh1[at : at + cols, :]
        for side, base in zip(sides, (at, half + at)):
            out[base : base + cols, :] = (nn(dh, side) + e3[base : base + cols, :]).astype(BF16)


def unpack_kernel(peers, batch, *refs):
    pieces, refs = refs[: peers + 1], refs[peers + 1 :]
    gwr, gwd, gwe, gg1, gs1, gg2, gs2, gg3, gs3, scr = refs
    wide = scr.shape[1]
    mids = wide // 2
    chans = gwe.shape[1]
    parts = chans // wide
    me = lax.axis_index("space")
    for k, ref in enumerate(pieces):
        piece = ref.shape[0]
        start = lax.rem(me + peers + 1 - k, peers + 1) * piece
        scr[pl.ds(pl.multiple_of(start, 16), piece), :] = ref[...].astype(F32) / batch
    for k in range(5):
        block = scr[k * mids : (k + 1) * mids, :]
        gwd[2 * k] = block[:, 0:mids]
        if k < 4:
            gwd[2 * k + 1] = swap_halves(block)[:, 0:mids]
    base = 5 * mids
    for ref in (gwr, gwe):
        for part in range(parts):
            ref[:, part * wide : (part + 1) * wide] = scr[base : base + mids, :]
            base = base + mids
    for ref in (gg1, gs1, gg2, gs2):
        ref[...] = scr[base : base + 1, 0:mids]
        base = base + 1
    for ref in (gg3, gs3):
        for part in range(parts):
            ref[:, part * wide : (part + 1) * wide] = scr[base : base + 1, :]
            base = base + 1


HBM = pl.BlockSpec(memory_space=pltpu.HBM)
VMEM = pl.BlockSpec(memory_space=pltpu.VMEM)


def call(kernel, name, outs, *args, scratch=(), flops=0, far=(), final=False):
    size = sum(item.size * item.dtype.itemsize for item in args)
    size = size + sum(functools.reduce(lambda x, y: x * y, s, 1) * 4 for s, _ in outs)
    kind_of = jax.ShapeDtypeStruct if final else pltpu.VMEM
    out = pl.pallas_call(
        kernel,
        name=name,
        out_shape=[kind_of(shape, kind) for shape, kind in outs],
        in_specs=[HBM if k in far else VMEM for k in range(len(args))],
        out_specs=[VMEM] * len(outs),
        scratch_shapes=list(scratch),
        cost_estimate=pl.CostEstimate(flops=flops, bytes_accessed=size, transcendentals=0),
        compiler_params=pltpu.CompilerParams(vmem_limit_bytes=16 * 1024 * 1024),
    )(*args)
    return out[0] if len(outs) == 1 else out


def swapped(value, axis, step):
    count = lax.axis_size(axis)
    return lax.ppermute(value, axis, [(i, (i + step) % count) for i in range(count)])


def exchange(msg, peers):
    if peers == 0:
        return msg
    if peers == 1:
        return swapped(msg, "space", 1)
    heads = [swapped(msg[0:HEAD], "space", k + 1) for k in range(peers)]
    if msg.shape[0] > HEAD:
        above = swapped(msg[HEAD:], "space", 1)
        below = swapped(msg[HEAD:], "space", peers)
        low = lax.broadcasted_iota(jnp.int32, above.shape, 1) < above.shape[1] // 2
        heads.append(jnp.where(low, above, below))
    return jnp.concatenate(heads, 0)


def summed_over_dp(part):
    count, sides = lax.axis_size("dp"), lax.axis_size("space")
    if count & (count - 1):
        return lax.psum(part.astype(F32), "dp").astype(BF16)
    bits = [1 << k for k in range(count.bit_length() - 1)]
    for k in range(len(bits)):
        pairs = []
        for i in range(count * sides):
            dp, side = divmod(i, sides)
            bit = bits[(k + side * (len(bits) // 2)) % len(bits)]
            pairs.append((i, (dp ^ bit) * sides + side))
        got = lax.ppermute(part, ("dp", "space"), pairs)
        part = (part.astype(F32) + got.astype(F32)).astype(BF16)
    return part


def shards(
    images, w_reduce, w_dilated, w_expand, gain_one, shift_one, gain_two, shift_two,
    gain_three, shift_three, cotangent,
):
    rows, cols, chans = images.shape[1:]
    mids = w_reduce.shape[1]
    wide = 2 * mids
    pixels = rows * cols
    half, edge = pixels // 2, 2 * cols
    ext_rows = half + 2 * edge
    count = lax.axis_size("space")
    peers = count - 1
    part = functools.partial
    im = images.reshape(pixels, chans)
    cot = cotangent.reshape(pixels, chans)
    row = lambda item: item.reshape(1, -1)
    gaps = lambda n: pltpu.VMEM((n, cols + 2 * GAP, wide), F32)
    chunks = half // cols
    w_rows = w_reduce.T
    gates = 2 * pixels * wide * chans

    pre1, own1, im_held = call(
        part(first_kernel, edge), "first",
        [((half, wide), F32), ((HEAD + edge, wide), F32), ((pixels, chans), BF16)],
        im, w_rows, flops=gates, far=(0,), scratch=[pltpu.SemaphoreType.DMA((2 * chunks,))],
    )
    fwd, we, prm = call(
        weights_kernel, "weights",
        [((3 * wide, 3 * wide), BF16), ((mids, chans), BF16), ((8, chans), F32)],
        w_dilated, w_expand, row(gain_one), row(shift_one), row(gain_two), row(shift_two),
        row(gain_three), row(shift_three), flops=10**6,
    )
    rec1 = exchange(own1, peers)
    ext, pre2, own2, cot_held = call(
        part(second_kernel, peers, edge), "second",
        [((ext_rows, wide), BF16), ((half, wide), F32), ((HEAD, wide), F32), ((pixels, chans), BF16)],
        pre1, own1, rec1, prm, fwd, cot, far=(5,),
        scratch=[gaps(2 * chunks), pltpu.SemaphoreType.DMA], flops=2 * half * 9 * wide * wide,
    )
    rec2 = exchange(own2, peers)
    act2, pre3, own3 = call(
        part(third_kernel, peers, cols), "third",
        [((half, wide), BF16), ((pixels, chans), F32), ((HEAD, chans), F32)],
        pre2, own2, rec2, prm, we, flops=gates,
    )
    rec3 = exchange(own3, peers)
    e3, own4 = call(
        part(fourth_kernel, peers, 64), "fourth", [((pixels, chans), F32), ((HEAD, chans), F32)],
        pre3, own3, rec3, prm, im_held, cot_held, flops=30 * pixels * chans,
    )
    rec4 = exchange(own4, peers)
    dh3, e2, own5 = call(
        part(fifth_kernel, peers, edge), "fifth",
        [((pixels, chans), BF16), ((half, wide), F32), ((HEAD + 2 * edge, wide), F32)],
        pre3, e3, own3, rec3, own4, rec4, prm, we, pre2, own2, rec2, flops=gates,
    )
    rec5 = exchange(own5, peers)
    gwe, bwd = call(
        expand_kernel, "expand", [((mids, chans), F32), ((3 * wide, 3 * wide), BF16)],
        act2, dh3, w_dilated, flops=gates,
    )
    dext, e1, own6 = call(
        part(sixth_kernel, peers, edge), "sixth",
        [((ext_rows, wide), BF16), ((half, wide), F32), ((HEAD, wide), F32)],
        pre2, e2, own5, rec5, own2, rec2, pre1, own1, rec1, prm, bwd,
        scratch=[gaps(2 * chunks)], flops=2 * half * 9 * wide * wide,
    )
    rec6 = exchange(own6, peers)
    gwd = call(
        part(dilated_kernel, edge), "dilated", [((5 * mids, wide), BF16)], ext, dext,
        scratch=[gaps(chunks), pltpu.VMEM((half, 3 * wide), BF16)],
        flops=2 * half * 9 * wide * wide,
    )
    length = 5 * mids + 2 * (chans // wide) * mids + 16
    piece = -(-length // (16 * count)) * 16
    dh1, *pieces = call(
        part(seventh_kernel, peers), "seventh",
        [((half, wide), BF16)] + [((piece, wide), BF16)] * count,
        pre1, e1, own6, rec6, own1, rec1, prm, im_held, gwd, gwe, own4, own5, flops=gates,
        scratch=[pltpu.VMEM((piece * count, wide), BF16)],
    )
    total = pieces[0].astype(F32)
    for k in range(peers):
        total = total + swapped(pieces[k + 1], "space", k + 1).astype(F32)
    total = summed_over_dp(total.astype(BF16))
    whole = [total] + [swapped(total, "space", k + 1) for k in range(peers)]
    grad_images = call(
        part(images_kernel, cols), "images", [((pixels, chans), BF16)], dh1, w_rows, e3,
        flops=gates, final=True,
    )
    result = call(
        part(result_kernel, peers, 64), "result", [((pixels, chans), BF16)],
        pre3, own3, rec3, prm, im_held, flops=10 * pixels * chans, final=True,
    )
    grads = call(
        part(unpack_kernel, peers, float(lax.axis_size("dp"))), "unpack",
        [((mids, chans), F32), ((9, mids, mids), F32), ((mids, chans), F32)]
        + [((1, mids), F32)] * 4 + [((1, chans), F32)] * 2,
        *whole, scratch=[pltpu.VMEM((piece * count, wide), F32)], final=True,
    )
    gwr, gwd, gwe = grads[:3]
    shape = images.shape
    return (
        result.reshape(shape), grad_images.reshape(shape), gwr.T, gwd.reshape(3, 3, mids, mids), gwe,
    ) + tuple(item.reshape(-1) for item in grads[3:])


def solution(mesh):
    big = P("dp", "space", None, None)
    return jax.shard_map(
        shards,
        mesh=mesh,
        in_specs=(big,) + (P(),) * 9 + (big,),
        out_specs=(big, big) + (P(),) * 9,
        check_vma=False,
    )
```

```python
import functools

import jax
import jax.numpy as jnp
from jax import lax
from jax.experimental import pallas as pl
from jax.experimental.pallas import tpu as pltpu
from jax.sharding import PartitionSpec as P

epsilon = 1e-05
F32 = jnp.float32
BF16 = jnp.bfloat16
HEAD = 8
WIDE_HEAD = 16
GAP = 8


def nn(left, right):
    return jnp.dot(left, right, preferred_element_type=F32)


def nt(left, right):
    return lax.dot_general(left, right, (((1,), (1,)), ((), ())), preferred_element_type=F32)


def tn(left, right):
    return lax.dot_general(left, right, (((0,), (0,)), ((), ())), preferred_element_type=F32)


def swap_halves(value):
    return pltpu.roll(value, value.shape[1] // 2, 1)


def lower_half(shape):
    return lax.broadcasted_iota(jnp.int32, shape, 1) < shape[1] // 2


def both_halves(row):
    return row + swap_halves(row)


def rowsum(value):
    return jnp.sum(value, 0, keepdims=True)


def group(value):
    return jnp.sum(value.reshape(value.shape[0] // 8, 8, value.shape[1]), 0)


def silu(value):
    half = 0.5 * value
    return half + half * jnp.tanh(half)


def slope(value):
    half = 0.5 * value
    turn = jnp.tanh(half)
    return (0.5 + 0.5 * turn) * (1.0 + half * (1.0 - turn))


def head_row(ref, item, which):
    if ref.dtype == BF16:
        terms = ref[WIDE_HEAD * item : WIDE_HEAD * (item + 1), :].astype(F32)
        at = 3 * which
        return terms[at : at + 1, :] + terms[at + 1 : at + 2, :] + terms[at + 2 : at + 3, :]
    at = HEAD * item + which
    return ref[at : at + 1, :]


def moments(own, rec, peers, local):
    means = [head_row(own, 0, 0)] + [head_row(rec, k, 0) for k in range(peers)]
    squares = [head_row(own, 0, 1)] + [head_row(rec, k, 1) for k in range(peers)]
    mean = sum(means) / (peers + 1)
    total = sum(squares) + local * sum((item - mean) * (item - mean) for item in means)
    return mean, lax.rsqrt(total / (local * (peers + 1)) + epsilon)


def totals(own, rec, peers):
    sums = head_row(own, 0, 0) + sum(head_row(rec, k, 0) for k in range(peers))
    cross = head_row(own, 0, 1) + sum(head_row(rec, k, 1) for k in range(peers))
    return sums, cross


def head_rows(first, second):
    rest = jnp.zeros((HEAD - 2, first.shape[1]), F32)
    return jnp.concatenate([first, second, rest], 0)


def three_terms(value):
    high = value.astype(BF16).astype(F32)
    mid = (value - high).astype(BF16).astype(F32)
    return [high, mid, value - high - mid]


def wide_head_rows(first, second):
    rest = jnp.zeros((WIDE_HEAD - 6, first.shape[1]), F32)
    return jnp.concatenate(three_terms(first) + three_terms(second) + [rest], 0).astype(BF16)


def edges(ref, edge, centre=0.0):
    size = ref.shape[0]
    top = ref[0:edge, :]
    return swap_halves(jnp.where(lower_half(top.shape), top, ref[size - edge : size, :]) - centre)


def fill_edges(ext, first, last, halo, edge):
    size = ext.shape[0]
    low = lower_half(halo.shape)
    halo = halo * edge_mask(halo.shape)
    ext[0:edge, :] = jnp.where(low, halo, swap_halves(last)).astype(BF16)
    ext[size - edge : size, :] = jnp.where(low, swap_halves(first), halo).astype(BF16)


def norm_coefs(gain, shift, mean, inv):
    scale = gain * inv
    return scale, shift - mean * scale


def back_coefs(gain, mean, inv, sums, cross, count):
    scale = gain * inv
    slant = -scale * inv * cross / count
    return scale, slant, -scale * sums / count - slant * mean


def centred_squares(ref, mean, step):
    acc = jnp.zeros((8, ref.shape[1]), F32)
    for at in range(0, ref.shape[0], step):
        gap = ref[at : at + step, :] - mean
        acc = acc + group(gap * gap)
    return rowsum(acc)


def first_kernel(edge, im, w, wd, pre, msg, held, w_held, wd_held, sems):
    half, cols = pre.shape[0], edge // 2
    fetch_w = pltpu.make_async_copy(w, w_held, sems.at[sems.shape[0] - 1])
    fetch_w.start()
    order = [base + at for at in range(0, half, cols) for base in (0, half)]
    copies = []
    for k, base in enumerate(order):
        rows = pl.ds(base, cols)
        copies.append(pltpu.make_async_copy(im.at[rows, :], held.at[rows, :], sems.at[k]))
        copies[-1].start()
    fetch_wd = pltpu.make_async_copy(wd, wd_held, sems.at[sems.shape[0] - 2])
    fetch_wd.start()
    fetch_w.wait()
    weight = w_held[...]
    zero = jnp.zeros_like(weight)
    upper = jnp.concatenate([weight, zero], 0)
    lower = jnp.concatenate([zero, weight], 0)
    acc = jnp.zeros((8, pre.shape[1]), F32)
    for k, at in enumerate(range(0, half, cols)):
        copies[2 * k].wait()
        copies[2 * k + 1].wait()
        part = nt(held[at : at + cols, :], upper) + nt(held[half + at : half + at + cols, :], lower)
        pre[at : at + cols, :] = part
        acc = acc + group(part)
    mean = both_halves(rowsum(acc)) / (2 * half)
    msg[0:WIDE_HEAD, :] = wide_head_rows(mean, both_halves(centred_squares(pre, mean, cols)))
    msg[WIDE_HEAD:, :] = edges(pre, edge, mean).astype(BF16)
    fetch_wd.wait()


def tap_blocks(w):
    mids = w.shape[-1]
    zero = jnp.zeros((mids, mids), BF16)
    for a in range(3):
        for b in range(3):
            block = w[a, b]
            yield a, b, jnp.concatenate(
                [jnp.concatenate([block, zero], 1), jnp.concatenate([zero, block], 1)], 0
            )


def weights_kernel(w, we, g1, s1, g2, s2, g3, s3, fwd, held, prm):
    wide = 2 * w.shape[-1]
    for a, b, both in tap_blocks(w):
        fwd[a * wide : (a + 1) * wide, b * wide : (b + 1) * wide] = both
    held[...] = we[...]
    prm[...] = jnp.zeros(prm.shape, F32)
    for k, ref in enumerate((g1, s1, g2, s2)):
        prm[k : k + 1, 0:wide] = jnp.concatenate([ref[...], ref[...]], 1)
    prm[4:5, :] = g3[...]
    prm[5:6, :] = s3[...]


def gain_shift(prm, norm, wide):
    return prm[2 * norm : 2 * norm + 1, 0:wide], prm[2 * norm + 1 : 2 * norm + 2, 0:wide]


def edge_mask(shape):
    me = lax.axis_index("space")
    above = jnp.where(me > 0, 1.0, 0.0)
    below = jnp.where(me < lax.axis_size("space") - 1, 1.0, 0.0)
    return jnp.where(lower_half(shape), above, below)


def taps(ext, edge, at, cols):
    return jnp.concatenate([ext[a * edge + at : a * edge + at + cols, :] for a in range(3)], 1)


def clear_gaps(scr, cols):
    zero = jnp.zeros((scr.shape[0], GAP, scr.shape[2]), F32)
    scr[:, 0:GAP, :] = zero
    scr[:, GAP + cols :, :] = zero


def second_kernel(
    peers, edge, pre1, own1, rec1, prm, w, cot, ext, pre2, msg, held, scr, sem
):
    half, cols, wide = pre2.shape[0], edge // 2, pre2.shape[1]
    fetch = pltpu.make_async_copy(cot, held, sem)
    fetch.start()
    g1, s1 = gain_shift(prm, 0, wide)
    mean, inv = moments(own1, rec1, peers, 2.0 * half)
    scale, bias = norm_coefs(g1, s1, mean, inv)
    clear_gaps(scr, cols)
    last = first = None
    acts = []
    for at in range(0, half, cols):
        act = silu(pre1[at : at + cols, :] * scale + bias)
        ext[edge + at : edge + at + cols, :] = act.astype(BF16)
        if at < edge or at >= half - edge:
            acts.append((at, act))
    first = jnp.concatenate([act for at, act in acts if at < edge], 0)
    last = jnp.concatenate([act for at, act in acts if at >= half - edge], 0)
    if peers:
        above, below = head_row(rec1, 0, 0), head_row(rec1, peers - 1, 0)
        centre = jnp.where(lower_half(above.shape), above, below)
        halo = silu((rec1[WIDE_HEAD * peers :, :].astype(F32) + centre) * scale + bias)
    else:
        halo = jnp.zeros((edge, wide), F32)
    fill_edges(ext, first, last, halo, edge)
    acc = jnp.zeros((8, wide), F32)
    for i, at in enumerate(range(0, half, cols)):
        out = nn(taps(ext, edge, at, cols), w[...])
        scr[2 * i, GAP : GAP + cols, :] = out[:, 0:wide]
        scr[2 * i + 1, GAP : GAP + cols, :] = out[:, 2 * wide :]
        part = (
            out[:, wide : 2 * wide]
            + scr[2 * i, GAP - 2 : GAP - 2 + cols, :]
            + scr[2 * i + 1, GAP + 2 : GAP + 2 + cols, :]
        )
        pre2[at : at + cols, :] = part
        acc = acc + group(part)
    mean = both_halves(rowsum(acc)) / (2 * half)
    msg[...] = head_rows(mean, both_halves(centred_squares(pre2, mean, cols)))
    fetch.wait()


def third_kernel(peers, cols, pre2, own2, rec2, prm, w, act2, pre3, msg):
    half = pre2.shape[0]
    g2, s2 = gain_shift(prm, 1, pre2.shape[1])
    mean, inv = moments(own2, rec2, peers, 2.0 * half)
    scale, bias = norm_coefs(g2, s2, mean, inv)
    weight = w[...]
    zero = jnp.zeros_like(weight)
    upper = jnp.concatenate([weight, zero], 0)
    lower = jnp.concatenate([zero, weight], 0)
    acc = jnp.zeros((8, pre3.shape[1]), F32)
    for at in range(0, half, cols):
        act = silu(pre2[at : at + cols, :] * scale + bias).astype(BF16)
        act2[at : at + cols, :] = act
        part = nn(act, upper)
        pre3[at : at + cols, :] = part
        acc = acc + group(part)
        part = nn(act, lower)
        pre3[half + at : half + at + cols, :] = part
        acc = acc + group(part)
    mean = rowsum(acc) / (2 * half)
    msg[...] = head_rows(mean, centred_squares(pre3, mean, cols))


def halved_coefs(peers, own3, rec3, prm, size):
    mean, inv = moments(own3, rec3, peers, float(size))
    gain, shift = gain_shift(prm, 2, own3.shape[1])
    scale, bias = norm_coefs(gain, shift, mean, inv)
    return 0.5 * scale, 0.5 * bias, mean, inv


def fourth_kernel(peers, step, pre3, own3, rec3, prm, im, cot, e3, msg):
    size, chans = pre3.shape
    scale, bias, mean, inv = halved_coefs(peers, own3, rec3, prm, size)

    def body(i, carry):
        sums, cross = carry
        at = pl.ds(pl.multiple_of(i * step, step), step)
        pre = pre3[at, :]
        half = pre * scale + (bias + 0.5 * im[at, :].astype(F32))
        turn = jnp.tanh(half)
        grad = cot[at, :].astype(F32) * ((0.5 + 0.5 * turn) * (1.0 + half * (1.0 - turn)))
        e3[at, :] = grad
        return sums + group(grad), cross + group(grad * (pre - mean))

    zero = jnp.zeros((8, chans), F32)
    sums, cross = lax.fori_loop(0, size // step, body, (zero, zero), unroll=2)
    msg[...] = head_rows(rowsum(sums), rowsum(cross) * inv)


def result_kernel(peers, step, pre3, own3, rec3, prm, im, out):
    size = pre3.shape[0]
    scale, bias, _, _ = halved_coefs(peers, own3, rec3, prm, size)

    def body(i, carry):
        at = pl.ds(pl.multiple_of(i * step, step), step)
        half = pre3[at, :] * scale + (bias + 0.5 * im[at, :].astype(F32))
        out[at, :] = (half + half * jnp.tanh(half)).astype(BF16)
        return carry

    lax.fori_loop(0, size // step, body, 0, unroll=2)


def fifth_kernel(
    peers, edge, pre3, e3, own3, rec3, own4, rec4, prm, w, pre2, own2, rec2, dh3, e2, msg
):
    size, half, cols, wide = pre3.shape[0], pre2.shape[0], edge // 2, pre2.shape[1]
    count = float(size * (peers + 1))
    g2, s2 = gain_shift(prm, 1, wide)
    g3, _ = gain_shift(prm, 2, pre3.shape[1])
    mean3, inv3 = moments(own3, rec3, peers, float(size))
    sums3, cross3 = totals(own4, rec4, peers)
    scale3, slant3, bias3 = back_coefs(g3, mean3, inv3, sums3, cross3, count)
    mean, inv = moments(own2, rec2, peers, float(size))
    scale, bias = norm_coefs(g2, s2, mean, inv)
    weight = w[...]
    zero = jnp.zeros_like(weight)
    upper = jnp.concatenate([weight, zero], 0)
    lower = jnp.concatenate([zero, weight], 0)
    sums = jnp.zeros((8, wide), F32)
    cross = jnp.zeros((8, wide), F32)
    for at in range(0, half, cols):
        back = None
        for base, side in ((at, upper), (half + at, lower)):
            rows = slice(base, base + cols)
            dh = (e3[rows, :] * scale3 + pre3[rows, :] * slant3 + bias3).astype(BF16)
            dh3[rows, :] = dh
            part = nt(dh, side)
            back = part if back is None else back + part
        pre = pre2[at : at + cols, :]
        grad = back * slope(pre * scale + bias)
        e2[at : at + cols, :] = grad
        sums = sums + group(grad)
        cross = cross + group(grad * (pre - mean))
    msg[0:WIDE_HEAD, :] = wide_head_rows(both_halves(rowsum(sums)), both_halves(rowsum(cross) * inv))
    msg[WIDE_HEAD : WIDE_HEAD + edge, :] = edges(e2, edge).astype(BF16)
    msg[WIDE_HEAD + edge :, :] = edges(pre2, edge, mean).astype(BF16)


def expand_kernel(act2, dh3, w, out, bwd):
    half = act2.shape[0]
    mids, wide = act2.shape[1] // 2, act2.shape[1]
    out[...] = tn(act2[...], dh3[0:half, :])[0:mids, :] + tn(act2[...], dh3[half:, :])[mids:, :]
    for a, b, both in tap_blocks(w):
        k = 2 - a
        bwd[b * wide : (b + 1) * wide, k * wide : (k + 1) * wide] = both


def sixth_kernel(
    peers, edge, pre2, e2, own5, rec5, own2, rec2, pre1, own1, rec1, prm, w,
    dext, e1, msg, scr,
):
    half, cols, wide = pre2.shape[0], edge // 2, pre2.shape[1]
    size = 2.0 * half
    count = size * (peers + 1)
    g1, s1 = gain_shift(prm, 0, wide)
    g2, _ = gain_shift(prm, 1, wide)
    mean2, inv2 = moments(own2, rec2, peers, size)
    sums2, cross2 = totals(own5, rec5, peers)
    scale2, slant2, bias2 = back_coefs(g2, mean2, inv2, sums2, cross2, count)
    mean, inv = moments(own1, rec1, peers, size)
    scale, bias = norm_coefs(g1, s1, mean, inv)
    clear_gaps(scr, cols)
    acts = []
    for at in range(0, half, cols):
        dh = e2[at : at + cols, :] * scale2 + pre2[at : at + cols, :] * slant2 + bias2
        dext[edge + at : edge + at + cols, :] = dh.astype(BF16)
        if at < edge or at >= half - edge:
            acts.append((at, dh))
    first = jnp.concatenate([act for at, act in acts if at < edge], 0)
    last = jnp.concatenate([act for at, act in acts if at >= half - edge], 0)
    if peers:
        base = WIDE_HEAD * peers
        halo = (
            rec5[base : base + edge, :].astype(F32) * scale2
            + rec5[base + edge :, :].astype(F32) * slant2
            + (bias2 + slant2 * mean2)
        )
    else:
        halo = jnp.zeros((edge, wide), F32)
    fill_edges(dext, first, last, halo, edge)
    sums = jnp.zeros((8, wide), F32)
    cross = jnp.zeros((8, wide), F32)
    for i, at in enumerate(range(0, half, cols)):
        out = nt(taps(dext, edge, at, cols), w[...])
        scr[2 * i, GAP : GAP + cols, :] = out[:, 0:wide]
        scr[2 * i + 1, GAP : GAP + cols, :] = out[:, 2 * wide :]
        back = (
            out[:, wide : 2 * wide]
            + scr[2 * i, GAP + 2 : GAP + 2 + cols, :]
            + scr[2 * i + 1, GAP - 2 : GAP - 2 + cols, :]
        )
        pre = pre1[at : at + cols, :]
        grad = back * slope(pre * scale + bias)
        e1[at : at + cols, :] = grad
        sums = sums + group(grad)
        cross = cross + group(grad * (pre - mean))
    msg[...] = head_rows(both_halves(rowsum(sums)), both_halves(rowsum(cross) * inv))


def fold(block, upper):
    mids = block.shape[0] // 2
    if upper:
        return swap_halves(block[0:mids, :]) + block[mids:, :]
    return block[0:mids, :] + swap_halves(block[mids:, :])


def dilated_kernel(edge, ext, dext, out, scr, dcat):
    cols, wide = edge // 2, ext.shape[1]
    half = dext.shape[0] - 2 * edge
    mids = wide // 2
    clear_gaps(scr, cols)
    for i, at in enumerate(range(0, half, cols)):
        mid = dext[edge + at : edge + at + cols, :]
        scr[i, GAP : GAP + cols, :] = mid.astype(F32)
        dcat[at : at + cols, 0:wide] = scr[i, GAP + 2 : GAP + 2 + cols, :].astype(BF16)
        dcat[at : at + cols, wide : 2 * wide] = mid
        dcat[at : at + cols, 2 * wide :] = scr[i, GAP - 2 : GAP - 2 + cols, :].astype(BF16)
    blocks = []
    for a in range(3):
        prod = tn(ext[a * edge : a * edge + half, :], dcat[...])
        blocks = blocks + [prod[:, b * wide : (b + 1) * wide] for b in range(3)]
    low = lower_half((mids, wide))
    for k in range(4):
        pair = jnp.where(low, fold(blocks[2 * k], False), fold(blocks[2 * k + 1], True))
        out[k * mids : (k + 1) * mids, :] = pair.astype(BF16)
    out[4 * mids : 5 * mids, :] = fold(blocks[8], False).astype(BF16)


def seventh_kernel(
    peers, pre1, e1, own6, rec6, own1, rec1, prm, im, gwd, gwe, own4, own5, dh1, *rest
):
    outs, scr = rest[:-1], rest[-1]
    half, wide = pre1.shape
    mids, chans = wide // 2, im.shape[1]
    size = 2.0 * half
    count = size * (peers + 1)
    g1, _ = gain_shift(prm, 0, wide)
    mean, inv = moments(own1, rec1, peers, size)
    sums, cross = totals(own6, rec6, peers)
    scale, slant, bias = back_coefs(g1, mean, inv, sums, cross, count)
    dh = (e1[...] * scale + pre1[...] * slant + bias).astype(BF16)
    dh1[...] = dh
    prod = tn(dh, im[0:half, :])[0:mids, :] + tn(dh, im[half:, :])[mids:, :]
    base = gwd.shape[0]
    scr[0:base, :] = gwd[...]
    for whole in (prod, gwe[...]):
        for part in range(chans // wide):
            scr[base : base + mids, :] = whole[:, part * wide : (part + 1) * wide].astype(BF16)
            base = base + mids
    rows = [head_row(own, 0, which) for own in (own6, own5) for which in (1, 0)]
    for row in (1, 0):
        rows = rows + [own4[row : row + 1, p * wide : (p + 1) * wide] for p in range(chans // wide)]
    rows.append(jnp.zeros((scr.shape[0] - base - len(rows), wide), F32))
    scr[base:, :] = jnp.concatenate(rows, 0).astype(BF16)
    me = lax.axis_index("space")
    for k, out in enumerate(outs):
        piece = out.shape[0]
        start = lax.rem(me + k, peers + 1) * piece
        out[...] = scr[pl.ds(pl.multiple_of(start, 16), piece), :]


def images_kernel(cols, dh1, w, e3, out):
    half = dh1.shape[0]
    weight = w[...]
    zero = jnp.zeros_like(weight)
    sides = (jnp.concatenate([weight, zero], 0), jnp.concatenate([zero, weight], 0))
    for at in range(0, half, cols):
        dh = dh1[at : at + cols, :]
        for side, base in zip(sides, (at, half + at)):
            out[base : base + cols, :] = (nn(dh, side) + e3[base : base + cols, :]).astype(BF16)


def unpack_kernel(peers, batch, *refs):
    pieces, refs = refs[: peers + 1], refs[peers + 1 :]
    gwr, gwd, gwe, gg1, gs1, gg2, gs2, gg3, gs3, scr = refs
    wide = scr.shape[1]
    mids = wide // 2
    chans = gwe.shape[1]
    parts = chans // wide
    me = lax.axis_index("space")
    for k, ref in enumerate(pieces):
        piece = ref.shape[0]
        start = lax.rem(me + peers + 1 - k, peers + 1) * piece
        scr[pl.ds(pl.multiple_of(start, 16), piece), :] = ref[...].astype(F32) / batch
    for k in range(5):
        block = scr[k * mids : (k + 1) * mids, :]
        gwd[2 * k] = block[:, 0:mids]
        if k < 4:
            gwd[2 * k + 1] = swap_halves(block)[:, 0:mids]
    base = 5 * mids
    for ref in (gwr, gwe):
        for part in range(parts):
            ref[:, part * wide : (part + 1) * wide] = scr[base : base + mids, :]
            base = base + mids
    for ref in (gg1, gs1, gg2, gs2):
        ref[...] = scr[base : base + 1, 0:mids]
        base = base + 1
    for ref in (gg3, gs3):
        for part in range(parts):
            ref[:, part * wide : (part + 1) * wide] = scr[base : base + 1, :]
            base = base + 1


HBM = pl.BlockSpec(memory_space=pltpu.HBM)
VMEM = pl.BlockSpec(memory_space=pltpu.VMEM)


def call(kernel, outs, *args, scratch=(), flops=0, far=(), final=False):
    size = sum(item.size * item.dtype.itemsize for item in args)
    size = size + sum(functools.reduce(lambda x, y: x * y, s, 1) * 4 for s, _ in outs)
    kind_of = jax.ShapeDtypeStruct if final else pltpu.VMEM
    args = [pltpu.with_memory_space_constraint(x, pltpu.HBM) if k in far else x for k, x in enumerate(args)]
    out = pl.pallas_call(
        kernel,
        out_shape=[kind_of(shape, kind) for shape, kind in outs],
        in_specs=[HBM if k in far else VMEM for k in range(len(args))],
        out_specs=[VMEM] * len(outs),
        scratch_shapes=list(scratch),
        cost_estimate=pl.CostEstimate(flops=flops, bytes_accessed=size, transcendentals=0),
        compiler_params=pltpu.CompilerParams(vmem_limit_bytes=16 * 1024 * 1024),
    )(*args)
    return out[0] if len(outs) == 1 else out


def swapped(value, axis, step):
    count = lax.axis_size(axis)
    return lax.ppermute(value, axis, [(i, (i + step) % count) for i in range(count)])


def exchange(msg, peers):
    if peers == 0:
        return msg
    if peers == 1:
        return swapped(msg, "space", 1)
    head = WIDE_HEAD if msg.dtype == BF16 else HEAD
    heads = [swapped(msg[0:head], "space", k + 1) for k in range(peers)]
    if msg.shape[0] > head:
        above = swapped(msg[head:], "space", 1)
        below = swapped(msg[head:], "space", peers)
        low = lax.broadcasted_iota(jnp.int32, above.shape, 1) < above.shape[1] // 2
        heads.append(jnp.where(low, above, below))
    return jnp.concatenate(heads, 0)


def summed_over_dp(part):
    count, sides = lax.axis_size("dp"), lax.axis_size("space")
    if count & (count - 1):
        return lax.psum(part.astype(F32), "dp").astype(BF16)
    bits = [1 << k for k in range(count.bit_length() - 1)]
    for k in range(len(bits)):
        pairs = []
        for i in range(count * sides):
            dp, side = divmod(i, sides)
            bit = bits[(k + side * (len(bits) // 2)) % len(bits)]
            pairs.append((i, (dp ^ bit) * sides + side))
        got = lax.ppermute(part, ("dp", "space"), pairs)
        part = (part.astype(F32) + got.astype(F32)).astype(BF16)
    return part


def shards(
    images, w_reduce, w_dilated, w_expand, gain_one, shift_one, gain_two, shift_two,
    gain_three, shift_three, cotangent,
):
    rows, cols, chans = images.shape[1:]
    mids = w_reduce.shape[1]
    wide = 2 * mids
    pixels = rows * cols
    half, edge = pixels // 2, 2 * cols
    ext_rows = half + 2 * edge
    count = lax.axis_size("space")
    peers = count - 1
    part = functools.partial
    im = images.reshape(pixels, chans)
    cot = cotangent.reshape(pixels, chans)
    row = lambda item: item.reshape(1, -1)
    gaps = lambda n: pltpu.VMEM((n, cols + 2 * GAP, wide), F32)
    chunks = half // cols
    w_rows = w_reduce.T
    gates = 2 * pixels * wide * chans

    pre1, own1, im_held, w_held, wd_held = call(
        part(first_kernel, edge),
        [((half, wide), F32), ((WIDE_HEAD + edge, wide), BF16), ((pixels, chans), BF16)]
        + [(w_rows.shape, BF16), (w_dilated.shape, BF16)],
        im, w_rows, w_dilated, flops=gates, far=(0, 1, 2),
        scratch=[pltpu.SemaphoreType.DMA((2 * chunks + 2,))],
    )
    fwd, we, prm = call(
        weights_kernel,
        [((3 * wide, 3 * wide), BF16), ((mids, chans), BF16), ((8, chans), F32)],
        wd_held, w_expand, row(gain_one), row(shift_one), row(gain_two), row(shift_two),
        row(gain_three), row(shift_three), flops=10**6,
    )
    rec1 = exchange(own1, peers)
    ext, pre2, own2, cot_held = call(
        part(second_kernel, peers, edge),
        [((ext_rows, wide), BF16), ((half, wide), F32), ((HEAD, wide), F32), ((pixels, chans), BF16)],
        pre1, own1, rec1, prm, fwd, cot, far=(5,),
        scratch=[gaps(2 * chunks), pltpu.SemaphoreType.DMA], flops=2 * half * 9 * wide * wide,
    )
    rec2 = exchange(own2, peers)
    act2, pre3, own3 = call(
        part(third_kernel, peers, cols),
        [((half, wide), BF16), ((pixels, chans), F32), ((HEAD, chans), F32)],
        pre2, own2, rec2, prm, we, flops=gates,
    )
    rec3 = exchange(own3, peers)
    e3, own4 = call(
        part(fourth_kernel, peers, 64), [((pixels, chans), F32), ((HEAD, chans), F32)],
        pre3, own3, rec3, prm, im_held, cot_held, flops=30 * pixels * chans,
    )
    rec4 = exchange(own4, peers)
    dh3, e2, own5 = call(
        part(fifth_kernel, peers, edge),
        [((pixels, chans), BF16), ((half, wide), F32), ((WIDE_HEAD + 2 * edge, wide), BF16)],
        pre3, e3, own3, rec3, own4, rec4, prm, we, pre2, own2, rec2, flops=gates,
    )
    rec5 = exchange(own5, peers)
    gwe, bwd = call(
        expand_kernel, [((mids, chans), F32), ((3 * wide, 3 * wide), BF16)],
        act2, dh3, wd_held, flops=gates,
    )
    dext, e1, own6 = call(
        part(sixth_kernel, peers, edge),
        [((ext_rows, wide), BF16), ((half, wide), F32), ((HEAD, wide), F32)],
        pre2, e2, own5, rec5, own2, rec2, pre1, own1, rec1, prm, bwd,
        scratch=[gaps(2 * chunks)], flops=2 * half * 9 * wide * wide,
    )
    rec6 = exchange(own6, peers)
    gwd = call(
        part(dilated_kernel, edge), [((5 * mids, wide), BF16)], ext, dext,
        scratch=[gaps(chunks), pltpu.VMEM((half, 3 * wide), BF16)],
        flops=2 * half * 9 * wide * wide,
    )
    length = 5 * mids + 2 * (chans // wide) * mids + 16
    piece = -(-length // (16 * count)) * 16
    dh1, *pieces = call(
        part(seventh_kernel, peers),
        [((half, wide), BF16)] + [((piece, wide), BF16)] * count,
        pre1, e1, own6, rec6, own1, rec1, prm, im_held, gwd, gwe, own4, own5, flops=gates,
        scratch=[pltpu.VMEM((piece * count, wide), BF16)],
    )
    total = pieces[0].astype(F32)
    for k in range(peers):
        total = total + swapped(pieces[k + 1], "space", k + 1).astype(F32)
    total = summed_over_dp(total.astype(BF16))
    whole = [total] + [swapped(total, "space", k + 1) for k in range(peers)]
    grad_images = call(
        part(images_kernel, cols), [((pixels, chans), BF16)], dh1, w_held, e3,
        flops=gates, final=True,
    )
    result = call(
        part(result_kernel, peers, 64), [((pixels, chans), BF16)],
        pre3, own3, rec3, prm, im_held, flops=10 * pixels * chans, final=True,
    )
    grads = call(
        part(unpack_kernel, peers, float(lax.axis_size("dp"))),
        [((mids, chans), F32), ((9, mids, mids), F32), ((mids, chans), F32)]
        + [((1, mids), F32)] * 4 + [((1, chans), F32)] * 2,
        *whole, scratch=[pltpu.VMEM((piece * count, wide), F32)], final=True,
    )
    gwr, gwd, gwe = grads[:3]
    shape = images.shape
    return (
        result.reshape(shape), grad_images.reshape(shape), gwr.T, gwd.reshape(3, 3, mids, mids), gwe,
    ) + tuple(item.reshape(-1) for item in grads[3:])


def solution(mesh):
    big = P("dp", "space", None, None)
    return jax.shard_map(
        shards,
        mesh=mesh,
        in_specs=(big,) + (P(),) * 9 + (big,),
        out_specs=(big, big) + (P(),) * 9,
        check_vma=False,
    )
```

```python
import functools

import jax
import jax.numpy as jnp
from jax import lax
from jax.experimental import pallas as pl
from jax.experimental.pallas import tpu as pltpu
from jax.sharding import PartitionSpec as P

epsilon = 1e-05
F32 = jnp.float32
BF16 = jnp.bfloat16
HEAD = 8
WIDE_HEAD = 16
GAP = 8


def nn(left, right):
    return jnp.dot(left, right, preferred_element_type=F32)


def nt(left, right):
    return lax.dot_general(left, right, (((1,), (1,)), ((), ())), preferred_element_type=F32)


def tn(left, right):
    return lax.dot_general(left, right, (((0,), (0,)), ((), ())), preferred_element_type=F32)


def swap_halves(value):
    return pltpu.roll(value, value.shape[1] // 2, 1)


def lower_half(shape):
    return lax.broadcasted_iota(jnp.int32, shape, 1) < shape[1] // 2


def both_halves(row):
    return row + swap_halves(row)


def rowsum(value):
    return jnp.sum(value, 0, keepdims=True)


def group(value):
    return jnp.sum(value.reshape(value.shape[0] // 8, 8, value.shape[1]), 0)


def silu(value):
    half = 0.5 * value
    return half + half * jnp.tanh(half)


def slope(value):
    half = 0.5 * value
    turn = jnp.tanh(half)
    return (0.5 + 0.5 * turn) * (1.0 + half * (1.0 - turn))


def head_row(ref, item, which):
    if ref.dtype == BF16:
        terms = ref[WIDE_HEAD * item : WIDE_HEAD * (item + 1), :].astype(F32)
        at = 3 * which
        return terms[at : at + 1, :] + terms[at + 1 : at + 2, :] + terms[at + 2 : at + 3, :]
    at = HEAD * item + which
    return ref[at : at + 1, :]


def moments(own, rec, peers, local):
    means = [head_row(own, 0, 0)] + [head_row(rec, k, 0) for k in range(peers)]
    squares = [head_row(own, 0, 1)] + [head_row(rec, k, 1) for k in range(peers)]
    mean = sum(means) / (peers + 1)
    total = sum(squares) + local * sum((item - mean) * (item - mean) for item in means)
    return mean, lax.rsqrt(total / (local * (peers + 1)) + epsilon)


def totals(own, rec, peers):
    sums = head_row(own, 0, 0) + sum(head_row(rec, k, 0) for k in range(peers))
    cross = head_row(own, 0, 1) + sum(head_row(rec, k, 1) for k in range(peers))
    return sums, cross


def head_rows(first, second):
    rest = jnp.zeros((HEAD - 2, first.shape[1]), F32)
    return jnp.concatenate([first, second, rest], 0)


def three_terms(value):
    high = value.astype(BF16).astype(F32)
    mid = (value - high).astype(BF16).astype(F32)
    return [high, mid, value - high - mid]


def wide_head_rows(first, second):
    rest = jnp.zeros((WIDE_HEAD - 6, first.shape[1]), F32)
    return jnp.concatenate(three_terms(first) + three_terms(second) + [rest], 0).astype(BF16)


def edges(ref, edge, centre=0.0):
    size = ref.shape[0]
    top = ref[0:edge, :]
    return swap_halves(jnp.where(lower_half(top.shape), top, ref[size - edge : size, :]) - centre)


def fill_edges(ext, first, last, halo, edge):
    size = ext.shape[0]
    low = lower_half(halo.shape)
    halo = halo * edge_mask(halo.shape)
    ext[0:edge, :] = jnp.where(low, halo, swap_halves(last)).astype(BF16)
    ext[size - edge : size, :] = jnp.where(low, swap_halves(first), halo).astype(BF16)


def norm_coefs(gain, shift, mean, inv):
    scale = gain * inv
    return scale, shift - mean * scale


def back_coefs(gain, mean, inv, sums, cross, count):
    scale = gain * inv
    slant = -scale * inv * cross / count
    return scale, slant, -scale * sums / count - slant * mean


def centred_squares(ref, mean, step):
    acc = jnp.zeros((8, ref.shape[1]), F32)
    for at in range(0, ref.shape[0], step):
        gap = ref[at : at + step, :] - mean
        acc = acc + group(gap * gap)
    return rowsum(acc)


def first_kernel(edge, im, w, pre, msg, im_held, w_held, im_near, w_near, sems):
    half, cols = pre.shape[0], edge // 2
    fetch_w = pltpu.make_async_copy(w, w_near, sems.at[0])
    fetch_w.start()
    copies = []
    for at in range(0, half, cols):
        for base in (at, half + at):
            rows = pl.ds(base, cols)
            sem = sems.at[1 + len(copies)]
            copies.append(pltpu.make_async_copy(im.at[rows, :], im_near.at[rows, :], sem))
            copies[-1].start()
    fetch_w.wait()
    weight = w_near[...]
    w_held[...] = weight
    zero = jnp.zeros_like(weight)
    upper = jnp.concatenate([weight, zero], 0)
    lower = jnp.concatenate([zero, weight], 0)
    acc = jnp.zeros((8, pre.shape[1]), F32)
    for k, at in enumerate(range(0, half, cols)):
        part = None
        for copy, base, side in ((2 * k, at, upper), (2 * k + 1, half + at, lower)):
            copies[copy].wait()
            block = im_near[base : base + cols, :]
            im_held[base : base + cols, :] = block
            prod = nt(block, side)
            part = prod if part is None else part + prod
        pre[at : at + cols, :] = part
        acc = acc + group(part)
    mean = both_halves(rowsum(acc)) / (2 * half)
    msg[0:WIDE_HEAD, :] = wide_head_rows(mean, both_halves(centred_squares(pre, mean, cols)))
    msg[WIDE_HEAD:, :] = edges(pre, edge, mean).astype(BF16)


def tap_blocks(w):
    mids = w.shape[-1]
    zero = jnp.zeros((mids, mids), BF16)
    for a in range(3):
        for b in range(3):
            block = w[a, b]
            yield a, b, jnp.concatenate(
                [jnp.concatenate([block, zero], 1), jnp.concatenate([zero, block], 1)], 0
            )


def weights_kernel(*refs):
    far, (we_held, fwd, bwd, prm), near, sems = refs[:8], refs[8:12], refs[12:-1], refs[-1]
    copies = [pltpu.make_async_copy(a, b, sems.at[k]) for k, (a, b) in enumerate(zip(far, near))]
    for item in copies:
        item.start()
    for item in copies:
        item.wait()
    wide = 2 * near[0].shape[-1]
    for a, b, both in tap_blocks(near[0]):
        k = 2 - a
        fwd[a * wide : (a + 1) * wide, b * wide : (b + 1) * wide] = both
        bwd[b * wide : (b + 1) * wide, k * wide : (k + 1) * wide] = both
    prm[...] = jnp.zeros(prm.shape, F32)
    we_held[...] = near[7][...]
    for k, ref in enumerate(near[1:5]):
        prm[k : k + 1, 0:wide] = jnp.concatenate([ref[...], ref[...]], 1)
    prm[4:5, :] = near[5][...]
    prm[5:6, :] = near[6][...]


def gain_shift(prm, norm, wide):
    return prm[2 * norm : 2 * norm + 1, 0:wide], prm[2 * norm + 1 : 2 * norm + 2, 0:wide]


def edge_mask(shape):
    me = lax.axis_index("space")
    above = jnp.where(me > 0, 1.0, 0.0)
    below = jnp.where(me < lax.axis_size("space") - 1, 1.0, 0.0)
    return jnp.where(lower_half(shape), above, below)


def taps(ext, edge, at, cols):
    return jnp.concatenate([ext[a * edge + at : a * edge + at + cols, :] for a in range(3)], 1)


def clear_gaps(scr, cols):
    zero = jnp.zeros((scr.shape[0], GAP, scr.shape[2]), F32)
    scr[:, 0:GAP, :] = zero
    scr[:, GAP + cols :, :] = zero


def second_kernel(
    peers, edge, pre1, own1, rec1, prm, w, ext, pre2, msg, scr
):
    half, cols, wide = pre2.shape[0], edge // 2, pre2.shape[1]
    g1, s1 = gain_shift(prm, 0, wide)
    mean, inv = moments(own1, rec1, peers, 2.0 * half)
    scale, bias = norm_coefs(g1, s1, mean, inv)
    clear_gaps(scr, cols)
    last = first = None
    acts = []
    for at in range(0, half, cols):
        act = silu(pre1[at : at + cols, :] * scale + bias)
        ext[edge + at : edge + at + cols, :] = act.astype(BF16)
        if at < edge or at >= half - edge:
            acts.append((at, act))
    first = jnp.concatenate([act for at, act in acts if at < edge], 0)
    last = jnp.concatenate([act for at, act in acts if at >= half - edge], 0)
    if peers:
        above, below = head_row(rec1, 0, 0), head_row(rec1, peers - 1, 0)
        centre = jnp.where(lower_half(above.shape), above, below)
        halo = silu((rec1[WIDE_HEAD * peers :, :].astype(F32) + centre) * scale + bias)
    else:
        halo = jnp.zeros((edge, wide), F32)
    fill_edges(ext, first, last, halo, edge)
    acc = jnp.zeros((8, wide), F32)
    for i, at in enumerate(range(0, half, cols)):
        out = nn(taps(ext, edge, at, cols), w[...])
        scr[2 * i, GAP : GAP + cols, :] = out[:, 0:wide]
        scr[2 * i + 1, GAP : GAP + cols, :] = out[:, 2 * wide :]
        part = (
            out[:, wide : 2 * wide]
            + scr[2 * i, GAP - 2 : GAP - 2 + cols, :]
            + scr[2 * i + 1, GAP + 2 : GAP + 2 + cols, :]
        )
        pre2[at : at + cols, :] = part
        acc = acc + group(part)
    mean = both_halves(rowsum(acc)) / (2 * half)
    msg[...] = head_rows(mean, both_halves(centred_squares(pre2, mean, cols)))


def third_kernel(peers, cols, pre2, own2, rec2, prm, w, act2, pre3, msg):
    half = pre2.shape[0]
    g2, s2 = gain_shift(prm, 1, pre2.shape[1])
    mean, inv = moments(own2, rec2, peers, 2.0 * half)
    scale, bias = norm_coefs(g2, s2, mean, inv)
    weight = w[...]
    zero = jnp.zeros_like(weight)
    upper = jnp.concatenate([weight, zero], 0)
    lower = jnp.concatenate([zero, weight], 0)
    acc = jnp.zeros((8, pre3.shape[1]), F32)
    for at in range(0, half, cols):
        act = silu(pre2[at : at + cols, :] * scale + bias).astype(BF16)
        act2[at : at + cols, :] = act
        part = nn(act, upper)
        pre3[at : at + cols, :] = part
        acc = acc + group(part)
        part = nn(act, lower)
        pre3[half + at : half + at + cols, :] = part
        acc = acc + group(part)
    mean = rowsum(acc) / (2 * half)
    msg[...] = head_rows(mean, centred_squares(pre3, mean, cols))


def halves_kernel(step, im, cot, im_half, cot_half):
    def body(i, carry):
        at = pl.ds(pl.multiple_of(i * step, step), step)
        im_half[at, :] = 0.5 * im[at, :].astype(F32)
        cot_half[at, :] = 0.5 * cot[at, :].astype(F32)
        return carry

    lax.fori_loop(0, im.shape[0] // step, body, 0, unroll=2)


def slopes_kernel(peers, step, pre1, own1, rec1, pre2, own2, rec2, prm, slope1, slope2):
    half, wide = pre1.shape
    for norm, pre, own, rec, out in ((0, pre1, own1, rec1, slope1), (1, pre2, own2, rec2, slope2)):
        mean, inv = moments(own, rec, peers, 2.0 * half)
        scale, bias = norm_coefs(*gain_shift(prm, norm, wide), mean, inv)
        for at in range(0, half, step):
            out[at : at + step, :] = slope(pre[at : at + step, :] * scale + bias)


def halved_coefs(peers, own3, rec3, prm, size):
    mean, inv = moments(own3, rec3, peers, float(size))
    gain, shift = gain_shift(prm, 2, own3.shape[1])
    scale, bias = norm_coefs(gain, shift, mean, inv)
    return 0.5 * scale, 0.5 * bias, gain, shift


def fourth_kernel(peers, step, pre3, own3, rec3, prm, im_half, cot_half, e3, msg):
    size, chans = pre3.shape
    scale, bias, gain, shift = halved_coefs(peers, own3, rec3, prm, size)

    def body(i, carry):
        sums, cross = carry
        at = pl.ds(pl.multiple_of(i * step, step), step)
        out = pre3[at, :] * scale + bias
        half = out + im_half[at, :]
        turn = jnp.tanh(half)
        grad = cot_half[at, :] * ((1.0 + turn) * (1.0 + half * (1.0 - turn)))
        e3[at, :] = grad
        return sums + group(grad), cross + group(grad * out)

    zero = jnp.zeros((8, chans), F32)
    sums, cross = lax.fori_loop(0, size // step, body, (zero, zero), unroll=2)
    sums = rowsum(sums)
    msg[...] = head_rows(sums, (2.0 * rowsum(cross) - shift * sums) / gain)


def result_kernel(peers, step, pre3, own3, rec3, prm, im_half, out):
    size = pre3.shape[0]
    scale, bias, _, _ = halved_coefs(peers, own3, rec3, prm, size)

    def body(i, carry):
        at = pl.ds(pl.multiple_of(i * step, step), step)
        half = pre3[at, :] * scale + bias + im_half[at, :]
        out[at, :] = (half + half * jnp.tanh(half)).astype(BF16)
        return carry

    lax.fori_loop(0, size // step, body, 0, unroll=2)


def fifth_kernel(
    peers, edge, pre3, e3, own3, rec3, own4, rec4, prm, w, pre2, own2, rec2, slope2, dh3, e2, msg
):
    size, half, cols, wide = pre3.shape[0], pre2.shape[0], edge // 2, pre2.shape[1]
    count = float(size * (peers + 1))
    g3, _ = gain_shift(prm, 2, pre3.shape[1])
    mean3, inv3 = moments(own3, rec3, peers, float(size))
    sums3, cross3 = totals(own4, rec4, peers)
    scale3, slant3, bias3 = back_coefs(g3, mean3, inv3, sums3, cross3, count)
    mean, inv = moments(own2, rec2, peers, float(size))
    weight = w[...]
    zero = jnp.zeros_like(weight)
    upper = jnp.concatenate([weight, zero], 0)
    lower = jnp.concatenate([zero, weight], 0)
    sums = jnp.zeros((8, wide), F32)
    cross = jnp.zeros((8, wide), F32)
    for at in range(0, half, cols):
        back = None
        for base, side in ((at, upper), (half + at, lower)):
            rows = slice(base, base + cols)
            dh = (e3[rows, :] * scale3 + pre3[rows, :] * slant3 + bias3).astype(BF16)
            dh3[rows, :] = dh
            part = nt(dh, side)
            back = part if back is None else back + part
        pre = pre2[at : at + cols, :]
        grad = back * slope2[at : at + cols, :]
        e2[at : at + cols, :] = grad
        sums = sums + group(grad)
        cross = cross + group(grad * (pre - mean))
    msg[0:WIDE_HEAD, :] = wide_head_rows(both_halves(rowsum(sums)), both_halves(rowsum(cross) * inv))
    msg[WIDE_HEAD : WIDE_HEAD + edge, :] = edges(e2, edge).astype(BF16)
    msg[WIDE_HEAD + edge :, :] = edges(pre2, edge, mean).astype(BF16)


def expand_kernel(act2, dh3, out):
    half = act2.shape[0]
    mids = act2.shape[1] // 2
    out[...] = tn(act2[...], dh3[0:half, :])[0:mids, :] + tn(act2[...], dh3[half:, :])[mids:, :]


def sixth_kernel(
    peers, edge, pre2, e2, own5, rec5, own2, rec2, pre1, own1, rec1, prm, w, slope1,
    dext, e1, msg, scr,
):
    half, cols, wide = pre2.shape[0], edge // 2, pre2.shape[1]
    size = 2.0 * half
    count = size * (peers + 1)
    g2, _ = gain_shift(prm, 1, wide)
    mean2, inv2 = moments(own2, rec2, peers, size)
    sums2, cross2 = totals(own5, rec5, peers)
    scale2, slant2, bias2 = back_coefs(g2, mean2, inv2, sums2, cross2, count)
    mean, inv = moments(own1, rec1, peers, size)
    clear_gaps(scr, cols)
    acts = []
    for at in range(0, half, cols):
        dh = e2[at : at + cols, :] * scale2 + pre2[at : at + cols, :] * slant2 + bias2
        dext[edge + at : edge + at + cols, :] = dh.astype(BF16)
        if at < edge or at >= half - edge:
            acts.append((at, dh))
    first = jnp.concatenate([act for at, act in acts if at < edge], 0)
    last = jnp.concatenate([act for at, act in acts if at >= half - edge], 0)
    if peers:
        base = WIDE_HEAD * peers
        halo = (
            rec5[base : base + edge, :].astype(F32) * scale2
            + rec5[base + edge :, :].astype(F32) * slant2
            + (bias2 + slant2 * mean2)
        )
    else:
        halo = jnp.zeros((edge, wide), F32)
    fill_edges(dext, first, last, halo, edge)
    sums = jnp.zeros((8, wide), F32)
    cross = jnp.zeros((8, wide), F32)
    for i, at in enumerate(range(0, half, cols)):
        out = nt(taps(dext, edge, at, cols), w[...])
        scr[2 * i, GAP : GAP + cols, :] = out[:, 0:wide]
        scr[2 * i + 1, GAP : GAP + cols, :] = out[:, 2 * wide :]
        back = (
            out[:, wide : 2 * wide]
            + scr[2 * i, GAP + 2 : GAP + 2 + cols, :]
            + scr[2 * i + 1, GAP - 2 : GAP - 2 + cols, :]
        )
        pre = pre1[at : at + cols, :]
        grad = back * slope1[at : at + cols, :]
        e1[at : at + cols, :] = grad
        sums = sums + group(grad)
        cross = cross + group(grad * (pre - mean))
    msg[...] = head_rows(both_halves(rowsum(sums)), both_halves(rowsum(cross) * inv))


def fold(block, upper):
    mids = block.shape[0] // 2
    if upper:
        return swap_halves(block[0:mids, :]) + block[mids:, :]
    return block[0:mids, :] + swap_halves(block[mids:, :])


def dilated_kernel(edge, ext, dext, out, scr, dcat):
    cols, wide = edge // 2, ext.shape[1]
    half = dext.shape[0] - 2 * edge
    mids = wide // 2
    clear_gaps(scr, cols)
    for i, at in enumerate(range(0, half, cols)):
        mid = dext[edge + at : edge + at + cols, :]
        scr[i, GAP : GAP + cols, :] = mid.astype(F32)
        dcat[at : at + cols, 0:wide] = scr[i, GAP + 2 : GAP + 2 + cols, :].astype(BF16)
        dcat[at : at + cols, wide : 2 * wide] = mid
        dcat[at : at + cols, 2 * wide :] = scr[i, GAP - 2 : GAP - 2 + cols, :].astype(BF16)
    blocks = []
    for a in range(3):
        prod = tn(ext[a * edge : a * edge + half, :], dcat[...])
        blocks = blocks + [prod[:, b * wide : (b + 1) * wide] for b in range(3)]
    low = lower_half((mids, wide))
    for k in range(4):
        pair = jnp.where(low, fold(blocks[2 * k], False), fold(blocks[2 * k + 1], True))
        out[k * mids : (k + 1) * mids, :] = pair.astype(BF16)
    out[4 * mids : 5 * mids, :] = fold(blocks[8], False).astype(BF16)


def seventh_kernel(
    peers, pre1, e1, own6, rec6, own1, rec1, prm, im, gwd, gwe, own4, own5, dh1, *rest
):
    outs, scr = rest[:-1], rest[-1]
    half, wide = pre1.shape
    mids, chans = wide // 2, im.shape[1]
    size = 2.0 * half
    count = size * (peers + 1)
    g1, _ = gain_shift(prm, 0, wide)
    mean, inv = moments(own1, rec1, peers, size)
    sums, cross = totals(own6, rec6, peers)
    scale, slant, bias = back_coefs(g1, mean, inv, sums, cross, count)
    dh = (e1[...] * scale + pre1[...] * slant + bias).astype(BF16)
    dh1[...] = dh
    prod = tn(dh, im[0:half, :])[0:mids, :] + tn(dh, im[half:, :])[mids:, :]
    base = gwd.shape[0]
    scr[0:base, :] = gwd[...]
    for whole in (prod, gwe[...]):
        for part in range(chans // wide):
            scr[base : base + mids, :] = whole[:, part * wide : (part + 1) * wide].astype(BF16)
            base = base + mids
    rows = [head_row(own, 0, which) for own in (own6, own5) for which in (1, 0)]
    for row in (1, 0):
        rows = rows + [own4[row : row + 1, p * wide : (p + 1) * wide] for p in range(chans // wide)]
    rows.append(jnp.zeros((scr.shape[0] - base - len(rows), wide), F32))
    scr[base:, :] = jnp.concatenate(rows, 0).astype(BF16)
    me = lax.axis_index("space")
    for k, out in enumerate(outs):
        piece = out.shape[0]
        start = lax.rem(me + k, peers + 1) * piece
        out[...] = scr[pl.ds(pl.multiple_of(start, 16), piece), :]


def images_kernel(cols, dh1, w, e3, out):
    half = dh1.shape[0]
    weight = w[...]
    zero = jnp.zeros_like(weight)
    sides = (jnp.concatenate([weight, zero], 0), jnp.concatenate([zero, weight], 0))
    for at in range(0, half, cols):
        dh = dh1[at : at + cols, :]
        for side, base in zip(sides, (at, half + at)):
            out[base : base + cols, :] = (nn(dh, side) + e3[base : base + cols, :]).astype(BF16)


def unpack_kernel(peers, batch, *refs):
    pieces, refs = refs[: peers + 1], refs[peers + 1 :]
    gwr, gwd, gwe, gg1, gs1, gg2, gs2, gg3, gs3, scr = refs
    wide = scr.shape[1]
    mids = wide // 2
    chans = gwe.shape[1]
    parts = chans // wide
    me = lax.axis_index("space")
    for k, ref in enumerate(pieces):
        piece = ref.shape[0]
        start = lax.rem(me + peers + 1 - k, peers + 1) * piece
        scr[pl.ds(pl.multiple_of(start, 16), piece), :] = ref[...].astype(F32) / batch
    for k in range(5):
        block = scr[k * mids : (k + 1) * mids, :]
        gwd[2 * k] = block[:, 0:mids]
        if k < 4:
            gwd[2 * k + 1] = swap_halves(block)[:, 0:mids]
    base = 5 * mids
    for ref in (gwr, gwe):
        for part in range(parts):
            ref[:, part * wide : (part + 1) * wide] = scr[base : base + mids, :]
            base = base + mids
    for ref in (gg1, gs1, gg2, gs2):
        ref[...] = scr[base : base + 1, 0:mids]
        base = base + 1
    for ref in (gg3, gs3):
        for part in range(parts):
            ref[:, part * wide : (part + 1) * wide] = scr[base : base + 1, :]
            base = base + 1


HBM = pl.BlockSpec(memory_space=pltpu.HBM)
VMEM = pl.BlockSpec(memory_space=pltpu.VMEM)


def call(kernel, outs, *args, scratch=(), flops=0, far=(), final=False):
    size = sum(item.size * item.dtype.itemsize for item in args)
    size = size + sum(functools.reduce(lambda x, y: x * y, s, 1) * 4 for s, _ in outs)
    kind_of = jax.ShapeDtypeStruct if final else pltpu.VMEM
    args = [pltpu.with_memory_space_constraint(x, pltpu.HBM) if k in far else x for k, x in enumerate(args)]
    out = pl.pallas_call(
        kernel,
        out_shape=[kind_of(shape, kind) for shape, kind in outs],
        in_specs=[HBM if k in far else VMEM for k in range(len(args))],
        out_specs=[VMEM] * len(outs),
        scratch_shapes=list(scratch),
        cost_estimate=pl.CostEstimate(flops=flops, bytes_accessed=size, transcendentals=0),
        compiler_params=pltpu.CompilerParams(vmem_limit_bytes=16 * 1024 * 1024),
    )(*args)
    return out[0] if len(outs) == 1 else out


def swapped(value, axis, step):
    count = lax.axis_size(axis)
    return lax.ppermute(value, axis, [(i, (i + step) % count) for i in range(count)])


def exchanged(msg, peers):
    if peers == 0:
        return msg
    if peers == 1:
        return swapped(msg, "space", 1)
    head = WIDE_HEAD if msg.dtype == BF16 else HEAD
    heads = [swapped(msg[0:head], "space", k + 1) for k in range(peers)]
    if msg.shape[0] > head:
        above = swapped(msg[head:], "space", 1)
        below = swapped(msg[head:], "space", peers)
        low = lax.broadcasted_iota(jnp.int32, above.shape, 1) < above.shape[1] // 2
        heads.append(jnp.where(low, above, below))
    return jnp.concatenate(heads, 0)


def summed_over_dp(part):
    count, sides = lax.axis_size("dp"), lax.axis_size("space")
    if count & (count - 1):
        return lax.psum(part.astype(F32), "dp").astype(BF16)
    bits = [1 << k for k in range(count.bit_length() - 1)]
    for k in range(len(bits)):
        pairs = []
        for i in range(count * sides):
            dp, side = divmod(i, sides)
            bit = bits[(k + side * (len(bits) // 2)) % len(bits)]
            pairs.append((i, (dp ^ bit) * sides + side))
        got = lax.ppermute(part, ("dp", "space"), pairs)
        part = (part.astype(F32) + got.astype(F32)).astype(BF16)
    return part


def shards(
    images, w_reduce, w_dilated, w_expand, gain_one, shift_one, gain_two, shift_two,
    gain_three, shift_three, cotangent,
):
    rows, cols, chans = images.shape[1:]
    mids = w_reduce.shape[1]
    wide = 2 * mids
    pixels = rows * cols
    half, edge = pixels // 2, 2 * cols
    ext_rows = half + 2 * edge
    count = lax.axis_size("space")
    peers = count - 1
    part = functools.partial
    im = images.reshape(pixels, chans)
    cot = cotangent.reshape(pixels, chans)
    row = lambda item: item.reshape(1, -1)
    gaps = lambda n: pltpu.VMEM((n, cols + 2 * GAP, wide), F32)
    chunks = half // cols
    w_rows = w_reduce.T
    gates = 2 * pixels * wide * chans

    pre1, own1, im_held, w_held = call(
        part(first_kernel, edge),
        [((half, wide), F32), ((WIDE_HEAD + edge, wide), BF16), ((pixels, chans), BF16)]
        + [(w_rows.shape, BF16)],
        im, w_rows, flops=gates, far=(0, 1),
        scratch=[pltpu.VMEM((pixels, chans), BF16), pltpu.VMEM(w_rows.shape, BF16)]
        + [pltpu.SemaphoreType.DMA((2 * chunks + 1,))],
    )
    own1, cot = lax.optimization_barrier((own1, cot))
    rec1 = exchanged(own1, peers)
    we, fwd, bwd, prm = call(
        weights_kernel,
        [(w_expand.shape, BF16)] + [((3 * wide, 3 * wide), BF16)] * 2 + [((8, chans), F32)],
        w_dilated, row(gain_one), row(shift_one), row(gain_two), row(shift_two),
        row(gain_three), row(shift_three), w_expand, flops=10**6, far=tuple(range(8)),
        scratch=[pltpu.VMEM(w_dilated.shape, BF16)] + [pltpu.VMEM((1, mids), F32)] * 4
        + [pltpu.VMEM((1, chans), F32)] * 2 + [pltpu.VMEM(w_expand.shape, BF16)]
        + [pltpu.SemaphoreType.DMA((8,))],
    )
    ext, pre2, own2 = call(
        part(second_kernel, peers, edge),
        [((ext_rows, wide), BF16), ((half, wide), F32), ((HEAD, wide), F32)],
        pre1, own1, rec1, prm, fwd, scratch=[gaps(2 * chunks)], flops=2 * half * 9 * wide * wide,
    )
    rec2 = exchanged(own2, peers)
    im_half, cot_half = call(
        part(halves_kernel, 64), [((pixels, chans), F32)] * 2, im_held, cot,
        flops=4 * pixels * chans,
    )
    act2, pre3, own3 = call(
        part(third_kernel, peers, cols),
        [((half, wide), BF16), ((pixels, chans), F32), ((HEAD, chans), F32)],
        pre2, own2, rec2, prm, we, flops=gates,
    )
    rec3 = exchanged(own3, peers)
    slope1, slope2 = call(
        part(slopes_kernel, peers, cols), [((half, wide), F32)] * 2,
        pre1, own1, rec1, pre2, own2, rec2, prm, flops=30 * half * wide,
    )
    e3, own4 = call(
        part(fourth_kernel, peers, 64), [((pixels, chans), F32), ((HEAD, chans), F32)],
        pre3, own3, rec3, prm, im_half, cot_half, flops=30 * pixels * chans,
    )
    rec4 = exchanged(own4, peers)
    dh3, e2, own5 = call(
        part(fifth_kernel, peers, edge),
        [((pixels, chans), BF16), ((half, wide), F32), ((WIDE_HEAD + 2 * edge, wide), BF16)],
        pre3, e3, own3, rec3, own4, rec4, prm, we, pre2, own2, rec2, slope2, flops=gates,
    )
    rec5 = exchanged(own5, peers)
    gwe = call(expand_kernel, [((mids, chans), F32)], act2, dh3, flops=gates)
    dext, e1, own6 = call(
        part(sixth_kernel, peers, edge),
        [((ext_rows, wide), BF16), ((half, wide), F32), ((HEAD, wide), F32)],
        pre2, e2, own5, rec5, own2, rec2, pre1, own1, rec1, prm, bwd, slope1,
        scratch=[gaps(2 * chunks)], flops=2 * half * 9 * wide * wide,
    )
    rec6 = exchanged(own6, peers)
    gwd = call(
        part(dilated_kernel, edge), [((5 * mids, wide), BF16)], ext, dext,
        scratch=[gaps(chunks), pltpu.VMEM((half, 3 * wide), BF16)],
        flops=2 * half * 9 * wide * wide,
    )
    length = 5 * mids + 2 * (chans // wide) * mids + 16
    piece = -(-length // (16 * count)) * 16
    dh1, *pieces = call(
        part(seventh_kernel, peers),
        [((half, wide), BF16)] + [((piece, wide), BF16)] * count,
        pre1, e1, own6, rec6, own1, rec1, prm, im_held, gwd, gwe, own4, own5, flops=gates,
        scratch=[pltpu.VMEM((piece * count, wide), BF16)],
    )
    total = pieces[0].astype(F32)
    for k in range(peers):
        total = total + swapped(pieces[k + 1], "space", k + 1).astype(F32)
    total = summed_over_dp(total.astype(BF16))
    whole = [total] + [swapped(total, "space", k + 1) for k in range(peers)]
    grad_images = call(
        part(images_kernel, cols), [((pixels, chans), BF16)], dh1, w_held, e3,
        flops=gates, final=True,
    )
    result = call(
        part(result_kernel, peers, 64), [((pixels, chans), BF16)],
        pre3, own3, rec3, prm, im_half, flops=10 * pixels * chans, final=True,
    )
    grads = call(
        part(unpack_kernel, peers, float(lax.axis_size("dp"))),
        [((mids, chans), F32), ((9, mids, mids), F32), ((mids, chans), F32)]
        + [((1, mids), F32)] * 4 + [((1, chans), F32)] * 2,
        *whole, scratch=[pltpu.VMEM((piece * count, wide), F32)], final=True,
    )
    gwr, gwd, gwe = grads[:3]
    shape = images.shape
    return (
        result.reshape(shape), grad_images.reshape(shape), gwr.T, gwd.reshape(3, 3, mids, mids), gwe,
    ) + tuple(item.reshape(-1) for item in grads[3:])


def solution(mesh):
    big = P("dp", "space", None, None)
    return jax.shard_map(
        shards,
        mesh=mesh,
        in_specs=(big,) + (P(),) * 9 + (big,),
        out_specs=(big, big) + (P(),) * 9,
        check_vma=False,
    )
```

```python
import functools

import jax
import jax.numpy as jnp
from jax import lax
from jax.experimental import pallas as pl
from jax.experimental.pallas import tpu as pltpu
from jax.sharding import PartitionSpec as P

epsilon = 1e-05
F32 = jnp.float32
BF16 = jnp.bfloat16
HEAD = 8
WIDE_HEAD = 16
GAP = 8


def nn(left, right):
    return jnp.dot(left, right, preferred_element_type=F32)


def nt(left, right):
    return lax.dot_general(left, right, (((1,), (1,)), ((), ())), preferred_element_type=F32)


def tn(left, right):
    return lax.dot_general(left, right, (((0,), (0,)), ((), ())), preferred_element_type=F32)


def swap_halves(value):
    return pltpu.roll(value, value.shape[1] // 2, 1)


def lower_half(shape):
    return lax.broadcasted_iota(jnp.int32, shape, 1) < shape[1] // 2


def both_halves(row):
    return row + swap_halves(row)


def rowsum(value):
    return jnp.sum(value, 0, keepdims=True)


def group(value):
    return jnp.sum(value.reshape(value.shape[0] // 8, 8, value.shape[1]), 0)


def silu(value):
    half = 0.5 * value
    return half + half * jnp.tanh(half)


def slope(value):
    half = 0.5 * value
    turn = jnp.tanh(half)
    return (0.5 + 0.5 * turn) * (1.0 + half * (1.0 - turn))


def head_row(ref, item, which):
    if ref.dtype == BF16:
        terms = ref[WIDE_HEAD * item : WIDE_HEAD * (item + 1), :].astype(F32)
        at = 3 * which
        return terms[at : at + 1, :] + terms[at + 1 : at + 2, :] + terms[at + 2 : at + 3, :]
    at = HEAD * item + which
    return ref[at : at + 1, :]


def moments(own, rec, peers, local):
    means = [head_row(own, 0, 0)] + [head_row(rec, k, 0) for k in range(peers)]
    squares = [head_row(own, 0, 1)] + [head_row(rec, k, 1) for k in range(peers)]
    mean = sum(means) / (peers + 1)
    total = sum(squares) + local * sum((item - mean) * (item - mean) for item in means)
    return mean, lax.rsqrt(total / (local * (peers + 1)) + epsilon)


def totals(own, rec, peers):
    sums = head_row(own, 0, 0) + sum(head_row(rec, k, 0) for k in range(peers))
    cross = head_row(own, 0, 1) + sum(head_row(rec, k, 1) for k in range(peers))
    return sums, cross


def head_rows(first, second):
    rest = jnp.zeros((HEAD - 2, first.shape[1]), F32)
    return jnp.concatenate([first, second, rest], 0)


def three_terms(value):
    high = value.astype(BF16).astype(F32)
    mid = (value - high).astype(BF16).astype(F32)
    return [high, mid, value - high - mid]


def wide_head_rows(first, second):
    rest = jnp.zeros((WIDE_HEAD - 6, first.shape[1]), F32)
    return jnp.concatenate(three_terms(first) + three_terms(second) + [rest], 0).astype(BF16)


def edges(ref, edge, centre=0.0):
    size = ref.shape[0]
    top = ref[0:edge, :]
    return swap_halves(jnp.where(lower_half(top.shape), top, ref[size - edge : size, :]) - centre)


def fill_edges(ext, first, last, halo, edge):
    size = ext.shape[0]
    low = lower_half(halo.shape)
    halo = halo * edge_mask(halo.shape)
    ext[0:edge, :] = jnp.where(low, halo, swap_halves(last)).astype(BF16)
    ext[size - edge : size, :] = jnp.where(low, swap_halves(first), halo).astype(BF16)


def norm_coefs(gain, shift, mean, inv):
    scale = gain * inv
    return scale, shift - mean * scale


def back_coefs(gain, mean, inv, sums, cross, count):
    scale = gain * inv
    slant = -scale * inv * cross / count
    return scale, slant, -scale * sums / count - slant * mean


def centred_squares(ref, mean, step):
    acc = jnp.zeros((8, ref.shape[1]), F32)
    for at in range(0, ref.shape[0], step):
        gap = ref[at : at + step, :] - mean
        acc = acc + group(gap * gap)
    return rowsum(acc)


def first_kernel(edge, *refs):
    im, far = refs[0], refs[1:10]
    pre, msg, im_held, w_held, wd_held, we_held, prm = refs[10:17]
    im_near, near, sems = refs[17], refs[18:27], refs[27]
    half, cols, wide = pre.shape[0], edge // 2, pre.shape[1]
    small = [pltpu.make_async_copy(a, b, sems.at[k]) for k, (a, b) in enumerate(zip(far, near))]
    small[0].start()
    copies = []
    for at in range(0, half, cols):
        for base in (at, half + at):
            rows = pl.ds(base, cols)
            sem = sems.at[len(small) + len(copies)]
            copies.append(pltpu.make_async_copy(im.at[rows, :], im_near.at[rows, :], sem))
            copies[-1].start()
    for item in small[1:]:
        item.start()
    small[0].wait()
    weight = near[0][...]
    w_held[...] = weight
    zero = jnp.zeros_like(weight)
    upper = jnp.concatenate([weight, zero], 0)
    lower = jnp.concatenate([zero, weight], 0)
    acc = jnp.zeros((8, wide), F32)
    for k, at in enumerate(range(0, half, cols)):
        part = None
        for copy, base, side in ((2 * k, at, upper), (2 * k + 1, half + at, lower)):
            copies[copy].wait()
            block = im_near[base : base + cols, :]
            im_held[base : base + cols, :] = block
            prod = nt(block, side)
            part = prod if part is None else part + prod
        pre[at : at + cols, :] = part
        acc = acc + group(part)
    mean = both_halves(rowsum(acc)) / (2 * half)
    msg[0:WIDE_HEAD, :] = wide_head_rows(mean, both_halves(centred_squares(pre, mean, cols)))
    msg[WIDE_HEAD:, :] = edges(pre, edge, mean).astype(BF16)
    for item in small[1:]:
        item.wait()
    wd_held[...] = near[1][...]
    we_held[...] = near[2][...]
    prm[...] = jnp.zeros(prm.shape, F32)
    for k, ref in enumerate(near[3:7]):
        prm[k : k + 1, 0:wide] = jnp.concatenate([ref[...], ref[...]], 1)
    prm[4:5, :] = near[7][...]
    prm[5:6, :] = near[8][...]


def tap_blocks(w):
    mids = w.shape[-1]
    zero = jnp.zeros((mids, mids), BF16)
    for a in range(3):
        for b in range(3):
            block = w[a, b]
            yield a, b, jnp.concatenate(
                [jnp.concatenate([block, zero], 1), jnp.concatenate([zero, block], 1)], 0
            )


def fetch_rows(far, near, sem, base):
    return pltpu.make_async_copy(far.at[pl.ds(base, near.shape[0]), :], near, sem)


def weights_kernel(wd, cot, fwd, bwd, cot_held, cot_near, sem):
    fetch = fetch_rows(cot, cot_near, sem, 0)
    fetch.start()
    wide = 2 * wd.shape[-1]
    for a, b, both in tap_blocks(wd):
        k = 2 - a
        fwd[a * wide : (a + 1) * wide, b * wide : (b + 1) * wide] = both
        bwd[b * wide : (b + 1) * wide, k * wide : (k + 1) * wide] = both
    fetch.wait()
    cot_held[...] = cot_near[...]


def gain_shift(prm, norm, wide):
    return prm[2 * norm : 2 * norm + 1, 0:wide], prm[2 * norm + 1 : 2 * norm + 2, 0:wide]


def edge_mask(shape):
    me = lax.axis_index("space")
    above = jnp.where(me > 0, 1.0, 0.0)
    below = jnp.where(me < lax.axis_size("space") - 1, 1.0, 0.0)
    return jnp.where(lower_half(shape), above, below)


def taps(ext, edge, at, cols):
    return jnp.concatenate([ext[a * edge + at : a * edge + at + cols, :] for a in range(3)], 1)


def clear_gaps(scr, cols):
    zero = jnp.zeros((scr.shape[0], GAP, scr.shape[2]), F32)
    scr[:, 0:GAP, :] = zero
    scr[:, GAP + cols :, :] = zero


def second_kernel(
    peers, edge, pre1, own1, rec1, prm, w, cot, ext, pre2, msg, cot_held, scr, cot_near, sem
):
    half, cols, wide = pre2.shape[0], edge // 2, pre2.shape[1]
    fetch = fetch_rows(cot, cot_near, sem, cot.shape[0] - cot_near.shape[0])
    fetch.start()
    g1, s1 = gain_shift(prm, 0, wide)
    mean, inv = moments(own1, rec1, peers, 2.0 * half)
    scale, bias = norm_coefs(g1, s1, mean, inv)
    clear_gaps(scr, cols)
    last = first = None
    acts = []
    for at in range(0, half, cols):
        act = silu(pre1[at : at + cols, :] * scale + bias)
        ext[edge + at : edge + at + cols, :] = act.astype(BF16)
        if at < edge or at >= half - edge:
            acts.append((at, act))
    first = jnp.concatenate([act for at, act in acts if at < edge], 0)
    last = jnp.concatenate([act for at, act in acts if at >= half - edge], 0)
    if peers:
        above, below = head_row(rec1, 0, 0), head_row(rec1, peers - 1, 0)
        centre = jnp.where(lower_half(above.shape), above, below)
        halo = silu((rec1[WIDE_HEAD * peers :, :].astype(F32) + centre) * scale + bias)
    else:
        halo = jnp.zeros((edge, wide), F32)
    fill_edges(ext, first, last, halo, edge)
    acc = jnp.zeros((8, wide), F32)
    for i, at in enumerate(range(0, half, cols)):
        out = nn(taps(ext, edge, at, cols), w[...])
        scr[2 * i, GAP : GAP + cols, :] = out[:, 0:wide]
        scr[2 * i + 1, GAP : GAP + cols, :] = out[:, 2 * wide :]
        part = (
            out[:, wide : 2 * wide]
            + scr[2 * i, GAP - 2 : GAP - 2 + cols, :]
            + scr[2 * i + 1, GAP + 2 : GAP + 2 + cols, :]
        )
        pre2[at : at + cols, :] = part
        acc = acc + group(part)
    mean = both_halves(rowsum(acc)) / (2 * half)
    msg[...] = head_rows(mean, both_halves(centred_squares(pre2, mean, cols)))
    fetch.wait()
    cot_held[...] = cot_near[...]


def third_kernel(peers, cols, pre2, own2, rec2, prm, w, act2, pre3, msg):
    half = pre2.shape[0]
    g2, s2 = gain_shift(prm, 1, pre2.shape[1])
    mean, inv = moments(own2, rec2, peers, 2.0 * half)
    scale, bias = norm_coefs(g2, s2, mean, inv)
    weight = w[...]
    zero = jnp.zeros_like(weight)
    upper = jnp.concatenate([weight, zero], 0)
    lower = jnp.concatenate([zero, weight], 0)
    acc = jnp.zeros((8, pre3.shape[1]), F32)
    for at in range(0, half, cols):
        act = silu(pre2[at : at + cols, :] * scale + bias).astype(BF16)
        act2[at : at + cols, :] = act
        part = nn(act, upper)
        pre3[at : at + cols, :] = part
        acc = acc + group(part)
        part = nn(act, lower)
        pre3[half + at : half + at + cols, :] = part
        acc = acc + group(part)
    mean = rowsum(acc) / (2 * half)
    msg[...] = head_rows(mean, centred_squares(pre3, mean, cols))


def halves_kernel(step, im, cot_first, cot_last, im_half, cot_half):
    split = cot_first.shape[0]

    def body(base, cot, i, carry):
        near = pl.ds(pl.multiple_of(i * step, step), step)
        at = pl.ds(pl.multiple_of(base + i * step, step), step)
        im_half[at, :] = 0.5 * im[at, :].astype(F32)
        cot_half[at, :] = 0.5 * cot[near, :].astype(F32)
        return carry

    for base, cot in ((0, cot_first), (split, cot_last)):
        lax.fori_loop(0, cot.shape[0] // step, functools.partial(body, base, cot), 0)


def slopes_kernel(peers, step, pre1, own1, rec1, pre2, own2, rec2, prm, slope1, slope2):
    half, wide = pre1.shape
    for norm, pre, own, rec, out in ((0, pre1, own1, rec1, slope1), (1, pre2, own2, rec2, slope2)):
        mean, inv = moments(own, rec, peers, 2.0 * half)
        scale, bias = norm_coefs(*gain_shift(prm, norm, wide), mean, inv)
        for at in range(0, half, step):
            out[at : at + step, :] = slope(pre[at : at + step, :] * scale + bias)


def halved_coefs(peers, own3, rec3, prm, size):
    mean, inv = moments(own3, rec3, peers, float(size))
    gain, shift = gain_shift(prm, 2, own3.shape[1])
    scale, bias = norm_coefs(gain, shift, mean, inv)
    return 0.5 * scale, 0.5 * bias, gain, shift


def fourth_kernel(peers, step, pre3, own3, rec3, prm, im_half, cot_half, e3, msg):
    size, chans = pre3.shape
    scale, bias, gain, shift = halved_coefs(peers, own3, rec3, prm, size)

    def body(i, carry):
        sums, cross = carry
        at = pl.ds(pl.multiple_of(i * step, step), step)
        out = pre3[at, :] * scale + bias
        half = out + im_half[at, :]
        turn = jnp.tanh(half)
        grad = cot_half[at, :] * ((1.0 + turn) * (1.0 + half * (1.0 - turn)))
        e3[at, :] = grad
        return sums + group(grad), cross + group(grad * out)

    zero = jnp.zeros((8, chans), F32)
    sums, cross = lax.fori_loop(0, size // step, body, (zero, zero), unroll=2)
    sums = rowsum(sums)
    msg[...] = head_rows(sums, (2.0 * rowsum(cross) - shift * sums) / gain)


def result_kernel(peers, step, pre3, own3, rec3, prm, im_half, out):
    size = pre3.shape[0]
    scale, bias, _, _ = halved_coefs(peers, own3, rec3, prm, size)

    def body(i, carry):
        at = pl.ds(pl.multiple_of(i * step, step), step)
        half = pre3[at, :] * scale + bias + im_half[at, :]
        out[at, :] = (half + half * jnp.tanh(half)).astype(BF16)
        return carry

    lax.fori_loop(0, size // step, body, 0, unroll=2)


def fifth_kernel(
    peers, edge, pre3, e3, own3, rec3, own4, rec4, prm, w, pre2, own2, rec2, slope2, dh3, e2, msg
):
    size, half, cols, wide = pre3.shape[0], pre2.shape[0], edge // 2, pre2.shape[1]
    count = float(size * (peers + 1))
    g3, _ = gain_shift(prm, 2, pre3.shape[1])
    mean3, inv3 = moments(own3, rec3, peers, float(size))
    sums3, cross3 = totals(own4, rec4, peers)
    scale3, slant3, bias3 = back_coefs(g3, mean3, inv3, sums3, cross3, count)
    mean, inv = moments(own2, rec2, peers, float(size))
    weight = w[...]
    zero = jnp.zeros_like(weight)
    upper = jnp.concatenate([weight, zero], 0)
    lower = jnp.concatenate([zero, weight], 0)
    sums = jnp.zeros((8, wide), F32)
    cross = jnp.zeros((8, wide), F32)
    for at in range(0, half, cols):
        back = None
        for base, side in ((at, upper), (half + at, lower)):
            rows = slice(base, base + cols)
            dh = (e3[rows, :] * scale3 + pre3[rows, :] * slant3 + bias3).astype(BF16)
            dh3[rows, :] = dh
            part = nt(dh, side)
            back = part if back is None else back + part
        pre = pre2[at : at + cols, :]
        grad = back * slope2[at : at + cols, :]
        e2[at : at + cols, :] = grad
        sums = sums + group(grad)
        cross = cross + group(grad * (pre - mean))
    msg[0:WIDE_HEAD, :] = wide_head_rows(both_halves(rowsum(sums)), both_halves(rowsum(cross) * inv))
    msg[WIDE_HEAD : WIDE_HEAD + edge, :] = edges(e2, edge).astype(BF16)
    msg[WIDE_HEAD + edge :, :] = edges(pre2, edge, mean).astype(BF16)


def expand_kernel(act2, dh3, out):
    half = act2.shape[0]
    mids = act2.shape[1] // 2
    out[...] = tn(act2[...], dh3[0:half, :])[0:mids, :] + tn(act2[...], dh3[half:, :])[mids:, :]


def sixth_kernel(
    peers, edge, pre2, e2, own5, rec5, own2, rec2, pre1, own1, rec1, prm, w, slope1,
    dext, e1, msg, scr,
):
    half, cols, wide = pre2.shape[0], edge // 2, pre2.shape[1]
    size = 2.0 * half
    count = size * (peers + 1)
    g2, _ = gain_shift(prm, 1, wide)
    mean2, inv2 = moments(own2, rec2, peers, size)
    sums2, cross2 = totals(own5, rec5, peers)
    scale2, slant2, bias2 = back_coefs(g2, mean2, inv2, sums2, cross2, count)
    mean, inv = moments(own1, rec1, peers, size)
    clear_gaps(scr, cols)
    acts = []
    for at in range(0, half, cols):
        dh = e2[at : at + cols, :] * scale2 + pre2[at : at + cols, :] * slant2 + bias2
        dext[edge + at : edge + at + cols, :] = dh.astype(BF16)
        if at < edge or at >= half - edge:
            acts.append((at, dh))
    first = jnp.concatenate([act for at, act in acts if at < edge], 0)
    last = jnp.concatenate([act for at, act in acts if at >= half - edge], 0)
    if peers:
        base = WIDE_HEAD * peers
        halo = (
            rec5[base : base + edge, :].astype(F32) * scale2
            + rec5[base + edge :, :].astype(F32) * slant2
            + (bias2 + slant2 * mean2)
        )
    else:
        halo = jnp.zeros((edge, wide), F32)
    fill_edges(dext, first, last, halo, edge)
    sums = jnp.zeros((8, wide), F32)
    cross = jnp.zeros((8, wide), F32)
    for i, at in enumerate(range(0, half, cols)):
        out = nt(taps(dext, edge, at, cols), w[...])
        scr[2 * i, GAP : GAP + cols, :] = out[:, 0:wide]
        scr[2 * i + 1, GAP : GAP + cols, :] = out[:, 2 * wide :]
        back = (
            out[:, wide : 2 * wide]
            + scr[2 * i, GAP + 2 : GAP + 2 + cols, :]
            + scr[2 * i + 1, GAP - 2 : GAP - 2 + cols, :]
        )
        pre = pre1[at : at + cols, :]
        grad = back * slope1[at : at + cols, :]
        e1[at : at + cols, :] = grad
        sums = sums + group(grad)
        cross = cross + group(grad * (pre - mean))
    msg[...] = head_rows(both_halves(rowsum(sums)), both_halves(rowsum(cross) * inv))


def fold(block, upper):
    mids = block.shape[0] // 2
    if upper:
        return swap_halves(block[0:mids, :]) + block[mids:, :]
    return block[0:mids, :] + swap_halves(block[mids:, :])


def dilated_kernel(edge, ext, dext, out, scr, dcat):
    cols, wide = edge // 2, ext.shape[1]
    half = dext.shape[0] - 2 * edge
    mids = wide // 2
    clear_gaps(scr, cols)
    for i, at in enumerate(range(0, half, cols)):
        mid = dext[edge + at : edge + at + cols, :]
        scr[i, GAP : GAP + cols, :] = mid.astype(F32)
        dcat[at : at + cols, 0:wide] = scr[i, GAP + 2 : GAP + 2 + cols, :].astype(BF16)
        dcat[at : at + cols, wide : 2 * wide] = mid
        dcat[at : at + cols, 2 * wide :] = scr[i, GAP - 2 : GAP - 2 + cols, :].astype(BF16)
    blocks = []
    for a in range(3):
        prod = tn(ext[a * edge : a * edge + half, :], dcat[...])
        blocks = blocks + [prod[:, b * wide : (b + 1) * wide] for b in range(3)]
    low = lower_half((mids, wide))
    for k in range(4):
        pair = jnp.where(low, fold(blocks[2 * k], False), fold(blocks[2 * k + 1], True))
        out[k * mids : (k + 1) * mids, :] = pair.astype(BF16)
    out[4 * mids : 5 * mids, :] = fold(blocks[8], False).astype(BF16)


def seventh_kernel(
    peers, pre1, e1, own6, rec6, own1, rec1, prm, im, gwd, gwe, own4, own5, dh1, *rest
):
    outs, scr = rest[:-1], rest[-1]
    half, wide = pre1.shape
    mids, chans = wide // 2, im.shape[1]
    size = 2.0 * half
    count = size * (peers + 1)
    g1, _ = gain_shift(prm, 0, wide)
    mean, inv = moments(own1, rec1, peers, size)
    sums, cross = totals(own6, rec6, peers)
    scale, slant, bias = back_coefs(g1, mean, inv, sums, cross, count)
    dh = (e1[...] * scale + pre1[...] * slant + bias).astype(BF16)
    dh1[...] = dh
    prod = tn(dh, im[0:half, :])[0:mids, :] + tn(dh, im[half:, :])[mids:, :]
    base = gwd.shape[0]
    scr[0:base, :] = gwd[...]
    for whole in (prod, gwe[...]):
        for part in range(chans // wide):
            scr[base : base + mids, :] = whole[:, part * wide : (part + 1) * wide].astype(BF16)
            base = base + mids
    rows = [head_row(own, 0, which) for own in (own6, own5) for which in (1, 0)]
    for row in (1, 0):
        rows = rows + [own4[row : row + 1, p * wide : (p + 1) * wide] for p in range(chans // wide)]
    rows.append(jnp.zeros((scr.shape[0] - base - len(rows), wide), F32))
    scr[base:, :] = jnp.concatenate(rows, 0).astype(BF16)
    me = lax.axis_index("space")
    for k, out in enumerate(outs):
        piece = out.shape[0]
        start = lax.rem(me + k, peers + 1) * piece
        out[...] = scr[pl.ds(pl.multiple_of(start, 16), piece), :]


def images_kernel(cols, dh1, w, e3, out):
    half = dh1.shape[0]
    weight = w[...]
    zero = jnp.zeros_like(weight)
    sides = (jnp.concatenate([weight, zero], 0), jnp.concatenate([zero, weight], 0))
    for at in range(0, half, cols):
        dh = dh1[at : at + cols, :]
        for side, base in zip(sides, (at, half + at)):
            out[base : base + cols, :] = (nn(dh, side) + e3[base : base + cols, :]).astype(BF16)


def unpack_kernel(peers, batch, *refs):
    pieces, refs = refs[: peers + 1], refs[peers + 1 :]
    gwr, gwd, gwe, gg1, gs1, gg2, gs2, gg3, gs3, scr = refs
    wide = scr.shape[1]
    mids = wide // 2
    chans = gwe.shape[1]
    parts = chans // wide
    me = lax.axis_index("space")
    for k, ref in enumerate(pieces):
        piece = ref.shape[0]
        start = lax.rem(me + peers + 1 - k, peers + 1) * piece
        scr[pl.ds(pl.multiple_of(start, 16), piece), :] = ref[...].astype(F32) / batch
    for k in range(5):
        block = scr[k * mids : (k + 1) * mids, :]
        gwd[2 * k] = block[:, 0:mids]
        if k < 4:
            gwd[2 * k + 1] = swap_halves(block)[:, 0:mids]
    base = 5 * mids
    for ref in (gwr, gwe):
        for part in range(parts):
            ref[:, part * wide : (part + 1) * wide] = scr[base : base + mids, :]
            base = base + mids
    for ref in (gg1, gs1, gg2, gs2):
        ref[...] = scr[base : base + 1, 0:mids]
        base = base + 1
    for ref in (gg3, gs3):
        for part in range(parts):
            ref[:, part * wide : (part + 1) * wide] = scr[base : base + 1, :]
            base = base + 1


HBM = pl.BlockSpec(memory_space=pltpu.HBM)
VMEM = pl.BlockSpec(memory_space=pltpu.VMEM)


def call(kernel, outs, *args, scratch=(), flops=0, far=(), final=False):
    size = sum(item.size * item.dtype.itemsize for item in args)
    size = size + sum(functools.reduce(lambda x, y: x * y, s, 1) * 4 for s, _ in outs)
    kind_of = jax.ShapeDtypeStruct if final else pltpu.VMEM
    args = [pltpu.with_memory_space_constraint(x, pltpu.HBM) if k in far else x for k, x in enumerate(args)]
    out = pl.pallas_call(
        kernel,
        out_shape=[kind_of(shape, kind) for shape, kind in outs],
        in_specs=[HBM if k in far else VMEM for k in range(len(args))],
        out_specs=[VMEM] * len(outs),
        scratch_shapes=list(scratch),
        cost_estimate=pl.CostEstimate(flops=flops, bytes_accessed=size, transcendentals=0),
        compiler_params=pltpu.CompilerParams(vmem_limit_bytes=16 * 1024 * 1024),
    )(*args)
    return out[0] if len(outs) == 1 else out


def swapped(value, axis, step):
    count = lax.axis_size(axis)
    return lax.ppermute(value, axis, [(i, (i + step) % count) for i in range(count)])


def exchanged(msg, peers):
    if peers == 0:
        return msg
    if peers == 1:
        return swapped(msg, "space", 1)
    head = WIDE_HEAD if msg.dtype == BF16 else HEAD
    heads = [swapped(msg[0:head], "space", k + 1) for k in range(peers)]
    if msg.shape[0] > head:
        above = swapped(msg[head:], "space", 1)
        below = swapped(msg[head:], "space", peers)
        low = lax.broadcasted_iota(jnp.int32, above.shape, 1) < above.shape[1] // 2
        heads.append(jnp.where(low, above, below))
    return jnp.concatenate(heads, 0)


def flipped_dp(part, masks):
    count, sides = lax.axis_size("dp"), lax.axis_size("space")
    pairs = []
    for i in range(count * sides):
        dp, side = divmod(i, sides)
        pairs.append((i, (dp ^ masks[side % len(masks)]) * sides + side))
    return lax.ppermute(part, ("dp", "space"), pairs).astype(F32)


def summed_over_dp(part):
    count = lax.axis_size("dp")
    if count & (count - 1):
        return lax.psum(part.astype(F32), "dp").astype(BF16)
    bits = [1 << k for k in range(count.bit_length() - 1)]
    twos = [bits[k : k + 2] for k in range(0, len(bits) - 1, 2)]
    for k in range(len(twos)):
        turn = [twos[(k + side * (len(twos) // 2)) % len(twos)] for side in range(2)]
        low = flipped_dp(part, [pair[0] for pair in turn])
        high = flipped_dp(part, [pair[1] for pair in turn])
        both = flipped_dp(part, [pair[0] + pair[1] for pair in turn])
        part = ((part.astype(F32) + low) + (high + both)).astype(BF16)
    if len(bits) % 2:
        part = (part.astype(F32) + flipped_dp(part, bits[-1:])).astype(BF16)
    return part


def shards(
    images, w_reduce, w_dilated, w_expand, gain_one, shift_one, gain_two, shift_two,
    gain_three, shift_three, cotangent,
):
    rows, cols, chans = images.shape[1:]
    mids = w_reduce.shape[1]
    wide = 2 * mids
    pixels = rows * cols
    half, edge = pixels // 2, 2 * cols
    ext_rows = half + 2 * edge
    count = lax.axis_size("space")
    peers = count - 1
    part = functools.partial
    im = images.reshape(pixels, chans)
    cot = cotangent.reshape(pixels, chans)
    row = lambda item: item.reshape(1, -1)
    gaps = lambda n: pltpu.VMEM((n, cols + 2 * GAP, wide), F32)
    chunks = half // cols
    w_rows = w_reduce.T
    gates = 2 * pixels * wide * chans

    small = (w_rows, w_dilated, w_expand) + tuple(
        row(item)
        for item in (gain_one, shift_one, gain_two, shift_two, gain_three, shift_three)
    )
    pre1, own1, im_held, w_held, wd_held, we, prm = call(
        part(first_kernel, edge),
        [((half, wide), F32), ((WIDE_HEAD + edge, wide), BF16), ((pixels, chans), BF16)]
        + [(item.shape, BF16) for item in small[:3]] + [((8, chans), F32)],
        im, *small, flops=gates, far=tuple(range(10)),
        scratch=[pltpu.VMEM((pixels, chans), BF16)]
        + [pltpu.VMEM(item.shape, item.dtype) for item in small]
        + [pltpu.SemaphoreType.DMA((2 * chunks + len(small),))],
    )
    rec1 = exchanged(own1, peers)
    split = edge
    held = lambda n: pltpu.VMEM((n, chans), BF16)
    fwd, bwd, cot_first = call(
        weights_kernel,
        [((3 * wide, 3 * wide), BF16)] * 2 + [((split, chans), BF16)], wd_held, cot,
        flops=10**6, far=(1,), scratch=[held(split), pltpu.SemaphoreType.DMA],
    )
    ext, pre2, own2, cot_last = call(
        part(second_kernel, peers, edge),
        [((ext_rows, wide), BF16), ((half, wide), F32), ((HEAD, wide), F32)]
        + [((pixels - split, chans), BF16)],
        pre1, own1, rec1, prm, fwd, cot, far=(5,),
        scratch=[gaps(2 * chunks), held(pixels - split), pltpu.SemaphoreType.DMA],
        flops=2 * half * 9 * wide * wide,
    )
    rec2 = exchanged(own2, peers)
    im_half, cot_half = call(
        part(halves_kernel, 64), [((pixels, chans), F32)] * 2, im_held, cot_first, cot_last,
        flops=4 * pixels * chans,
    )
    act2, pre3, own3 = call(
        part(third_kernel, peers, cols),
        [((half, wide), BF16), ((pixels, chans), F32), ((HEAD, chans), F32)],
        pre2, own2, rec2, prm, we, flops=gates,
    )
    rec3 = exchanged(own3, peers)
    slope1, slope2 = call(
        part(slopes_kernel, peers, cols), [((half, wide), F32)] * 2,
        pre1, own1, rec1, pre2, own2, rec2, prm, flops=30 * half * wide,
    )
    e3, own4 = call(
        part(fourth_kernel, peers, 64), [((pixels, chans), F32), ((HEAD, chans), F32)],
        pre3, own3, rec3, prm, im_half, cot_half, flops=30 * pixels * chans,
    )
    rec4 = exchanged(own4, peers)
    dh3, e2, own5 = call(
        part(fifth_kernel, peers, edge),
        [((pixels, chans), BF16), ((half, wide), F32), ((WIDE_HEAD + 2 * edge, wide), BF16)],
        pre3, e3, own3, rec3, own4, rec4, prm, we, pre2, own2, rec2, slope2, flops=gates,
    )
    rec5 = exchanged(own5, peers)
    gwe = call(expand_kernel, [((mids, chans), F32)], act2, dh3, flops=gates)
    dext, e1, own6 = call(
        part(sixth_kernel, peers, edge),
        [((ext_rows, wide), BF16), ((half, wide), F32), ((HEAD, wide), F32)],
        pre2, e2, own5, rec5, own2, rec2, pre1, own1, rec1, prm, bwd, slope1,
        scratch=[gaps(2 * chunks)], flops=2 * half * 9 * wide * wide,
    )
    rec6 = exchanged(own6, peers)
    gwd = call(
        part(dilated_kernel, edge), [((5 * mids, wide), BF16)], ext, dext,
        scratch=[gaps(chunks), pltpu.VMEM((half, 3 * wide), BF16)],
        flops=2 * half * 9 * wide * wide,
    )
    length = 5 * mids + 2 * (chans // wide) * mids + 16
    piece = -(-length // (16 * count)) * 16
    dh1, *pieces = call(
        part(seventh_kernel, peers),
        [((half, wide), BF16)] + [((piece, wide), BF16)] * count,
        pre1, e1, own6, rec6, own1, rec1, prm, im_held, gwd, gwe, own4, own5, flops=gates,
        scratch=[pltpu.VMEM((piece * count, wide), BF16)],
    )
    total = pieces[0].astype(F32)
    for k in range(peers):
        total = total + swapped(pieces[k + 1], "space", k + 1).astype(F32)
    total = summed_over_dp(total.astype(BF16))
    whole = [total] + [swapped(total, "space", k + 1) for k in range(peers)]
    grad_images = call(
        part(images_kernel, cols), [((pixels, chans), BF16)], dh1, w_held, e3,
        flops=gates, final=True,
    )
    result = call(
        part(result_kernel, peers, 64), [((pixels, chans), BF16)],
        pre3, own3, rec3, prm, im_half, flops=10 * pixels * chans, final=True,
    )
    grads = call(
        part(unpack_kernel, peers, float(lax.axis_size("dp"))),
        [((mids, chans), F32), ((9, mids, mids), F32), ((mids, chans), F32)]
        + [((1, mids), F32)] * 4 + [((1, chans), F32)] * 2,
        *whole, scratch=[pltpu.VMEM((piece * count, wide), F32)], final=True,
    )
    gwr, gwd, gwe = grads[:3]
    shape = images.shape
    return (
        result.reshape(shape), grad_images.reshape(shape), gwr.T, gwd.reshape(3, 3, mids, mids), gwe,
    ) + tuple(item.reshape(-1) for item in grads[3:])


def solution(mesh):
    big = P("dp", "space", None, None)
    return jax.shard_map(
        shards,
        mesh=mesh,
        in_specs=(big,) + (P(),) * 9 + (big,),
        out_specs=(big, big) + (P(),) * 9,
        check_vma=False,
    )
```

```python
import functools

import jax
import jax.numpy as jnp
from jax import lax
from jax.experimental import pallas as pl
from jax.experimental.pallas import tpu as pltpu
from jax.sharding import PartitionSpec as P

epsilon = 1e-05
F32 = jnp.float32
BF16 = jnp.bfloat16
HEAD = 8
WIDE_HEAD = 16
GAP = 8


def nn(left, right):
    return jnp.dot(left, right, preferred_element_type=F32)


def nt(left, right):
    return lax.dot_general(left, right, (((1,), (1,)), ((), ())), preferred_element_type=F32)


def tn(left, right):
    return lax.dot_general(left, right, (((0,), (0,)), ((), ())), preferred_element_type=F32)


def swap_halves(value):
    return pltpu.roll(value, value.shape[1] // 2, 1)


def lower_half(shape):
    return lax.broadcasted_iota(jnp.int32, shape, 1) < shape[1] // 2


def both_halves(row):
    return row + swap_halves(row)


def rowsum(value):
    return jnp.sum(value, 0, keepdims=True)


def group(value):
    return jnp.sum(value.reshape(value.shape[0] // 8, 8, value.shape[1]), 0)


def silu(value):
    half = 0.5 * value
    return half + half * jnp.tanh(half)


def slope(value):
    half = 0.5 * value
    turn = jnp.tanh(half)
    return (0.5 + 0.5 * turn) * (1.0 + half * (1.0 - turn))


def head_row(ref, item, which):
    if ref.dtype == BF16:
        terms = ref[WIDE_HEAD * item : WIDE_HEAD * (item + 1), :].astype(F32)
        at = 3 * which
        return terms[at : at + 1, :] + terms[at + 1 : at + 2, :] + terms[at + 2 : at + 3, :]
    at = HEAD * item + which
    return ref[at : at + 1, :]


def moments(own, rec, peers, local):
    means = [head_row(own, 0, 0)] + [head_row(rec, k, 0) for k in range(peers)]
    squares = [head_row(own, 0, 1)] + [head_row(rec, k, 1) for k in range(peers)]
    mean = sum(means) / (peers + 1)
    total = sum(squares) + local * sum((item - mean) * (item - mean) for item in means)
    return mean, lax.rsqrt(total / (local * (peers + 1)) + epsilon)


def totals(own, rec, peers):
    sums = head_row(own, 0, 0) + sum(head_row(rec, k, 0) for k in range(peers))
    cross = head_row(own, 0, 1) + sum(head_row(rec, k, 1) for k in range(peers))
    return sums, cross


def head_rows(first, second):
    rest = jnp.zeros((HEAD - 2, first.shape[1]), F32)
    return jnp.concatenate([first, second, rest], 0)


def three_terms(value):
    high = value.astype(BF16).astype(F32)
    mid = (value - high).astype(BF16).astype(F32)
    return [high, mid, value - high - mid]


def wide_head_rows(first, second):
    rest = jnp.zeros((WIDE_HEAD - 6, first.shape[1]), F32)
    return jnp.concatenate(three_terms(first) + three_terms(second) + [rest], 0).astype(BF16)


def edges(ref, edge, centre=0.0):
    size = ref.shape[0]
    top = ref[0:edge, :]
    return swap_halves(jnp.where(lower_half(top.shape), top, ref[size - edge : size, :]) - centre)


def fill_edges(ext, first, last, halo, edge):
    size = ext.shape[0]
    low = lower_half(halo.shape)
    halo = halo * edge_mask(halo.shape)
    ext[0:edge, :] = jnp.where(low, halo, swap_halves(last)).astype(BF16)
    ext[size - edge : size, :] = jnp.where(low, swap_halves(first), halo).astype(BF16)


def norm_coefs(gain, shift, mean, inv):
    scale = gain * inv
    return scale, shift - mean * scale


def back_coefs(gain, mean, inv, sums, cross, count):
    scale = gain * inv
    slant = -scale * inv * cross / count
    return scale, slant, -scale * sums / count - slant * mean


def centred_squares(ref, mean, step):
    acc = jnp.zeros((8, ref.shape[1]), F32)
    for at in range(0, ref.shape[0], step):
        gap = ref[at : at + step, :] - mean
        acc = acc + group(gap * gap)
    return rowsum(acc)


def first_kernel(edge, im, w, pre, msg, im_held, w_held, im_near, w_near, sems):
    half, cols, wide = pre.shape[0], edge // 2, pre.shape[1]
    fetch = pltpu.make_async_copy(w, w_near, sems.at[0])
    fetch.start()
    cut = half // cols // 2 * cols
    copies = []
    for k, (base, size) in enumerate(((0, cut), (cut, half - cut))):
        rows = pl.ds(base, size)
        copies.append(
            pltpu.make_async_copy(im.at[:, rows, :], im_near.at[:, rows, :], sems.at[k + 1])
        )
        copies[-1].start()
    fetch.wait()
    weight = w_near[...]
    w_held[...] = weight
    zero = jnp.zeros_like(weight)
    sides = (jnp.concatenate([weight, zero], 0), jnp.concatenate([zero, weight], 0))
    acc = jnp.zeros((8, wide), F32)
    for at in range(0, half, cols):
        if at in (0, cut):
            copies[min(at, 1)].wait()
        part = None
        for k, side in enumerate(sides):
            block = im_near[k, at : at + cols, :]
            im_held[k * half + at : k * half + at + cols, :] = block
            prod = nt(block, side)
            part = prod if part is None else part + prod
        pre[at : at + cols, :] = part
        acc = acc + group(part)
    mean = both_halves(rowsum(acc)) / (2 * half)
    msg[0:WIDE_HEAD, :] = wide_head_rows(mean, both_halves(centred_squares(pre, mean, cols)))
    msg[WIDE_HEAD:, :] = edges(pre, edge, mean).astype(BF16)


def tap_blocks(w):
    mids = w.shape[-1]
    zero = jnp.zeros((mids, mids), BF16)
    for a in range(3):
        for b in range(3):
            block = w[a, b]
            yield a, b, jnp.concatenate(
                [jnp.concatenate([block, zero], 1), jnp.concatenate([zero, block], 1)], 0
            )


def weights_kernel(wd, we, g1, s1, g2, s2, g3, s3, fwd, bwd, we_held, prm, wd_near, sem):
    fetch = pltpu.make_async_copy(wd, wd_near, sem)
    fetch.start()
    wide = 2 * wd.shape[-1]
    we_held[...] = we[...]
    prm[...] = jnp.zeros(prm.shape, F32)
    for k, ref in enumerate((g1, s1, g2, s2)):
        prm[k : k + 1, 0:wide] = jnp.concatenate([ref[...], ref[...]], 1)
    prm[4:5, :] = g3[...]
    prm[5:6, :] = s3[...]
    fetch.wait()
    for a, b, both in tap_blocks(wd_near):
        k = 2 - a
        fwd[a * wide : (a + 1) * wide, b * wide : (b + 1) * wide] = both
        bwd[b * wide : (b + 1) * wide, k * wide : (k + 1) * wide] = both


def gain_shift(prm, norm, wide):
    return prm[2 * norm : 2 * norm + 1, 0:wide], prm[2 * norm + 1 : 2 * norm + 2, 0:wide]


def edge_mask(shape):
    me = lax.axis_index("space")
    above = jnp.where(me > 0, 1.0, 0.0)
    below = jnp.where(me < lax.axis_size("space") - 1, 1.0, 0.0)
    return jnp.where(lower_half(shape), above, below)


def taps(ext, edge, at, cols):
    return jnp.concatenate([ext[a * edge + at : a * edge + at + cols, :] for a in range(3)], 1)


def clear_gaps(scr, cols):
    zero = jnp.zeros((scr.shape[0], GAP, scr.shape[2]), F32)
    scr[:, 0:GAP, :] = zero
    scr[:, GAP + cols :, :] = zero


def second_kernel(
    peers, edge, pre1, own1, rec1, prm, w, ext, pre2, msg, scr
):
    half, cols, wide = pre2.shape[0], edge // 2, pre2.shape[1]
    g1, s1 = gain_shift(prm, 0, wide)
    mean, inv = moments(own1, rec1, peers, 2.0 * half)
    scale, bias = norm_coefs(g1, s1, mean, inv)
    clear_gaps(scr, cols)
    last = first = None
    acts = []
    for at in range(0, half, cols):
        act = silu(pre1[at : at + cols, :] * scale + bias)
        ext[edge + at : edge + at + cols, :] = act.astype(BF16)
        if at < edge or at >= half - edge:
            acts.append((at, act))
    first = jnp.concatenate([act for at, act in acts if at < edge], 0)
    last = jnp.concatenate([act for at, act in acts if at >= half - edge], 0)
    if peers:
        above, below = head_row(rec1, 0, 0), head_row(rec1, peers - 1, 0)
        centre = jnp.where(lower_half(above.shape), above, below)
        halo = silu((rec1[WIDE_HEAD * peers :, :].astype(F32) + centre) * scale + bias)
    else:
        halo = jnp.zeros((edge, wide), F32)
    fill_edges(ext, first, last, halo, edge)
    acc = jnp.zeros((8, wide), F32)
    for i, at in enumerate(range(0, half, cols)):
        out = nn(taps(ext, edge, at, cols), w[...])
        scr[2 * i, GAP : GAP + cols, :] = out[:, 0:wide]
        scr[2 * i + 1, GAP : GAP + cols, :] = out[:, 2 * wide :]
        part = (
            out[:, wide : 2 * wide]
            + scr[2 * i, GAP - 2 : GAP - 2 + cols, :]
            + scr[2 * i + 1, GAP + 2 : GAP + 2 + cols, :]
        )
        pre2[at : at + cols, :] = part
        acc = acc + group(part)
    mean = both_halves(rowsum(acc)) / (2 * half)
    msg[...] = head_rows(mean, both_halves(centred_squares(pre2, mean, cols)))


def third_kernel(peers, cols, pre2, own2, rec2, prm, w, act2, pre3, msg):
    half = pre2.shape[0]
    g2, s2 = gain_shift(prm, 1, pre2.shape[1])
    mean, inv = moments(own2, rec2, peers, 2.0 * half)
    scale, bias = norm_coefs(g2, s2, mean, inv)
    weight = w[...]
    zero = jnp.zeros_like(weight)
    upper = jnp.concatenate([weight, zero], 0)
    lower = jnp.concatenate([zero, weight], 0)
    acc = jnp.zeros((8, pre3.shape[1]), F32)
    for at in range(0, half, cols):
        act = silu(pre2[at : at + cols, :] * scale + bias).astype(BF16)
        act2[at : at + cols, :] = act
        part = nn(act, upper)
        pre3[at : at + cols, :] = part
        acc = acc + group(part)
        part = nn(act, lower)
        pre3[half + at : half + at + cols, :] = part
        acc = acc + group(part)
    mean = rowsum(acc) / (2 * half)
    msg[...] = head_rows(mean, centred_squares(pre3, mean, cols))


def halves_kernel(step, im, cot, im_half, cot_half):
    def body(i, carry):
        at = pl.ds(pl.multiple_of(i * step, step), step)
        im_half[at, :] = 0.5 * im[at, :].astype(F32)
        cot_half[at, :] = 0.5 * cot[at, :].astype(F32)
        return carry

    lax.fori_loop(0, im.shape[0] // step, body, 0, unroll=2)


def slopes_kernel(peers, step, pre1, own1, rec1, pre2, own2, rec2, prm, slope1, slope2):
    half, wide = pre1.shape
    for norm, pre, own, rec, out in ((0, pre1, own1, rec1, slope1), (1, pre2, own2, rec2, slope2)):
        mean, inv = moments(own, rec, peers, 2.0 * half)
        scale, bias = norm_coefs(*gain_shift(prm, norm, wide), mean, inv)
        for at in range(0, half, step):
            out[at : at + step, :] = slope(pre[at : at + step, :] * scale + bias)


def halved_coefs(peers, own3, rec3, prm, size):
    mean, inv = moments(own3, rec3, peers, float(size))
    gain, shift = gain_shift(prm, 2, own3.shape[1])
    scale, bias = norm_coefs(gain, shift, mean, inv)
    return 0.5 * scale, 0.5 * bias, gain, shift


def fourth_kernel(peers, step, pre3, own3, rec3, prm, im_half, cot_half, e3, msg):
    size, chans = pre3.shape
    scale, bias, gain, shift = halved_coefs(peers, own3, rec3, prm, size)

    def body(i, carry):
        sums, cross = carry
        at = pl.ds(pl.multiple_of(i * step, step), step)
        out = pre3[at, :] * scale + bias
        half = out + im_half[at, :]
        turn = jnp.tanh(half)
        grad = cot_half[at, :] * ((1.0 + turn) * (1.0 + half * (1.0 - turn)))
        e3[at, :] = grad
        return sums + group(grad), cross + group(grad * out)

    zero = jnp.zeros((8, chans), F32)
    sums, cross = lax.fori_loop(0, size // step, body, (zero, zero), unroll=2)
    sums = rowsum(sums)
    msg[...] = head_rows(sums, (2.0 * rowsum(cross) - shift * sums) / gain)


def result_kernel(peers, step, pre3, own3, rec3, prm, im_half, out):
    size = pre3.shape[0]
    scale, bias, _, _ = halved_coefs(peers, own3, rec3, prm, size)

    def body(i, carry):
        at = pl.ds(pl.multiple_of(i * step, step), step)
        half = pre3[at, :] * scale + bias + im_half[at, :]
        out[at, :] = (half + half * jnp.tanh(half)).astype(BF16)
        return carry

    lax.fori_loop(0, size // step, body, 0, unroll=2)


def fifth_kernel(
    peers, edge, pre3, e3, own3, rec3, own4, rec4, prm, w, pre2, own2, rec2, slope2, dh3, e2, msg
):
    size, half, cols, wide = pre3.shape[0], pre2.shape[0], edge // 2, pre2.shape[1]
    count = float(size * (peers + 1))
    g3, _ = gain_shift(prm, 2, pre3.shape[1])
    mean3, inv3 = moments(own3, rec3, peers, float(size))
    sums3, cross3 = totals(own4, rec4, peers)
    scale3, slant3, bias3 = back_coefs(g3, mean3, inv3, sums3, cross3, count)
    mean, inv = moments(own2, rec2, peers, float(size))
    weight = w[...]
    zero = jnp.zeros_like(weight)
    upper = jnp.concatenate([weight, zero], 0)
    lower = jnp.concatenate([zero, weight], 0)
    sums = jnp.zeros((8, wide), F32)
    cross = jnp.zeros((8, wide), F32)
    for at in range(0, half, cols):
        back = None
        for base, side in ((at, upper), (half + at, lower)):
            rows = slice(base, base + cols)
            dh = (e3[rows, :] * scale3 + pre3[rows, :] * slant3 + bias3).astype(BF16)
            dh3[rows, :] = dh
            part = nt(dh, side)
            back = part if back is None else back + part
        pre = pre2[at : at + cols, :]
        grad = back * slope2[at : at + cols, :]
        e2[at : at + cols, :] = grad
        sums = sums + group(grad)
        cross = cross + group(grad * (pre - mean))
    msg[0:WIDE_HEAD, :] = wide_head_rows(both_halves(rowsum(sums)), both_halves(rowsum(cross) * inv))
    msg[WIDE_HEAD : WIDE_HEAD + edge, :] = edges(e2, edge).astype(BF16)
    msg[WIDE_HEAD + edge :, :] = edges(pre2, edge, mean).astype(BF16)


def expand_kernel(act2, dh3, out):
    half = act2.shape[0]
    mids = act2.shape[1] // 2
    out[...] = tn(act2[...], dh3[0:half, :])[0:mids, :] + tn(act2[...], dh3[half:, :])[mids:, :]


def sixth_kernel(
    peers, edge, pre2, e2, own5, rec5, own2, rec2, pre1, own1, rec1, prm, w, slope1,
    dext, e1, msg, scr,
):
    half, cols, wide = pre2.shape[0], edge // 2, pre2.shape[1]
    size = 2.0 * half
    count = size * (peers + 1)
    g2, _ = gain_shift(prm, 1, wide)
    mean2, inv2 = moments(own2, rec2, peers, size)
    sums2, cross2 = totals(own5, rec5, peers)
    scale2, slant2, bias2 = back_coefs(g2, mean2, inv2, sums2, cross2, count)
    mean, inv = moments(own1, rec1, peers, size)
    clear_gaps(scr, cols)
    acts = []
    for at in range(0, half, cols):
        dh = e2[at : at + cols, :] * scale2 + pre2[at : at + cols, :] * slant2 + bias2
        dext[edge + at : edge + at + cols, :] = dh.astype(BF16)
        if at < edge or at >= half - edge:
            acts.append((at, dh))
    first = jnp.concatenate([act for at, act in acts if at < edge], 0)
    last = jnp.concatenate([act for at, act in acts if at >= half - edge], 0)
    if peers:
        base = WIDE_HEAD * peers
        halo = (
            rec5[base : base + edge, :].astype(F32) * scale2
            + rec5[base + edge :, :].astype(F32) * slant2
            + (bias2 + slant2 * mean2)
        )
    else:
        halo = jnp.zeros((edge, wide), F32)
    fill_edges(dext, first, last, halo, edge)
    sums = jnp.zeros((8, wide), F32)
    cross = jnp.zeros((8, wide), F32)
    for i, at in enumerate(range(0, half, cols)):
        out = nt(taps(dext, edge, at, cols), w[...])
        scr[2 * i, GAP : GAP + cols, :] = out[:, 0:wide]
        scr[2 * i + 1, GAP : GAP + cols, :] = out[:, 2 * wide :]
        back = (
            out[:, wide : 2 * wide]
            + scr[2 * i, GAP + 2 : GAP + 2 + cols, :]
            + scr[2 * i + 1, GAP - 2 : GAP - 2 + cols, :]
        )
        pre = pre1[at : at + cols, :]
        grad = back * slope1[at : at + cols, :]
        e1[at : at + cols, :] = grad
        sums = sums + group(grad)
        cross = cross + group(grad * (pre - mean))
    msg[...] = head_rows(both_halves(rowsum(sums)), both_halves(rowsum(cross) * inv))


def fold(block, upper):
    mids = block.shape[0] // 2
    if upper:
        return swap_halves(block[0:mids, :]) + block[mids:, :]
    return block[0:mids, :] + swap_halves(block[mids:, :])


def dilated_kernel(edge, ext, dext, out, scr, dcat):
    cols, wide = edge // 2, ext.shape[1]
    half = dext.shape[0] - 2 * edge
    mids = wide // 2
    clear_gaps(scr, cols)
    for i, at in enumerate(range(0, half, cols)):
        mid = dext[edge + at : edge + at + cols, :]
        scr[i, GAP : GAP + cols, :] = mid.astype(F32)
        dcat[at : at + cols, 0:wide] = scr[i, GAP + 2 : GAP + 2 + cols, :].astype(BF16)
        dcat[at : at + cols, wide : 2 * wide] = mid
        dcat[at : at + cols, 2 * wide :] = scr[i, GAP - 2 : GAP - 2 + cols, :].astype(BF16)
    blocks = []
    for a in range(3):
        prod = tn(ext[a * edge : a * edge + half, :], dcat[...])
        blocks = blocks + [prod[:, b * wide : (b + 1) * wide] for b in range(3)]
    low = lower_half((mids, wide))
    for k in range(4):
        pair = jnp.where(low, fold(blocks[2 * k], False), fold(blocks[2 * k + 1], True))
        out[k * mids : (k + 1) * mids, :] = pair.astype(BF16)
    out[4 * mids : 5 * mids, :] = fold(blocks[8], False).astype(BF16)


def seventh_kernel(
    peers, pre1, e1, own6, rec6, own1, rec1, prm, im, gwd, gwe, own4, own5, dh1, *rest
):
    outs, scr = rest[:-1], rest[-1]
    half, wide = pre1.shape
    mids, chans = wide // 2, im.shape[1]
    size = 2.0 * half
    count = size * (peers + 1)
    g1, _ = gain_shift(prm, 0, wide)
    mean, inv = moments(own1, rec1, peers, size)
    sums, cross = totals(own6, rec6, peers)
    scale, slant, bias = back_coefs(g1, mean, inv, sums, cross, count)
    dh = (e1[...] * scale + pre1[...] * slant + bias).astype(BF16)
    dh1[...] = dh
    prod = tn(dh, im[0:half, :])[0:mids, :] + tn(dh, im[half:, :])[mids:, :]
    base = gwd.shape[0]
    scr[0:base, :] = gwd[...]
    for whole in (prod, gwe[...]):
        for part in range(chans // wide):
            scr[base : base + mids, :] = whole[:, part * wide : (part + 1) * wide].astype(BF16)
            base = base + mids
    rows = [head_row(own, 0, which) for own in (own6, own5) for which in (1, 0)]
    for row in (1, 0):
        rows = rows + [own4[row : row + 1, p * wide : (p + 1) * wide] for p in range(chans // wide)]
    rows.append(jnp.zeros((scr.shape[0] - base - len(rows), wide), F32))
    scr[base:, :] = jnp.concatenate(rows, 0).astype(BF16)
    me = lax.axis_index("space")
    for k, out in enumerate(outs):
        piece = out.shape[0]
        start = lax.rem(me + k, peers + 1) * piece
        out[...] = scr[pl.ds(pl.multiple_of(start, 16), piece), :]


def images_kernel(cols, dh1, w, e3, out):
    half = dh1.shape[0]
    weight = w[...]
    zero = jnp.zeros_like(weight)
    sides = (jnp.concatenate([weight, zero], 0), jnp.concatenate([zero, weight], 0))
    for at in range(0, half, cols):
        dh = dh1[at : at + cols, :]
        for side, base in zip(sides, (at, half + at)):
            out[base : base + cols, :] = (nn(dh, side) + e3[base : base + cols, :]).astype(BF16)


def unpack_kernel(peers, batch, *refs):
    pieces, refs = refs[: peers + 1], refs[peers + 1 :]
    gwr, gwd, gwe, gg1, gs1, gg2, gs2, gg3, gs3, scr = refs
    wide = scr.shape[1]
    mids = wide // 2
    chans = gwe.shape[1]
    parts = chans // wide
    me = lax.axis_index("space")
    for k, ref in enumerate(pieces):
        piece = ref.shape[0]
        start = lax.rem(me + peers + 1 - k, peers + 1) * piece
        scr[pl.ds(pl.multiple_of(start, 16), piece), :] = ref[...].astype(F32) / batch
    for k in range(5):
        block = scr[k * mids : (k + 1) * mids, :]
        gwd[2 * k] = block[:, 0:mids]
        if k < 4:
            gwd[2 * k + 1] = swap_halves(block)[:, 0:mids]
    base = 5 * mids
    for ref in (gwr, gwe):
        for part in range(parts):
            ref[:, part * wide : (part + 1) * wide] = scr[base : base + mids, :]
            base = base + mids
    for ref in (gg1, gs1, gg2, gs2):
        ref[...] = scr[base : base + 1, 0:mids]
        base = base + 1
    for ref in (gg3, gs3):
        for part in range(parts):
            ref[:, part * wide : (part + 1) * wide] = scr[base : base + 1, :]
            base = base + 1


HBM = pl.BlockSpec(memory_space=pltpu.HBM)
VMEM = pl.BlockSpec(memory_space=pltpu.VMEM)


def call(kernel, outs, *args, scratch=(), flops=0, far=(), final=False):
    size = sum(item.size * item.dtype.itemsize for item in args)
    size = size + sum(functools.reduce(lambda x, y: x * y, s, 1) * 4 for s, _ in outs)
    kind_of = jax.ShapeDtypeStruct if final else pltpu.VMEM
    args = [pltpu.with_memory_space_constraint(x, pltpu.HBM) if k in far else x for k, x in enumerate(args)]
    out = pl.pallas_call(
        kernel,
        out_shape=[kind_of(shape, kind) for shape, kind in outs],
        in_specs=[HBM if k in far else VMEM for k in range(len(args))],
        out_specs=[VMEM] * len(outs),
        scratch_shapes=list(scratch),
        cost_estimate=pl.CostEstimate(flops=flops, bytes_accessed=size, transcendentals=0),
        compiler_params=pltpu.CompilerParams(vmem_limit_bytes=16 * 1024 * 1024),
    )(*args)
    return out[0] if len(outs) == 1 else out


def swapped(value, axis, step):
    count = lax.axis_size(axis)
    return lax.ppermute(value, axis, [(i, (i + step) % count) for i in range(count)])


def exchanged(msg, peers):
    if peers == 0:
        return msg
    if peers == 1:
        return swapped(msg, "space", 1)
    head = WIDE_HEAD if msg.dtype == BF16 else HEAD
    heads = [swapped(msg[0:head], "space", k + 1) for k in range(peers)]
    if msg.shape[0] > head:
        above = swapped(msg[head:], "space", 1)
        below = swapped(msg[head:], "space", peers)
        low = lax.broadcasted_iota(jnp.int32, above.shape, 1) < above.shape[1] // 2
        heads.append(jnp.where(low, above, below))
    return jnp.concatenate(heads, 0)


def flipped_dp(part, masks):
    count, sides = lax.axis_size("dp"), lax.axis_size("space")
    pairs = []
    for i in range(count * sides):
        dp, side = divmod(i, sides)
        pairs.append((i, (dp ^ masks[side % len(masks)]) * sides + side))
    return lax.ppermute(part, ("dp", "space"), pairs).astype(F32)


def summed_over_dp(part):
    count = lax.axis_size("dp")
    if count & (count - 1):
        return lax.psum(part.astype(F32), "dp").astype(BF16)
    bits = [1 << k for k in range(count.bit_length() - 1)]
    twos = [bits[k : k + 2] for k in range(0, len(bits) - 1, 2)]
    for k in range(len(twos)):
        turn = [twos[(k + side * (len(twos) // 2)) % len(twos)] for side in range(2)]
        low = flipped_dp(part, [pair[0] for pair in turn])
        high = flipped_dp(part, [pair[1] for pair in turn])
        both = flipped_dp(part, [pair[0] + pair[1] for pair in turn])
        part = ((part.astype(F32) + low) + (high + both)).astype(BF16)
    if len(bits) % 2:
        part = (part.astype(F32) + flipped_dp(part, bits[-1:])).astype(BF16)
    return part


def shards(
    images, w_reduce, w_dilated, w_expand, gain_one, shift_one, gain_two, shift_two,
    gain_three, shift_three, cotangent,
):
    rows, cols, chans = images.shape[1:]
    mids = w_reduce.shape[1]
    wide = 2 * mids
    pixels = rows * cols
    half, edge = pixels // 2, 2 * cols
    ext_rows = half + 2 * edge
    count = lax.axis_size("space")
    peers = count - 1
    part = functools.partial
    im = images.reshape(pixels, chans)
    cot = cotangent.reshape(pixels, chans)
    row = lambda item: item.reshape(1, -1)
    gaps = lambda n: pltpu.VMEM((n, cols + 2 * GAP, wide), F32)
    chunks = half // cols
    w_rows = w_reduce.T
    gates = 2 * pixels * wide * chans

    pre1, own1, im_held, w_held = call(
        part(first_kernel, edge),
        [((half, wide), F32), ((WIDE_HEAD + edge, wide), BF16), ((pixels, chans), BF16)]
        + [(w_rows.shape, BF16)],
        im.reshape(2, half, chans), w_rows, flops=gates, far=(0, 1),
        scratch=[pltpu.VMEM((2, half, chans), BF16), pltpu.VMEM(w_rows.shape, BF16)]
        + [pltpu.SemaphoreType.DMA((3,))],
    )
    rec1 = exchanged(own1, peers)
    fwd, bwd, we, prm = call(
        weights_kernel,
        [((3 * wide, 3 * wide), BF16)] * 2 + [(w_expand.shape, BF16), ((8, chans), F32)],
        w_dilated, w_expand, row(gain_one), row(shift_one), row(gain_two), row(shift_two),
        row(gain_three), row(shift_three), flops=10**10, far=(0,),
        scratch=[pltpu.VMEM(w_dilated.shape, BF16), pltpu.SemaphoreType.DMA],
    )
    ext, pre2, own2 = call(
        part(second_kernel, peers, edge),
        [((ext_rows, wide), BF16), ((half, wide), F32), ((HEAD, wide), F32)],
        pre1, own1, rec1, prm, fwd, scratch=[gaps(2 * chunks)], flops=2 * half * 9 * wide * wide,
    )
    rec2 = exchanged(own2, peers)
    im_half, cot_half = call(
        part(halves_kernel, 64), [((pixels, chans), F32)] * 2, im_held, cot,
        flops=4 * pixels * chans,
    )
    act2, pre3, own3 = call(
        part(third_kernel, peers, cols),
        [((half, wide), BF16), ((pixels, chans), F32), ((HEAD, chans), F32)],
        pre2, own2, rec2, prm, we, flops=gates,
    )
    rec3 = exchanged(own3, peers)
    slope1, slope2 = call(
        part(slopes_kernel, peers, cols), [((half, wide), F32)] * 2,
        pre1, own1, rec1, pre2, own2, rec2, prm, flops=30 * half * wide,
    )
    e3, own4 = call(
        part(fourth_kernel, peers, 64), [((pixels, chans), F32), ((HEAD, chans), F32)],
        pre3, own3, rec3, prm, im_half, cot_half, flops=30 * pixels * chans,
    )
    rec4 = exchanged(own4, peers)
    dh3, e2, own5 = call(
        part(fifth_kernel, peers, edge),
        [((pixels, chans), BF16), ((half, wide), F32), ((WIDE_HEAD + 2 * edge, wide), BF16)],
        pre3, e3, own3, rec3, own4, rec4, prm, we, pre2, own2, rec2, slope2, flops=gates,
    )
    rec5 = exchanged(own5, peers)
    gwe = call(expand_kernel, [((mids, chans), F32)], act2, dh3, flops=gates)
    dext, e1, own6 = call(
        part(sixth_kernel, peers, edge),
        [((ext_rows, wide), BF16), ((half, wide), F32), ((HEAD, wide), F32)],
        pre2, e2, own5, rec5, own2, rec2, pre1, own1, rec1, prm, bwd, slope1,
        scratch=[gaps(2 * chunks)], flops=2 * half * 9 * wide * wide,
    )
    rec6 = exchanged(own6, peers)
    gwd = call(
        part(dilated_kernel, edge), [((5 * mids, wide), BF16)], ext, dext,
        scratch=[gaps(chunks), pltpu.VMEM((half, 3 * wide), BF16)],
        flops=2 * half * 9 * wide * wide,
    )
    length = 5 * mids + 2 * (chans // wide) * mids + 16
    piece = -(-length // (16 * count)) * 16
    dh1, *pieces = call(
        part(seventh_kernel, peers),
        [((half, wide), BF16)] + [((piece, wide), BF16)] * count,
        pre1, e1, own6, rec6, own1, rec1, prm, im_held, gwd, gwe, own4, own5, flops=gates,
        scratch=[pltpu.VMEM((piece * count, wide), BF16)],
    )
    total = pieces[0].astype(F32)
    for k in range(peers):
        total = total + swapped(pieces[k + 1], "space", k + 1).astype(F32)
    total = summed_over_dp(total.astype(BF16))
    whole = [total] + [swapped(total, "space", k + 1) for k in range(peers)]
    grad_images = call(
        part(images_kernel, cols), [((pixels, chans), BF16)], dh1, w_held, e3,
        flops=gates, final=True,
    )
    result = call(
        part(result_kernel, peers, 64), [((pixels, chans), BF16)],
        pre3, own3, rec3, prm, im_half, flops=10 * pixels * chans, final=True,
    )
    grads = call(
        part(unpack_kernel, peers, float(lax.axis_size("dp"))),
        [((mids, chans), F32), ((9, mids, mids), F32), ((mids, chans), F32)]
        + [((1, mids), F32)] * 4 + [((1, chans), F32)] * 2,
        *whole, scratch=[pltpu.VMEM((piece * count, wide), F32)], final=True,
    )
    gwr, gwd, gwe = grads[:3]
    shape = images.shape
    return (
        result.reshape(shape), grad_images.reshape(shape), gwr.T, gwd.reshape(3, 3, mids, mids), gwe,
    ) + tuple(item.reshape(-1) for item in grads[3:])


def solution(mesh):
    big = P("dp", "space", None, None)
    return jax.shard_map(
        shards,
        mesh=mesh,
        in_specs=(big,) + (P(),) * 9 + (big,),
        out_specs=(big, big) + (P(),) * 9,
        check_vma=False,
    )
```

```python
import functools

import jax
import jax.numpy as jnp
from jax import lax
from jax.experimental import pallas as pl
from jax.experimental.pallas import tpu as pltpu
from jax.sharding import PartitionSpec as P

epsilon = 1e-05
F32 = jnp.float32
BF16 = jnp.bfloat16
HEAD = 8
WIDE_HEAD = 16
GAP = 8


def nn(left, right):
    return jnp.dot(left, right, preferred_element_type=F32)


def nt(left, right):
    return lax.dot_general(left, right, (((1,), (1,)), ((), ())), preferred_element_type=F32)


def tn(left, right):
    return lax.dot_general(left, right, (((0,), (0,)), ((), ())), preferred_element_type=F32)


def swap_halves(value):
    return pltpu.roll(value, value.shape[1] // 2, 1)


def lower_half(shape):
    return lax.broadcasted_iota(jnp.int32, shape, 1) < shape[1] // 2


def both_halves(row):
    return row + swap_halves(row)


def rowsum(value):
    return jnp.sum(value, 0, keepdims=True)


def group(value):
    return jnp.sum(value.reshape(value.shape[0] // 8, 8, value.shape[1]), 0)


def silu(value):
    half = 0.5 * value
    return half + half * jnp.tanh(half)


def slope(value):
    half = 0.5 * value
    turn = jnp.tanh(half)
    return (0.5 + 0.5 * turn) * (1.0 + half * (1.0 - turn))


def head_row(ref, item, which):
    if ref.dtype == BF16:
        terms = ref[WIDE_HEAD * item : WIDE_HEAD * (item + 1), :].astype(F32)
        at = 3 * which
        return terms[at : at + 1, :] + terms[at + 1 : at + 2, :] + terms[at + 2 : at + 3, :]
    at = HEAD * item + which
    return ref[at : at + 1, :]


def moments(own, rec, peers, local):
    means = [head_row(own, 0, 0)] + [head_row(rec, k, 0) for k in range(peers)]
    squares = [head_row(own, 0, 1)] + [head_row(rec, k, 1) for k in range(peers)]
    mean = sum(means) / (peers + 1)
    total = sum(squares) + local * sum((item - mean) * (item - mean) for item in means)
    return mean, lax.rsqrt(total / (local * (peers + 1)) + epsilon)


def totals(own, rec, peers):
    sums = head_row(own, 0, 0) + sum(head_row(rec, k, 0) for k in range(peers))
    cross = head_row(own, 0, 1) + sum(head_row(rec, k, 1) for k in range(peers))
    return sums, cross


def head_rows(first, second):
    rest = jnp.zeros((HEAD - 2, first.shape[1]), F32)
    return jnp.concatenate([first, second, rest], 0)


def three_terms(value):
    high = value.astype(BF16).astype(F32)
    mid = (value - high).astype(BF16).astype(F32)
    return [high, mid, value - high - mid]


def wide_head_rows(first, second):
    rest = jnp.zeros((WIDE_HEAD - 6, first.shape[1]), F32)
    return jnp.concatenate(three_terms(first) + three_terms(second) + [rest], 0).astype(BF16)


def edges(ref, edge, centre=0.0):
    size = ref.shape[0]
    top = ref[0:edge, :]
    return swap_halves(jnp.where(lower_half(top.shape), top, ref[size - edge : size, :]) - centre)


def fill_edges(ext, first, last, halo, edge):
    size = ext.shape[0]
    low = lower_half(halo.shape)
    halo = halo * edge_mask(halo.shape)
    ext[0:edge, :] = jnp.where(low, halo, swap_halves(last)).astype(BF16)
    ext[size - edge : size, :] = jnp.where(low, swap_halves(first), halo).astype(BF16)


def norm_coefs(gain, shift, mean, inv):
    scale = gain * inv
    return scale, shift - mean * scale


def back_coefs(gain, mean, inv, sums, cross, count):
    scale = gain * inv
    slant = -scale * inv * cross / count
    return scale, slant, -scale * sums / count - slant * mean


def centred_squares(ref, mean, step):
    acc = jnp.zeros((8, ref.shape[1]), F32)
    for at in range(0, ref.shape[0], step):
        gap = ref[at : at + step, :] - mean
        acc = acc + group(gap * gap)
    return rowsum(acc)


def first_kernel(
    edge, im, w, wd, pre, msg, im_held, w_held, wd_held, im_near, w_near, wd_near, sems
):
    half, cols, wide = pre.shape[0], edge // 2, pre.shape[1]
    fetch = pltpu.make_async_copy(w, w_near, sems.at[0])
    fetch.start()
    cut = half // cols // 2 * cols
    copies = []
    for k, (base, size) in enumerate(((0, cut), (cut, half - cut))):
        rows = pl.ds(base, size)
        copies.append(
            pltpu.make_async_copy(im.at[:, rows, :], im_near.at[:, rows, :], sems.at[k + 1])
        )
        copies[-1].start()
    fetch_wd = pltpu.make_async_copy(wd, wd_near, sems.at[3])
    fetch_wd.start()
    fetch.wait()
    weight = w_near[...]
    w_held[...] = weight
    zero = jnp.zeros_like(weight)
    sides = (jnp.concatenate([weight, zero], 0), jnp.concatenate([zero, weight], 0))
    acc = jnp.zeros((8, wide), F32)
    for at in range(0, half, cols):
        if at in (0, cut):
            copies[min(at, 1)].wait()
        part = None
        for k, side in enumerate(sides):
            block = im_near[k, at : at + cols, :]
            im_held[k * half + at : k * half + at + cols, :] = block
            prod = nt(block, side)
            part = prod if part is None else part + prod
        pre[at : at + cols, :] = part
        acc = acc + group(part)
    mean = both_halves(rowsum(acc)) / (2 * half)
    msg[0:WIDE_HEAD, :] = wide_head_rows(mean, both_halves(centred_squares(pre, mean, cols)))
    msg[WIDE_HEAD:, :] = edges(pre, edge, mean).astype(BF16)
    fetch_wd.wait()
    wd_held[...] = wd_near[...]


def tap_blocks(w):
    mids = w.shape[-1]
    zero = jnp.zeros((mids, mids), BF16)
    for a in range(3):
        for b in range(3):
            block = w[a, b]
            yield a, b, jnp.concatenate(
                [jnp.concatenate([block, zero], 1), jnp.concatenate([zero, block], 1)], 0
            )


def weights_kernel(wd, we, g1, s1, g2, s2, g3, s3, fwd, bwd, we_held, prm):
    wide = 2 * wd.shape[-1]
    we_held[...] = we[...]
    prm[...] = jnp.zeros(prm.shape, F32)
    for k, ref in enumerate((g1, s1, g2, s2)):
        prm[k : k + 1, 0:wide] = jnp.concatenate([ref[...], ref[...]], 1)
    prm[4:5, :] = g3[...]
    prm[5:6, :] = s3[...]
    for a, b, both in tap_blocks(wd):
        k = 2 - a
        fwd[a * wide : (a + 1) * wide, b * wide : (b + 1) * wide] = both
        bwd[b * wide : (b + 1) * wide, k * wide : (k + 1) * wide] = both


def gain_shift(prm, norm, wide):
    return prm[2 * norm : 2 * norm + 1, 0:wide], prm[2 * norm + 1 : 2 * norm + 2, 0:wide]


def edge_mask(shape):
    me = lax.axis_index("space")
    above = jnp.where(me > 0, 1.0, 0.0)
    below = jnp.where(me < lax.axis_size("space") - 1, 1.0, 0.0)
    return jnp.where(lower_half(shape), above, below)


def taps(ext, edge, at, cols):
    return jnp.concatenate([ext[a * edge + at : a * edge + at + cols, :] for a in range(3)], 1)


def clear_gaps(scr, cols):
    zero = jnp.zeros((scr.shape[0], GAP, scr.shape[2]), F32)
    scr[:, 0:GAP, :] = zero
    scr[:, GAP + cols :, :] = zero


def second_kernel(
    peers, edge, pre1, own1, rec1, prm, w, ext, pre2, msg, scr
):
    half, cols, wide = pre2.shape[0], edge // 2, pre2.shape[1]
    g1, s1 = gain_shift(prm, 0, wide)
    mean, inv = moments(own1, rec1, peers, 2.0 * half)
    scale, bias = norm_coefs(g1, s1, mean, inv)
    clear_gaps(scr, cols)
    last = first = None
    acts = []
    for at in range(0, half, cols):
        act = silu(pre1[at : at + cols, :] * scale + bias)
        ext[edge + at : edge + at + cols, :] = act.astype(BF16)
        if at < edge or at >= half - edge:
            acts.append((at, act))
    first = jnp.concatenate([act for at, act in acts if at < edge], 0)
    last = jnp.concatenate([act for at, act in acts if at >= half - edge], 0)
    if peers:
        above, below = head_row(rec1, 0, 0), head_row(rec1, peers - 1, 0)
        centre = jnp.where(lower_half(above.shape), above, below)
        halo = silu((rec1[WIDE_HEAD * peers :, :].astype(F32) + centre) * scale + bias)
    else:
        halo = jnp.zeros((edge, wide), F32)
    fill_edges(ext, first, last, halo, edge)
    acc = jnp.zeros((8, wide), F32)
    for i, at in enumerate(range(0, half, cols)):
        out = nn(taps(ext, edge, at, cols), w[...])
        scr[2 * i, GAP : GAP + cols, :] = out[:, 0:wide]
        scr[2 * i + 1, GAP : GAP + cols, :] = out[:, 2 * wide :]
        part = (
            out[:, wide : 2 * wide]
            + scr[2 * i, GAP - 2 : GAP - 2 + cols, :]
            + scr[2 * i + 1, GAP + 2 : GAP + 2 + cols, :]
        )
        pre2[at : at + cols, :] = part
        acc = acc + group(part)
    mean = both_halves(rowsum(acc)) / (2 * half)
    msg[...] = head_rows(mean, both_halves(centred_squares(pre2, mean, cols)))


def third_kernel(peers, cols, pre2, own2, rec2, prm, w, act2, pre3, msg):
    half = pre2.shape[0]
    g2, s2 = gain_shift(prm, 1, pre2.shape[1])
    mean, inv = moments(own2, rec2, peers, 2.0 * half)
    scale, bias = norm_coefs(g2, s2, mean, inv)
    weight = w[...]
    zero = jnp.zeros_like(weight)
    upper = jnp.concatenate([weight, zero], 0)
    lower = jnp.concatenate([zero, weight], 0)
    acc = jnp.zeros((8, pre3.shape[1]), F32)
    for at in range(0, half, cols):
        act = silu(pre2[at : at + cols, :] * scale + bias).astype(BF16)
        act2[at : at + cols, :] = act
        part = nn(act, upper)
        pre3[at : at + cols, :] = part
        acc = acc + group(part)
        part = nn(act, lower)
        pre3[half + at : half + at + cols, :] = part
        acc = acc + group(part)
    mean = rowsum(acc) / (2 * half)
    msg[...] = head_rows(mean, centred_squares(pre3, mean, cols))


def halves_kernel(step, im, cot, im_half, cot_half):
    def body(i, carry):
        at = pl.ds(pl.multiple_of(i * step, step), step)
        im_half[at, :] = 0.5 * im[at, :].astype(F32)
        cot_half[at, :] = 0.5 * cot[at, :].astype(F32)
        return carry

    lax.fori_loop(0, im.shape[0] // step, body, 0, unroll=2)


def slopes_kernel(peers, step, pre1, own1, rec1, pre2, own2, rec2, prm, slope1, slope2):
    half, wide = pre1.shape
    for norm, pre, own, rec, out in ((0, pre1, own1, rec1, slope1), (1, pre2, own2, rec2, slope2)):
        mean, inv = moments(own, rec, peers, 2.0 * half)
        scale, bias = norm_coefs(*gain_shift(prm, norm, wide), mean, inv)
        for at in range(0, half, step):
            out[at : at + step, :] = slope(pre[at : at + step, :] * scale + bias)


def halved_coefs(peers, own3, rec3, prm, size):
    mean, inv = moments(own3, rec3, peers, float(size))
    gain, shift = gain_shift(prm, 2, own3.shape[1])
    scale, bias = norm_coefs(gain, shift, mean, inv)
    return 0.5 * scale, 0.5 * bias, gain, shift


def fourth_kernel(peers, step, pre3, own3, rec3, prm, im_half, cot_half, e3, msg):
    size, chans = pre3.shape
    scale, bias, gain, shift = halved_coefs(peers, own3, rec3, prm, size)

    def body(i, carry):
        sums, cross = carry
        at = pl.ds(pl.multiple_of(i * step, step), step)
        out = pre3[at, :] * scale + bias
        half = out + im_half[at, :]
        turn = jnp.tanh(half)
        grad = cot_half[at, :] * ((1.0 + turn) * (1.0 + half * (1.0 - turn)))
        e3[at, :] = grad
        return sums + group(grad), cross + group(grad * out)

    zero = jnp.zeros((8, chans), F32)
    sums, cross = lax.fori_loop(0, size // step, body, (zero, zero), unroll=2)
    sums = rowsum(sums)
    msg[...] = head_rows(sums, (2.0 * rowsum(cross) - shift * sums) / gain)


def result_kernel(peers, step, pre3, own3, rec3, prm, im_half, out):
    size = pre3.shape[0]
    scale, bias, _, _ = halved_coefs(peers, own3, rec3, prm, size)

    def body(i, carry):
        at = pl.ds(pl.multiple_of(i * step, step), step)
        half = pre3[at, :] * scale + bias + im_half[at, :]
        out[at, :] = (half + half * jnp.tanh(half)).astype(BF16)
        return carry

    lax.fori_loop(0, size // step, body, 0, unroll=2)


def fifth_kernel(
    peers, edge, pre3, e3, own3, rec3, own4, rec4, prm, w, pre2, own2, rec2, slope2, dh3, e2, msg
):
    size, half, cols, wide = pre3.shape[0], pre2.shape[0], edge // 2, pre2.shape[1]
    count = float(size * (peers + 1))
    g3, _ = gain_shift(prm, 2, pre3.shape[1])
    mean3, inv3 = moments(own3, rec3, peers, float(size))
    sums3, cross3 = totals(own4, rec4, peers)
    scale3, slant3, bias3 = back_coefs(g3, mean3, inv3, sums3, cross3, count)
    mean, inv = moments(own2, rec2, peers, float(size))
    weight = w[...]
    zero = jnp.zeros_like(weight)
    upper = jnp.concatenate([weight, zero], 0)
    lower = jnp.concatenate([zero, weight], 0)
    sums = jnp.zeros((8, wide), F32)
    cross = jnp.zeros((8, wide), F32)
    for at in range(0, half, cols):
        back = None
        for base, side in ((at, upper), (half + at, lower)):
            rows = slice(base, base + cols)
            dh = (e3[rows, :] * scale3 + pre3[rows, :] * slant3 + bias3).astype(BF16)
            dh3[rows, :] = dh
            part = nt(dh, side)
            back = part if back is None else back + part
        pre = pre2[at : at + cols, :]
        grad = back * slope2[at : at + cols, :]
        e2[at : at + cols, :] = grad
        sums = sums + group(grad)
        cross = cross + group(grad * (pre - mean))
    msg[0:WIDE_HEAD, :] = wide_head_rows(both_halves(rowsum(sums)), both_halves(rowsum(cross) * inv))
    msg[WIDE_HEAD : WIDE_HEAD + edge, :] = edges(e2, edge).astype(BF16)
    msg[WIDE_HEAD + edge :, :] = edges(pre2, edge, mean).astype(BF16)


def expand_kernel(act2, dh3, out):
    half = act2.shape[0]
    mids = act2.shape[1] // 2
    out[...] = tn(act2[...], dh3[0:half, :])[0:mids, :] + tn(act2[...], dh3[half:, :])[mids:, :]


def sixth_kernel(
    peers, edge, pre2, e2, own5, rec5, own2, rec2, pre1, own1, rec1, prm, w, slope1,
    dext, e1, msg, scr,
):
    half, cols, wide = pre2.shape[0], edge // 2, pre2.shape[1]
    size = 2.0 * half
    count = size * (peers + 1)
    g2, _ = gain_shift(prm, 1, wide)
    mean2, inv2 = moments(own2, rec2, peers, size)
    sums2, cross2 = totals(own5, rec5, peers)
    scale2, slant2, bias2 = back_coefs(g2, mean2, inv2, sums2, cross2, count)
    mean, inv = moments(own1, rec1, peers, size)
    clear_gaps(scr, cols)
    acts = []
    for at in range(0, half, cols):
        dh = e2[at : at + cols, :] * scale2 + pre2[at : at + cols, :] * slant2 + bias2
        dext[edge + at : edge + at + cols, :] = dh.astype(BF16)
        if at < edge or at >= half - edge:
            acts.append((at, dh))
    first = jnp.concatenate([act for at, act in acts if at < edge], 0)
    last = jnp.concatenate([act for at, act in acts if at >= half - edge], 0)
    if peers:
        base = WIDE_HEAD * peers
        halo = (
            rec5[base : base + edge, :].astype(F32) * scale2
            + rec5[base + edge :, :].astype(F32) * slant2
            + (bias2 + slant2 * mean2)
        )
    else:
        halo = jnp.zeros((edge, wide), F32)
    fill_edges(dext, first, last, halo, edge)
    sums = jnp.zeros((8, wide), F32)
    cross = jnp.zeros((8, wide), F32)
    for i, at in enumerate(range(0, half, cols)):
        out = nt(taps(dext, edge, at, cols), w[...])
        scr[2 * i, GAP : GAP + cols, :] = out[:, 0:wide]
        scr[2 * i + 1, GAP : GAP + cols, :] = out[:, 2 * wide :]
        back = (
            out[:, wide : 2 * wide]
            + scr[2 * i, GAP + 2 : GAP + 2 + cols, :]
            + scr[2 * i + 1, GAP - 2 : GAP - 2 + cols, :]
        )
        pre = pre1[at : at + cols, :]
        grad = back * slope1[at : at + cols, :]
        e1[at : at + cols, :] = grad
        sums = sums + group(grad)
        cross = cross + group(grad * (pre - mean))
    msg[...] = head_rows(both_halves(rowsum(sums)), both_halves(rowsum(cross) * inv))


def fold(block, upper):
    mids = block.shape[0] // 2
    if upper:
        return swap_halves(block[0:mids, :]) + block[mids:, :]
    return block[0:mids, :] + swap_halves(block[mids:, :])


def dilated_kernel(edge, ext, dext, out, scr, dcat):
    cols, wide = edge // 2, ext.shape[1]
    half = dext.shape[0] - 2 * edge
    mids = wide // 2
    clear_gaps(scr, cols)
    for i, at in enumerate(range(0, half, cols)):
        mid = dext[edge + at : edge + at + cols, :]
        scr[i, GAP : GAP + cols, :] = mid.astype(F32)
        dcat[at : at + cols, 0:wide] = scr[i, GAP + 2 : GAP + 2 + cols, :].astype(BF16)
        dcat[at : at + cols, wide : 2 * wide] = mid
        dcat[at : at + cols, 2 * wide :] = scr[i, GAP - 2 : GAP - 2 + cols, :].astype(BF16)
    blocks = []
    for a in range(3):
        prod = tn(ext[a * edge : a * edge + half, :], dcat[...])
        blocks = blocks + [prod[:, b * wide : (b + 1) * wide] for b in range(3)]
    low = lower_half((mids, wide))
    for k in range(4):
        pair = jnp.where(low, fold(blocks[2 * k], False), fold(blocks[2 * k + 1], True))
        out[k * mids : (k + 1) * mids, :] = pair.astype(BF16)
    out[4 * mids : 5 * mids, :] = fold(blocks[8], False).astype(BF16)


def seventh_kernel(
    peers, pre1, e1, own6, rec6, own1, rec1, prm, im, gwd, gwe, own4, own5, dh1, *rest
):
    outs, scr = rest[:-1], rest[-1]
    half, wide = pre1.shape
    mids, chans = wide // 2, im.shape[1]
    size = 2.0 * half
    count = size * (peers + 1)
    g1, _ = gain_shift(prm, 0, wide)
    mean, inv = moments(own1, rec1, peers, size)
    sums, cross = totals(own6, rec6, peers)
    scale, slant, bias = back_coefs(g1, mean, inv, sums, cross, count)
    dh = (e1[...] * scale + pre1[...] * slant + bias).astype(BF16)
    dh1[...] = dh
    prod = tn(dh, im[0:half, :])[0:mids, :] + tn(dh, im[half:, :])[mids:, :]
    base = gwd.shape[0]
    scr[0:base, :] = gwd[...]
    for whole in (prod, gwe[...]):
        for part in range(chans // wide):
            scr[base : base + mids, :] = whole[:, part * wide : (part + 1) * wide].astype(BF16)
            base = base + mids
    rows = [head_row(own, 0, which) for own in (own6, own5) for which in (1, 0)]
    for row in (1, 0):
        rows = rows + [own4[row : row + 1, p * wide : (p + 1) * wide] for p in range(chans // wide)]
    rows.append(jnp.zeros((scr.shape[0] - base - len(rows), wide), F32))
    scr[base:, :] = jnp.concatenate(rows, 0).astype(BF16)
    me = lax.axis_index("space")
    for k, out in enumerate(outs):
        piece = out.shape[0]
        start = lax.rem(me + k, peers + 1) * piece
        out[...] = scr[pl.ds(pl.multiple_of(start, 16), piece), :]


def images_kernel(cols, dh1, w, e3, out):
    half = dh1.shape[0]
    weight = w[...]
    zero = jnp.zeros_like(weight)
    sides = (jnp.concatenate([weight, zero], 0), jnp.concatenate([zero, weight], 0))
    for at in range(0, half, cols):
        dh = dh1[at : at + cols, :]
        for side, base in zip(sides, (at, half + at)):
            out[base : base + cols, :] = (nn(dh, side) + e3[base : base + cols, :]).astype(BF16)


def unpack_kernel(peers, batch, *refs):
    pieces, refs = refs[: peers + 1], refs[peers + 1 :]
    gwr, gwd, gwe, gg1, gs1, gg2, gs2, gg3, gs3, scr = refs
    wide = scr.shape[1]
    mids = wide // 2
    chans = gwe.shape[1]
    parts = chans // wide
    me = lax.axis_index("space")
    for k, ref in enumerate(pieces):
        piece = ref.shape[0]
        start = lax.rem(me + peers + 1 - k, peers + 1) * piece
        scr[pl.ds(pl.multiple_of(start, 16), piece), :] = ref[...].astype(F32) / batch
    for k in range(5):
        block = scr[k * mids : (k + 1) * mids, :]
        gwd[2 * k] = block[:, 0:mids]
        if k < 4:
            gwd[2 * k + 1] = swap_halves(block)[:, 0:mids]
    base = 5 * mids
    for ref in (gwr, gwe):
        for part in range(parts):
            ref[:, part * wide : (part + 1) * wide] = scr[base : base + mids, :]
            base = base + mids
    for ref in (gg1, gs1, gg2, gs2):
        ref[...] = scr[base : base + 1, 0:mids]
        base = base + 1
    for ref in (gg3, gs3):
        for part in range(parts):
            ref[:, part * wide : (part + 1) * wide] = scr[base : base + 1, :]
            base = base + 1


HBM = pl.BlockSpec(memory_space=pltpu.HBM)
VMEM = pl.BlockSpec(memory_space=pltpu.VMEM)


def call(kernel, outs, *args, scratch=(), flops=0, far=(), final=False):
    size = sum(item.size * item.dtype.itemsize for item in args)
    size = size + sum(functools.reduce(lambda x, y: x * y, s, 1) * 4 for s, _ in outs)
    kind_of = jax.ShapeDtypeStruct if final else pltpu.VMEM
    args = [pltpu.with_memory_space_constraint(x, pltpu.HBM) if k in far else x for k, x in enumerate(args)]
    out = pl.pallas_call(
        kernel,
        out_shape=[kind_of(shape, kind) for shape, kind in outs],
        in_specs=[HBM if k in far else VMEM for k in range(len(args))],
        out_specs=[VMEM] * len(outs),
        scratch_shapes=list(scratch),
        cost_estimate=pl.CostEstimate(flops=flops, bytes_accessed=size, transcendentals=0),
        compiler_params=pltpu.CompilerParams(vmem_limit_bytes=16 * 1024 * 1024),
    )(*args)
    return out[0] if len(outs) == 1 else out


def swapped(value, axis, step):
    count = lax.axis_size(axis)
    return lax.ppermute(value, axis, [(i, (i + step) % count) for i in range(count)])


def exchanged(msg, peers):
    if peers == 0:
        return msg
    if peers == 1:
        return swapped(msg, "space", 1)
    head = WIDE_HEAD if msg.dtype == BF16 else HEAD
    heads = [swapped(msg[0:head], "space", k + 1) for k in range(peers)]
    if msg.shape[0] > head:
        above = swapped(msg[head:], "space", 1)
        below = swapped(msg[head:], "space", peers)
        low = lax.broadcasted_iota(jnp.int32, above.shape, 1) < above.shape[1] // 2
        heads.append(jnp.where(low, above, below))
    return jnp.concatenate(heads, 0)


def flipped_dp(part, masks):
    count, sides = lax.axis_size("dp"), lax.axis_size("space")
    pairs = []
    for i in range(count * sides):
        dp, side = divmod(i, sides)
        pairs.append((i, (dp ^ masks[side % len(masks)]) * sides + side))
    return lax.ppermute(part, ("dp", "space"), pairs).astype(F32)


def summed_over_dp(part):
    count = lax.axis_size("dp")
    if count & (count - 1):
        return lax.psum(part.astype(F32), "dp").astype(BF16)
    bits = [1 << k for k in range(count.bit_length() - 1)]
    twos = [bits[k : k + 2] for k in range(0, len(bits) - 1, 2)]
    for k in range(len(twos)):
        turn = [twos[(k + side * (len(twos) // 2)) % len(twos)] for side in range(2)]
        both = flipped_dp(part, [pair[0] + pair[1] for pair in turn])
        low = flipped_dp(part, [pair[0] for pair in turn])
        high = flipped_dp(part, [pair[1] for pair in turn])
        part = ((part.astype(F32) + low) + (high + both)).astype(BF16)
    if len(bits) % 2:
        part = (part.astype(F32) + flipped_dp(part, bits[-1:])).astype(BF16)
    return part


def shards(
    images, w_reduce, w_dilated, w_expand, gain_one, shift_one, gain_two, shift_two,
    gain_three, shift_three, cotangent,
):
    rows, cols, chans = images.shape[1:]
    mids = w_reduce.shape[1]
    wide = 2 * mids
    pixels = rows * cols
    half, edge = pixels // 2, 2 * cols
    ext_rows = half + 2 * edge
    count = lax.axis_size("space")
    peers = count - 1
    part = functools.partial
    im = images.reshape(pixels, chans)
    cot = cotangent.reshape(pixels, chans)
    row = lambda item: item.reshape(1, -1)
    gaps = lambda n: pltpu.VMEM((n, cols + 2 * GAP, wide), F32)
    chunks = half // cols
    w_rows = w_reduce.T
    gates = 2 * pixels * wide * chans

    pre1, own1, im_held, w_held, wd_held = call(
        part(first_kernel, edge),
        [((half, wide), F32), ((WIDE_HEAD + edge, wide), BF16), ((pixels, chans), BF16)]
        + [(w_rows.shape, BF16), (w_dilated.shape, BF16)],
        im.reshape(2, half, chans), w_rows, w_dilated, flops=gates, far=(0, 1, 2),
        scratch=[pltpu.VMEM((2, half, chans), BF16), pltpu.VMEM(w_rows.shape, BF16)]
        + [pltpu.VMEM(w_dilated.shape, BF16), pltpu.SemaphoreType.DMA((4,))],
    )
    rec1 = exchanged(own1, peers)
    fwd, bwd, we, prm = call(
        weights_kernel,
        [((3 * wide, 3 * wide), BF16)] * 2 + [(w_expand.shape, BF16), ((8, chans), F32)],
        wd_held, w_expand, row(gain_one), row(shift_one), row(gain_two), row(shift_two),
        row(gain_three), row(shift_three), flops=10**10,
    )
    ext, pre2, own2 = call(
        part(second_kernel, peers, edge),
        [((ext_rows, wide), BF16), ((half, wide), F32), ((HEAD, wide), F32)],
        pre1, own1, rec1, prm, fwd, scratch=[gaps(2 * chunks)], flops=2 * half * 9 * wide * wide,
    )
    rec2 = exchanged(own2, peers)
    im_half, cot_half = call(
        part(halves_kernel, 64), [((pixels, chans), F32)] * 2, im_held, cot,
        flops=4 * pixels * chans,
    )
    act2, pre3, own3 = call(
        part(third_kernel, peers, cols),
        [((half, wide), BF16), ((pixels, chans), F32), ((HEAD, chans), F32)],
        pre2, own2, rec2, prm, we, flops=gates,
    )
    rec3 = exchanged(own3, peers)
    slope1, slope2 = call(
        part(slopes_kernel, peers, cols), [((half, wide), F32)] * 2,
        pre1, own1, rec1, pre2, own2, rec2, prm, flops=30 * half * wide,
    )
    e3, own4 = call(
        part(fourth_kernel, peers, 64), [((pixels, chans), F32), ((HEAD, chans), F32)],
        pre3, own3, rec3, prm, im_half, cot_half, flops=30 * pixels * chans,
    )
    rec4 = exchanged(own4, peers)
    dh3, e2, own5 = call(
        part(fifth_kernel, peers, edge),
        [((pixels, chans), BF16), ((half, wide), F32), ((WIDE_HEAD + 2 * edge, wide), BF16)],
        pre3, e3, own3, rec3, own4, rec4, prm, we, pre2, own2, rec2, slope2, flops=gates,
    )
    rec5 = exchanged(own5, peers)
    gwe = call(expand_kernel, [((mids, chans), F32)], act2, dh3, flops=gates)
    dext, e1, own6 = call(
        part(sixth_kernel, peers, edge),
        [((ext_rows, wide), BF16), ((half, wide), F32), ((HEAD, wide), F32)],
        pre2, e2, own5, rec5, own2, rec2, pre1, own1, rec1, prm, bwd, slope1,
        scratch=[gaps(2 * chunks)], flops=2 * half * 9 * wide * wide,
    )
    rec6 = exchanged(own6, peers)
    gwd = call(
        part(dilated_kernel, edge), [((5 * mids, wide), BF16)], ext, dext,
        scratch=[gaps(chunks), pltpu.VMEM((half, 3 * wide), BF16)],
        flops=2 * half * 9 * wide * wide,
    )
    length = 5 * mids + 2 * (chans // wide) * mids + 16
    piece = -(-length // (16 * count)) * 16
    dh1, *pieces = call(
        part(seventh_kernel, peers),
        [((half, wide), BF16)] + [((piece, wide), BF16)] * count,
        pre1, e1, own6, rec6, own1, rec1, prm, im_held, gwd, gwe, own4, own5, flops=gates,
        scratch=[pltpu.VMEM((piece * count, wide), BF16)],
    )
    total = pieces[0].astype(F32)
    for k in range(peers):
        total = total + swapped(pieces[k + 1], "space", k + 1).astype(F32)
    total = summed_over_dp(total.astype(BF16))
    whole = [total] + [swapped(total, "space", k + 1) for k in range(peers)]
    grad_images = call(
        part(images_kernel, cols), [((pixels, chans), BF16)], dh1, w_held, e3,
        flops=gates, final=True,
    )
    result = call(
        part(result_kernel, peers, 64), [((pixels, chans), BF16)],
        pre3, own3, rec3, prm, im_half, flops=10 * pixels * chans, final=True,
    )
    grads = call(
        part(unpack_kernel, peers, float(lax.axis_size("dp"))),
        [((mids, chans), F32), ((9, mids, mids), F32), ((mids, chans), F32)]
        + [((1, mids), F32)] * 4 + [((1, chans), F32)] * 2,
        *whole, scratch=[pltpu.VMEM((piece * count, wide), F32)], final=True,
    )
    gwr, gwd, gwe = grads[:3]
    shape = images.shape
    return (
        result.reshape(shape), grad_images.reshape(shape), gwr.T, gwd.reshape(3, 3, mids, mids), gwe,
    ) + tuple(item.reshape(-1) for item in grads[3:])


def solution(mesh):
    big = P("dp", "space", None, None)
    return jax.shard_map(
        shards,
        mesh=mesh,
        in_specs=(big,) + (P(),) * 9 + (big,),
        out_specs=(big, big) + (P(),) * 9,
        check_vma=False,
    )
```

```python
import functools

import jax
import jax.numpy as jnp
from jax import lax
from jax.experimental import pallas as pl
from jax.experimental.pallas import tpu as pltpu
from jax.sharding import PartitionSpec as P

epsilon = 1e-05
F32 = jnp.float32
BF16 = jnp.bfloat16
HEAD = 8
WIDE_HEAD = 16
GAP = 8


def nn(left, right):
    return jnp.dot(left, right, preferred_element_type=F32)


def nt(left, right):
    return lax.dot_general(left, right, (((1,), (1,)), ((), ())), preferred_element_type=F32)


def tn(left, right):
    return lax.dot_general(left, right, (((0,), (0,)), ((), ())), preferred_element_type=F32)


def swap_halves(value):
    return pltpu.roll(value, value.shape[1] // 2, 1)


def lower_half(shape):
    return lax.broadcasted_iota(jnp.int32, shape, 1) < shape[1] // 2


def both_halves(row):
    return row + swap_halves(row)


def rowsum(value):
    return jnp.sum(value, 0, keepdims=True)


def group(value):
    return jnp.sum(value.reshape(value.shape[0] // 8, 8, value.shape[1]), 0)


def silu(value):
    half = 0.5 * value
    return half + half * jnp.tanh(half)


def slope(value):
    half = 0.5 * value
    turn = jnp.tanh(half)
    return (0.5 + 0.5 * turn) * (1.0 + half * (1.0 - turn))


def head_row(ref, item, which):
    if ref.dtype == BF16:
        terms = ref[WIDE_HEAD * item : WIDE_HEAD * (item + 1), :].astype(F32)
        at = 3 * which
        return terms[at : at + 1, :] + terms[at + 1 : at + 2, :] + terms[at + 2 : at + 3, :]
    at = HEAD * item + which
    return ref[at : at + 1, :]


def moments(own, rec, peers, local):
    means = [head_row(own, 0, 0)] + [head_row(rec, k, 0) for k in range(peers)]
    squares = [head_row(own, 0, 1)] + [head_row(rec, k, 1) for k in range(peers)]
    mean = sum(means) / (peers + 1)
    total = sum(squares) + local * sum((item - mean) * (item - mean) for item in means)
    return mean, lax.rsqrt(total / (local * (peers + 1)) + epsilon)


def totals(own, rec, peers):
    sums = head_row(own, 0, 0) + sum(head_row(rec, k, 0) for k in range(peers))
    cross = head_row(own, 0, 1) + sum(head_row(rec, k, 1) for k in range(peers))
    return sums, cross


def head_rows(first, second):
    rest = jnp.zeros((HEAD - 2, first.shape[1]), F32)
    return jnp.concatenate([first, second, rest], 0)


def three_terms(value):
    high = value.astype(BF16).astype(F32)
    mid = (value - high).astype(BF16).astype(F32)
    return [high, mid, value - high - mid]


def wide_head_rows(first, second):
    rest = jnp.zeros((WIDE_HEAD - 6, first.shape[1]), F32)
    return jnp.concatenate(three_terms(first) + three_terms(second) + [rest], 0).astype(BF16)


def halo_rows(edge, peers):
    return edge // 2 if peers == 1 else edge


def edges(ref, edge, peers, centre=0.0):
    size, cols = ref.shape[0], edge // 2
    top, low = ref[0:edge, :], ref[size - edge : size, :]
    if peers != 1:
        return swap_halves(jnp.where(lower_half(top.shape), top, low) - centre)
    first = lax.axis_index("space") == 0
    turned = swap_halves(jnp.where(first, low[0:cols, :], top[cols:, :]) - centre)
    straight = jnp.where(first, low[cols:, :], top[0:cols, :]) - centre
    lanes = lower_half(turned.shape)
    return jnp.where(first, jnp.where(lanes, turned, straight), jnp.where(lanes, straight, turned))


def received(rec, base, edge, peers):
    part = rec[base : base + halo_rows(edge, peers), :].astype(F32)
    if peers != 1:
        return part
    turned = swap_halves(part)
    lanes = lower_half(part.shape)
    return jnp.concatenate(
        [jnp.where(lanes, part, turned), jnp.where(lanes, turned, part)], 0
    )


def sender_row(rec, peers, which):
    above, below = head_row(rec, 0, which), head_row(rec, peers - 1, which)
    return jnp.where(lower_half(above.shape), above, below)


def fill_edges(ext, first, last, halo, edge):
    size = ext.shape[0]
    low = lower_half(halo.shape)
    halo = halo * edge_mask(halo.shape)
    ext[0:edge, :] = jnp.where(low, halo, swap_halves(last)).astype(BF16)
    ext[size - edge : size, :] = jnp.where(low, swap_halves(first), halo).astype(BF16)


def norm_coefs(gain, shift, mean, inv):
    scale = gain * inv
    return scale, shift - mean * scale


def back_coefs(gain, mean, inv, sums, cross, count):
    scale = gain * inv
    slant = -scale * inv * cross / count
    return scale, slant, -scale * sums / count - slant * mean


def centred_squares(ref, mean, step):
    acc = jnp.zeros((8, ref.shape[1]), F32)
    for at in range(0, ref.shape[0], step):
        gap = ref[at : at + step, :] - mean
        acc = acc + group(gap * gap)
    return rowsum(acc)


def first_kernel(
    peers, edge, im, w, wd, pre, msg, im_held, w_held, wd_held, im_near, w_near, wd_near, sems
):
    half, cols, wide = pre.shape[0], edge // 2, pre.shape[1]
    fetch = pltpu.make_async_copy(w, w_near, sems.at[0])
    fetch.start()
    cut = half // cols // 2 * cols
    copies = []
    for k, (base, size) in enumerate(((0, cut), (cut, half - cut))):
        rows = pl.ds(base, size)
        copies.append(
            pltpu.make_async_copy(im.at[:, rows, :], im_near.at[:, rows, :], sems.at[k + 1])
        )
        copies[-1].start()
    fetch_wd = pltpu.make_async_copy(wd, wd_near, sems.at[3])
    fetch_wd.start()
    fetch.wait()
    weight = w_near[...]
    w_held[...] = weight
    zero = jnp.zeros_like(weight)
    sides = (jnp.concatenate([weight, zero], 0), jnp.concatenate([zero, weight], 0))
    acc = jnp.zeros((8, wide), F32)
    for at in range(0, half, cols):
        if at in (0, cut):
            copies[min(at, 1)].wait()
        part = None
        for k, side in enumerate(sides):
            block = im_near[k, at : at + cols, :]
            im_held[k * half + at : k * half + at + cols, :] = block
            prod = nt(block, side)
            part = prod if part is None else part + prod
        pre[at : at + cols, :] = part
        acc = acc + group(part)
    mean = both_halves(rowsum(acc)) / (2 * half)
    msg[0:WIDE_HEAD, :] = wide_head_rows(mean, both_halves(centred_squares(pre, mean, cols)))
    msg[WIDE_HEAD:, :] = edges(pre, edge, peers, mean).astype(BF16)
    fetch_wd.wait()
    wd_held[...] = wd_near[...]


def tap_blocks(w):
    mids = w.shape[-1]
    zero = jnp.zeros((mids, mids), BF16)
    for a in range(3):
        for b in range(3):
            block = w[a, b]
            yield a, b, jnp.concatenate(
                [jnp.concatenate([block, zero], 1), jnp.concatenate([zero, block], 1)], 0
            )


def weights_kernel(wd, we, g1, s1, g2, s2, g3, s3, fwd, bwd, we_held, prm):
    wide = 2 * wd.shape[-1]
    we_held[...] = we[...]
    prm[...] = jnp.zeros(prm.shape, F32)
    for k, ref in enumerate((g1, s1, g2, s2)):
        prm[k : k + 1, 0:wide] = jnp.concatenate([ref[...], ref[...]], 1)
    prm[4:5, :] = g3[...]
    prm[5:6, :] = s3[...]
    for a, b, both in tap_blocks(wd):
        k = 2 - a
        fwd[a * wide : (a + 1) * wide, b * wide : (b + 1) * wide] = both
        bwd[b * wide : (b + 1) * wide, k * wide : (k + 1) * wide] = both


def gain_shift(prm, norm, wide):
    return prm[2 * norm : 2 * norm + 1, 0:wide], prm[2 * norm + 1 : 2 * norm + 2, 0:wide]


def edge_mask(shape):
    me = lax.axis_index("space")
    above = jnp.where(me > 0, 1.0, 0.0)
    below = jnp.where(me < lax.axis_size("space") - 1, 1.0, 0.0)
    return jnp.where(lower_half(shape), above, below)


def taps(ext, edge, at, cols):
    return jnp.concatenate([ext[a * edge + at : a * edge + at + cols, :] for a in range(3)], 1)


def clear_gaps(scr, cols):
    zero = jnp.zeros((scr.shape[0], GAP, scr.shape[2]), F32)
    scr[:, 0:GAP, :] = zero
    scr[:, GAP + cols :, :] = zero


def second_kernel(
    peers, edge, pre1, own1, rec1, prm, w, ext, pre2, msg, scr
):
    half, cols, wide = pre2.shape[0], edge // 2, pre2.shape[1]
    g1, s1 = gain_shift(prm, 0, wide)
    mean, inv = moments(own1, rec1, peers, 2.0 * half)
    scale, bias = norm_coefs(g1, s1, mean, inv)
    clear_gaps(scr, cols)
    last = first = None
    acts = []
    for at in range(0, half, cols):
        act = silu(pre1[at : at + cols, :] * scale + bias)
        ext[edge + at : edge + at + cols, :] = act.astype(BF16)
        if at < edge or at >= half - edge:
            acts.append((at, act))
    first = jnp.concatenate([act for at, act in acts if at < edge], 0)
    last = jnp.concatenate([act for at, act in acts if at >= half - edge], 0)
    if peers:
        centre = sender_row(rec1, peers, 0)
        halo = silu((received(rec1, WIDE_HEAD * peers, edge, peers) + centre) * scale + bias)
    else:
        halo = jnp.zeros((edge, wide), F32)
    fill_edges(ext, first, last, halo, edge)
    acc = jnp.zeros((8, wide), F32)
    for i, at in enumerate(range(0, half, cols)):
        out = nn(taps(ext, edge, at, cols), w[...])
        scr[2 * i, GAP : GAP + cols, :] = out[:, 0:wide]
        scr[2 * i + 1, GAP : GAP + cols, :] = out[:, 2 * wide :]
        part = (
            out[:, wide : 2 * wide]
            + scr[2 * i, GAP - 2 : GAP - 2 + cols, :]
            + scr[2 * i + 1, GAP + 2 : GAP + 2 + cols, :]
        )
        pre2[at : at + cols, :] = part
        acc = acc + group(part)
    mean = both_halves(rowsum(acc)) / (2 * half)
    msg[...] = head_rows(mean, both_halves(centred_squares(pre2, mean, cols)))


def third_kernel(peers, cols, pre2, own2, rec2, prm, w, act2, pre3, msg):
    half = pre2.shape[0]
    g2, s2 = gain_shift(prm, 1, pre2.shape[1])
    mean, inv = moments(own2, rec2, peers, 2.0 * half)
    scale, bias = norm_coefs(g2, s2, mean, inv)
    weight = w[...]
    zero = jnp.zeros_like(weight)
    upper = jnp.concatenate([weight, zero], 0)
    lower = jnp.concatenate([zero, weight], 0)
    acc = jnp.zeros((8, pre3.shape[1]), F32)
    for at in range(0, half, cols):
        act = silu(pre2[at : at + cols, :] * scale + bias).astype(BF16)
        act2[at : at + cols, :] = act
        part = nn(act, upper)
        pre3[at : at + cols, :] = part
        acc = acc + group(part)
        part = nn(act, lower)
        pre3[half + at : half + at + cols, :] = part
        acc = acc + group(part)
    mean = rowsum(acc) / (2 * half)
    msg[...] = head_rows(mean, centred_squares(pre3, mean, cols))


def halves_kernel(step, im, cot, im_half, cot_half):
    def body(i, carry):
        at = pl.ds(pl.multiple_of(i * step, step), step)
        im_half[at, :] = 0.5 * im[at, :].astype(F32)
        cot_half[at, :] = 0.5 * cot[at, :].astype(F32)
        return carry

    lax.fori_loop(0, im.shape[0] // step, body, 0, unroll=2)


def slopes_kernel(peers, step, pre1, own1, rec1, pre2, own2, rec2, prm, slope1, slope2):
    half, wide = pre1.shape
    for norm, pre, own, rec, out in ((0, pre1, own1, rec1, slope1), (1, pre2, own2, rec2, slope2)):
        mean, inv = moments(own, rec, peers, 2.0 * half)
        scale, bias = norm_coefs(*gain_shift(prm, norm, wide), mean, inv)
        for at in range(0, half, step):
            out[at : at + step, :] = slope(pre[at : at + step, :] * scale + bias)


def halved_coefs(peers, own3, rec3, prm, size):
    mean, inv = moments(own3, rec3, peers, float(size))
    gain, shift = gain_shift(prm, 2, own3.shape[1])
    scale, bias = norm_coefs(gain, shift, mean, inv)
    return 0.5 * scale, 0.5 * bias, gain, shift


def fourth_kernel(peers, step, pre3, own3, rec3, prm, im_half, cot_half, e3, msg):
    size, chans = pre3.shape
    scale, bias, gain, shift = halved_coefs(peers, own3, rec3, prm, size)

    def body(i, carry):
        sums, cross = carry
        at = pl.ds(pl.multiple_of(i * step, step), step)
        out = pre3[at, :] * scale + bias
        half = out + im_half[at, :]
        turn = jnp.tanh(half)
        grad = cot_half[at, :] * ((1.0 + turn) * (1.0 + half * (1.0 - turn)))
        e3[at, :] = grad
        return sums + group(grad), cross + group(grad * out)

    zero = jnp.zeros((8, chans), F32)
    sums, cross = lax.fori_loop(0, size // step, body, (zero, zero), unroll=2)
    sums = rowsum(sums)
    msg[...] = head_rows(sums, (2.0 * rowsum(cross) - shift * sums) / gain)


def result_kernel(peers, step, pre3, own3, rec3, prm, im_half, out):
    size = pre3.shape[0]
    scale, bias, _, _ = halved_coefs(peers, own3, rec3, prm, size)

    def body(i, carry):
        at = pl.ds(pl.multiple_of(i * step, step), step)
        half = pre3[at, :] * scale + bias + im_half[at, :]
        out[at, :] = (half + half * jnp.tanh(half)).astype(BF16)
        return carry

    lax.fori_loop(0, size // step, body, 0, unroll=2)


def fifth_kernel(
    peers, edge, pre3, e3, own3, rec3, own4, rec4, prm, w, pre2, own2, rec2, slope2, dh3, e2, msg
):
    size, half, cols, wide = pre3.shape[0], pre2.shape[0], edge // 2, pre2.shape[1]
    count = float(size * (peers + 1))
    g3, _ = gain_shift(prm, 2, pre3.shape[1])
    mean3, inv3 = moments(own3, rec3, peers, float(size))
    sums3, cross3 = totals(own4, rec4, peers)
    scale3, slant3, bias3 = back_coefs(g3, mean3, inv3, sums3, cross3, count)
    mean, inv = moments(own2, rec2, peers, float(size))
    weight = w[...]
    zero = jnp.zeros_like(weight)
    upper = jnp.concatenate([weight, zero], 0)
    lower = jnp.concatenate([zero, weight], 0)
    sums = jnp.zeros((8, wide), F32)
    cross = jnp.zeros((8, wide), F32)
    for at in range(0, half, cols):
        back = None
        for base, side in ((at, upper), (half + at, lower)):
            rows = slice(base, base + cols)
            dh = (e3[rows, :] * scale3 + pre3[rows, :] * slant3 + bias3).astype(BF16)
            dh3[rows, :] = dh
            part = nt(dh, side)
            back = part if back is None else back + part
        pre = pre2[at : at + cols, :]
        grad = back * slope2[at : at + cols, :]
        e2[at : at + cols, :] = grad
        sums = sums + group(grad)
        cross = cross + group(grad * (pre - mean))
    sums = both_halves(rowsum(sums))
    msg[0:WIDE_HEAD, :] = wide_head_rows(sums, both_halves(rowsum(cross) * inv))
    base = WIDE_HEAD + halo_rows(edge, peers)
    msg[WIDE_HEAD:base, :] = edges(e2, edge, peers, sums / size).astype(BF16)
    msg[base:, :] = edges(pre2, edge, peers, mean).astype(BF16)


def expand_kernel(act2, dh3, out):
    half = act2.shape[0]
    mids = act2.shape[1] // 2
    out[...] = tn(act2[...], dh3[0:half, :])[0:mids, :] + tn(act2[...], dh3[half:, :])[mids:, :]


def sixth_kernel(
    peers, edge, pre2, e2, own5, rec5, own2, rec2, pre1, own1, rec1, prm, w, slope1,
    dext, e1, msg, scr,
):
    half, cols, wide = pre2.shape[0], edge // 2, pre2.shape[1]
    size = 2.0 * half
    count = size * (peers + 1)
    g2, _ = gain_shift(prm, 1, wide)
    mean2, inv2 = moments(own2, rec2, peers, size)
    sums2, cross2 = totals(own5, rec5, peers)
    scale2, slant2, bias2 = back_coefs(g2, mean2, inv2, sums2, cross2, count)
    mean, inv = moments(own1, rec1, peers, size)
    clear_gaps(scr, cols)
    acts = []
    for at in range(0, half, cols):
        dh = e2[at : at + cols, :] * scale2 + pre2[at : at + cols, :] * slant2 + bias2
        dext[edge + at : edge + at + cols, :] = dh.astype(BF16)
        if at < edge or at >= half - edge:
            acts.append((at, dh))
    first = jnp.concatenate([act for at, act in acts if at < edge], 0)
    last = jnp.concatenate([act for at, act in acts if at >= half - edge], 0)
    if peers:
        base = WIDE_HEAD * peers
        grad = received(rec5, base, edge, peers) + sender_row(rec5, peers, 0) / size
        pre = received(rec5, base + halo_rows(edge, peers), edge, peers) + mean2
        halo = grad * scale2 + pre * slant2 + bias2
    else:
        halo = jnp.zeros((edge, wide), F32)
    fill_edges(dext, first, last, halo, edge)
    sums = jnp.zeros((8, wide), F32)
    cross = jnp.zeros((8, wide), F32)
    for i, at in enumerate(range(0, half, cols)):
        out = nt(taps(dext, edge, at, cols), w[...])
        scr[2 * i, GAP : GAP + cols, :] = out[:, 0:wide]
        scr[2 * i + 1, GAP : GAP + cols, :] = out[:, 2 * wide :]
        back = (
            out[:, wide : 2 * wide]
            + scr[2 * i, GAP + 2 : GAP + 2 + cols, :]
            + scr[2 * i + 1, GAP - 2 : GAP - 2 + cols, :]
        )
        pre = pre1[at : at + cols, :]
        grad = back * slope1[at : at + cols, :]
        e1[at : at + cols, :] = grad
        sums = sums + group(grad)
        cross = cross + group(grad * (pre - mean))
    msg[...] = head_rows(both_halves(rowsum(sums)), both_halves(rowsum(cross) * inv))


def fold(block, upper):
    mids = block.shape[0] // 2
    if upper:
        return swap_halves(block[0:mids, :]) + block[mids:, :]
    return block[0:mids, :] + swap_halves(block[mids:, :])


def dilated_kernel(edge, ext, dext, out, scr, dcat):
    cols, wide = edge // 2, ext.shape[1]
    half = dext.shape[0] - 2 * edge
    mids = wide // 2
    clear_gaps(scr, cols)
    for i, at in enumerate(range(0, half, cols)):
        mid = dext[edge + at : edge + at + cols, :]
        scr[i, GAP : GAP + cols, :] = mid.astype(F32)
        dcat[at : at + cols, 0:wide] = scr[i, GAP + 2 : GAP + 2 + cols, :].astype(BF16)
        dcat[at : at + cols, wide : 2 * wide] = mid
        dcat[at : at + cols, 2 * wide :] = scr[i, GAP - 2 : GAP - 2 + cols, :].astype(BF16)
    blocks = []
    for a in range(3):
        prod = tn(ext[a * edge : a * edge + half, :], dcat[...])
        blocks = blocks + [prod[:, b * wide : (b + 1) * wide] for b in range(3)]
    low = lower_half((mids, wide))
    for k in range(4):
        pair = jnp.where(low, fold(blocks[2 * k], False), fold(blocks[2 * k + 1], True))
        out[k * mids : (k + 1) * mids, :] = pair.astype(BF16)
    out[4 * mids : 5 * mids, :] = fold(blocks[8], False).astype(BF16)


def seventh_kernel(
    peers, pre1, e1, own6, rec6, own1, rec1, prm, im, gwd, gwe, own4, own5, dh1, *rest
):
    outs, scr = rest[:-1], rest[-1]
    half, wide = pre1.shape
    mids, chans = wide // 2, im.shape[1]
    size = 2.0 * half
    count = size * (peers + 1)
    g1, _ = gain_shift(prm, 0, wide)
    mean, inv = moments(own1, rec1, peers, size)
    sums, cross = totals(own6, rec6, peers)
    scale, slant, bias = back_coefs(g1, mean, inv, sums, cross, count)
    dh = (e1[...] * scale + pre1[...] * slant + bias).astype(BF16)
    dh1[...] = dh
    prod = tn(dh, im[0:half, :])[0:mids, :] + tn(dh, im[half:, :])[mids:, :]
    base = gwd.shape[0]
    scr[0:base, :] = gwd[...]
    for whole in (prod, gwe[...]):
        for part in range(chans // wide):
            scr[base : base + mids, :] = whole[:, part * wide : (part + 1) * wide].astype(BF16)
            base = base + mids
    rows = [head_row(own, 0, which) for own in (own6, own5) for which in (1, 0)]
    for row in (1, 0):
        rows = rows + [own4[row : row + 1, p * wide : (p + 1) * wide] for p in range(chans // wide)]
    rows.append(jnp.zeros((scr.shape[0] - base - len(rows), wide), F32))
    scr[base:, :] = jnp.concatenate(rows, 0).astype(BF16)
    me = lax.axis_index("space")
    for k, out in enumerate(outs):
        piece = out.shape[0]
        start = lax.rem(me + k, peers + 1) * piece
        out[...] = scr[pl.ds(pl.multiple_of(start, 16), piece), :]


def images_kernel(cols, dh1, w, e3, out):
    half = dh1.shape[0]
    weight = w[...]
    zero = jnp.zeros_like(weight)
    sides = (jnp.concatenate([weight, zero], 0), jnp.concatenate([zero, weight], 0))
    for at in range(0, half, cols):
        dh = dh1[at : at + cols, :]
        for side, base in zip(sides, (at, half + at)):
            out[base : base + cols, :] = (nn(dh, side) + e3[base : base + cols, :]).astype(BF16)


def unpack_kernel(peers, batch, *refs):
    pieces, refs = refs[: peers + 1], refs[peers + 1 :]
    gwr, gwd, gwe, gg1, gs1, gg2, gs2, gg3, gs3, scr = refs
    wide = scr.shape[1]
    mids = wide // 2
    chans = gwe.shape[1]
    parts = chans // wide
    me = lax.axis_index("space")
    for k, ref in enumerate(pieces):
        piece = ref.shape[0]
        start = lax.rem(me + peers + 1 - k, peers + 1) * piece
        scr[pl.ds(pl.multiple_of(start, 16), piece), :] = ref[...].astype(F32) / batch
    for k in range(5):
        block = scr[k * mids : (k + 1) * mids, :]
        gwd[2 * k] = block[:, 0:mids]
        if k < 4:
            gwd[2 * k + 1] = swap_halves(block)[:, 0:mids]
    base = 5 * mids
    for ref in (gwr, gwe):
        for part in range(parts):
            ref[:, part * wide : (part + 1) * wide] = scr[base : base + mids, :]
            base = base + mids
    for ref in (gg1, gs1, gg2, gs2):
        ref[...] = scr[base : base + 1, 0:mids]
        base = base + 1
    for ref in (gg3, gs3):
        for part in range(parts):
            ref[:, part * wide : (part + 1) * wide] = scr[base : base + 1, :]
            base = base + 1


HBM = pl.BlockSpec(memory_space=pltpu.HBM)
VMEM = pl.BlockSpec(memory_space=pltpu.VMEM)


def call(kernel, outs, *args, scratch=(), flops=0, far=(), final=False):
    size = sum(item.size * item.dtype.itemsize for item in args)
    size = size + sum(functools.reduce(lambda x, y: x * y, s, 1) * 4 for s, _ in outs)
    kind_of = jax.ShapeDtypeStruct if final else pltpu.VMEM
    args = [pltpu.with_memory_space_constraint(x, pltpu.HBM) if k in far else x for k, x in enumerate(args)]
    out = pl.pallas_call(
        kernel,
        out_shape=[kind_of(shape, kind) for shape, kind in outs],
        in_specs=[HBM if k in far else VMEM for k in range(len(args))],
        out_specs=[VMEM] * len(outs),
        scratch_shapes=list(scratch),
        cost_estimate=pl.CostEstimate(flops=flops, bytes_accessed=size, transcendentals=0),
        compiler_params=pltpu.CompilerParams(vmem_limit_bytes=16 * 1024 * 1024),
    )(*args)
    return out[0] if len(outs) == 1 else out


def swapped(value, axis, step):
    count = lax.axis_size(axis)
    return lax.ppermute(value, axis, [(i, (i + step) % count) for i in range(count)])


def exchanged(msg, peers):
    if peers == 0:
        return msg
    if peers == 1:
        return swapped(msg, "space", 1)
    head = WIDE_HEAD if msg.dtype == BF16 else HEAD
    heads = [swapped(msg[0:head], "space", k + 1) for k in range(peers)]
    if msg.shape[0] > head:
        above = swapped(msg[head:], "space", 1)
        below = swapped(msg[head:], "space", peers)
        low = lax.broadcasted_iota(jnp.int32, above.shape, 1) < above.shape[1] // 2
        heads.append(jnp.where(low, above, below))
    return jnp.concatenate(heads, 0)


def flipped_dp(part, masks):
    count, sides = lax.axis_size("dp"), lax.axis_size("space")
    pairs = []
    for i in range(count * sides):
        dp, side = divmod(i, sides)
        pairs.append((i, (dp ^ masks[side % len(masks)]) * sides + side))
    return lax.ppermute(part, ("dp", "space"), pairs).astype(F32)


def summed_over_dp(part):
    count = lax.axis_size("dp")
    if count & (count - 1):
        return lax.psum(part.astype(F32), "dp").astype(BF16)
    bits = [1 << k for k in range(count.bit_length() - 1)]
    twos = [bits[k : k + 2] for k in range(0, len(bits) - 1, 2)]
    for k in range(len(twos)):
        turn = [twos[(k + side * (len(twos) // 2)) % len(twos)] for side in range(2)]
        both = flipped_dp(part, [pair[0] + pair[1] for pair in turn])
        low = flipped_dp(part, [pair[0] for pair in turn])
        high = flipped_dp(part, [pair[1] for pair in turn])
        part = ((part.astype(F32) + low) + (high + both)).astype(BF16)
    if len(bits) % 2:
        part = (part.astype(F32) + flipped_dp(part, bits[-1:])).astype(BF16)
    return part


def shards(
    images, w_reduce, w_dilated, w_expand, gain_one, shift_one, gain_two, shift_two,
    gain_three, shift_three, cotangent,
):
    rows, cols, chans = images.shape[1:]
    mids = w_reduce.shape[1]
    wide = 2 * mids
    pixels = rows * cols
    half, edge = pixels // 2, 2 * cols
    ext_rows = half + 2 * edge
    count = lax.axis_size("space")
    peers = count - 1
    part = functools.partial
    im = images.reshape(pixels, chans)
    cot = cotangent.reshape(pixels, chans)
    row = lambda item: item.reshape(1, -1)
    gaps = lambda n: pltpu.VMEM((n, cols + 2 * GAP, wide), F32)
    chunks = half // cols
    w_rows = w_reduce.T
    gates = 2 * pixels * wide * chans

    pre1, own1, im_held, w_held, wd_held = call(
        part(first_kernel, peers, edge),
        [((half, wide), F32), ((WIDE_HEAD + halo_rows(edge, peers), wide), BF16), ((pixels, chans), BF16)]
        + [(w_rows.shape, BF16), (w_dilated.shape, BF16)],
        im.reshape(2, half, chans), w_rows, w_dilated, flops=gates, far=(0, 1, 2),
        scratch=[pltpu.VMEM((2, half, chans), BF16), pltpu.VMEM(w_rows.shape, BF16)]
        + [pltpu.VMEM(w_dilated.shape, BF16), pltpu.SemaphoreType.DMA((4,))],
    )
    rec1 = exchanged(own1, peers)
    fwd, bwd, we, prm = call(
        weights_kernel,
        [((3 * wide, 3 * wide), BF16)] * 2 + [(w_expand.shape, BF16), ((8, chans), F32)],
        wd_held, w_expand, row(gain_one), row(shift_one), row(gain_two), row(shift_two),
        row(gain_three), row(shift_three), flops=10**10,
    )
    ext, pre2, own2 = call(
        part(second_kernel, peers, edge),
        [((ext_rows, wide), BF16), ((half, wide), F32), ((HEAD, wide), F32)],
        pre1, own1, rec1, prm, fwd, scratch=[gaps(2 * chunks)], flops=2 * half * 9 * wide * wide,
    )
    rec2 = exchanged(own2, peers)
    im_half, cot_half = call(
        part(halves_kernel, 64), [((pixels, chans), F32)] * 2, im_held, cot,
        flops=4 * pixels * chans,
    )
    act2, pre3, own3 = call(
        part(third_kernel, peers, cols),
        [((half, wide), BF16), ((pixels, chans), F32), ((HEAD, chans), F32)],
        pre2, own2, rec2, prm, we, flops=gates,
    )
    rec3 = exchanged(own3, peers)
    slope1, slope2 = call(
        part(slopes_kernel, peers, cols), [((half, wide), F32)] * 2,
        pre1, own1, rec1, pre2, own2, rec2, prm, flops=30 * half * wide,
    )
    e3, own4 = call(
        part(fourth_kernel, peers, 64), [((pixels, chans), F32), ((HEAD, chans), F32)],
        pre3, own3, rec3, prm, im_half, cot_half, flops=30 * pixels * chans,
    )
    rec4 = exchanged(own4, peers)
    dh3, e2, own5 = call(
        part(fifth_kernel, peers, edge),
        [((pixels, chans), BF16), ((half, wide), F32), ((WIDE_HEAD + 2 * halo_rows(edge, peers), wide), BF16)],
        pre3, e3, own3, rec3, own4, rec4, prm, we, pre2, own2, rec2, slope2, flops=gates,
    )
    rec5 = exchanged(own5, peers)
    gwe = call(expand_kernel, [((mids, chans), F32)], act2, dh3, flops=gates)
    dext, e1, own6 = call(
        part(sixth_kernel, peers, edge),
        [((ext_rows, wide), BF16), ((half, wide), F32), ((HEAD, wide), F32)],
        pre2, e2, own5, rec5, own2, rec2, pre1, own1, rec1, prm, bwd, slope1,
        scratch=[gaps(2 * chunks)], flops=2 * half * 9 * wide * wide,
    )
    rec6 = exchanged(own6, peers)
    gwd = call(
        part(dilated_kernel, edge), [((5 * mids, wide), BF16)], ext, dext,
        scratch=[gaps(chunks), pltpu.VMEM((half, 3 * wide), BF16)],
        flops=2 * half * 9 * wide * wide,
    )
    length = 5 * mids + 2 * (chans // wide) * mids + 16
    piece = -(-length // (16 * count)) * 16
    dh1, *pieces = call(
        part(seventh_kernel, peers),
        [((half, wide), BF16)] + [((piece, wide), BF16)] * count,
        pre1, e1, own6, rec6, own1, rec1, prm, im_held, gwd, gwe, own4, own5, flops=gates,
        scratch=[pltpu.VMEM((piece * count, wide), BF16)],
    )
    total = pieces[0].astype(F32)
    for k in range(peers):
        total = total + swapped(pieces[k + 1], "space", k + 1).astype(F32)
    total = summed_over_dp(total.astype(BF16))
    whole = [total] + [swapped(total, "space", k + 1) for k in range(peers)]
    grad_images = call(
        part(images_kernel, cols), [((pixels, chans), BF16)], dh1, w_held, e3,
        flops=gates, final=True,
    )
    result = call(
        part(result_kernel, peers, 64), [((pixels, chans), BF16)],
        pre3, own3, rec3, prm, im_half, flops=10 * pixels * chans, final=True,
    )
    grads = call(
        part(unpack_kernel, peers, float(lax.axis_size("dp"))),
        [((mids, chans), F32), ((9, mids, mids), F32), ((mids, chans), F32)]
        + [((1, mids), F32)] * 4 + [((1, chans), F32)] * 2,
        *whole, scratch=[pltpu.VMEM((piece * count, wide), F32)], final=True,
    )
    gwr, gwd, gwe = grads[:3]
    shape = images.shape
    return (
        result.reshape(shape), grad_images.reshape(shape), gwr.T, gwd.reshape(3, 3, mids, mids), gwe,
    ) + tuple(item.reshape(-1) for item in grads[3:])


def solution(mesh):
    big = P("dp", "space", None, None)
    return jax.shard_map(
        shards,
        mesh=mesh,
        in_specs=(big,) + (P(),) * 9 + (big,),
        out_specs=(big, big) + (P(),) * 9,
        check_vma=False,
    )
```
